32 devices in a mesh: dp: 8 (over z, x), chan: 4 (over y, core).
Axes of the slice: x: 2, y: 2, z: 4, core: 2. Of those that a mesh axis runs over, the one named last changes fastest.
Arguments:
- features: bfloat16 [64, 16, 16, 1024], P('dp', None, None, 'chan')
- cotangent: bfloat16 [64, 8, 8, 2048], P('dp', None, None, 'chan')
- reduce_a: bfloat16 [1024, 512], P('chan', 'dp'), may hold values from -0.1875 to 0.1875
- spatial_a: bfloat16 [9, 512, 512], P(None, 'chan', 'dp'), may hold values from -0.09375 to 0.09375
- expand_a: bfloat16 [512, 2048], P('dp', 'chan'), may hold values from -0.25 to 0.25
- shortcut: bfloat16 [1024, 2048], P('dp', 'chan'), may hold values from -0.1875 to 0.1875
- reduce_b: bfloat16 [2048, 512], P('chan', 'dp'), may hold values from -0.125 to 0.125
- spatial_b: bfloat16 [9, 512, 512], P(None, 'chan', 'dp'), may hold values from -0.09375 to 0.09375
- expand_b: bfloat16 [512, 2048], P('dp', 'chan'), may hold values from -0.25 to 0.25
- norms_mid: float32 [4, 2, 512], replicated, may hold values from 0.4 to 1.6
- norms_out: float32 [3, 2, 2048], P(None, None, 'chan'), may hold values from 0.4 to 1.6
- crop_side: int32 [64], P('dp'), may hold values from 6 to 14, as said below
- subnet_of: int32 [64], P('dp'), may hold values from 0 to 3, as said below
- width_of: int32 [4], replicated, may hold values from 128 to 512, as said below
Outputs:
- output: float32 [64, 8, 8, 2048], P('dp', None, None, 'chan')
- grad_features: float32 [64, 16, 16, 1024], P('dp', None, None, 'chan')
- grad_reduce_a: float32 [1024, 512], P('chan', 'dp')
- grad_spatial_a: float32 [9, 512, 512], P(None, 'chan', 'dp')
- grad_expand_a: float32 [512, 2048], P('dp', 'chan')
- grad_shortcut: float32 [1024, 2048], P('dp', 'chan')
- grad_reduce_b: float32 [2048, 512], P('chan', 'dp')
- grad_spatial_b: float32 [9, 512, 512], P(None, 'chan', 'dp')
- grad_expand_b: float32 [512, 2048], P('dp', 'chan')
- grad_norms_mid: float32 [4, 2, 512], replicated
- grad_norms_out: float32 [3, 2, 2048], P(None, None, 'chan')
- stats_mid: float32 [4, 2, 4, 512], replicated
- stats_out: float32 [3, 2, 4, 2048], P(None, None, None, 'chan')
The draws below stay inside these ranges and needn't reach their ends.
Inputs may be any that keep to these rules, and one draw needn't show every extreme that they name: `crop_side`: each aligned run of 4 frames is one image: two frames hold one global crop each (side 14) and 2 frames hold four local crops each (side 6), in drawn order. `subnet_of`: each subnet is named by exactly 16 frames; the four local crops of a frame share its subnet. `width_of`: the subnets' widths are k * 128 for k = 1 to 4, each once.
All inputs are finite; a program needn't handle non-finite values.
Results may differ from the reference program's by a relative error of at most 0.035.
Values may be sent and summed in bfloat16 or wider, within the bound.
No kernel may reach another device: no remote copies, remote signals or barrier semaphores. Data moves between devices by JAX's collectives and lax.ppermute only.
A program may use at most 128 MiB of HBM per device.

```python
import jax
import jax.numpy as jnp
from jax import lax

CIN = 1024
MID = 512
COUT = 2048
FRAME = 16
LSIDE = 14
SSIDE = 6
LOCAL = 8
SUBNETS = 4
FRAMES = 64


def frame_ramp():
    return (0.5 + jnp.arange(FRAMES, dtype=jnp.float32) / FRAMES)[:, None, None, None]


def draw_features(key, part):
    noise_key, chan_key = jax.random.split(key, 2)
    chan_scale = jnp.exp(jax.random.uniform(chan_key, (CIN,), minval=-1.15, maxval=1.15))
    array_shape = (FRAMES, FRAME, FRAME, CIN)
    noise = jnp.clip(jax.random.normal(noise_key, array_shape), -4.0, 4.0)
    return (noise * frame_ramp() * chan_scale).astype(jnp.bfloat16)


def draw_cotangent(key, part):
    noise_key = jax.random.fold_in(key, 0)
    array_shape = (FRAMES, FRAME // 2, FRAME // 2, COUT)
    noise = jnp.clip(jax.random.normal(noise_key, array_shape), -4.0, 4.0)
    return (noise * frame_ramp()).astype(jnp.bfloat16)


def draw_crop_side(key, part):
    per_image = 2 + LOCAL // 4
    images = FRAMES // per_image
    pattern = jnp.where(jnp.arange(per_image) < 2, LSIDE, SSIDE).astype(jnp.int32)
    orders = jax.vmap(lambda image_key: jax.random.permutation(image_key, pattern))(jax.random.split(key, images))
    return orders.reshape(FRAMES).astype(jnp.int32)


def draw_subnet_of(key, part):
    return (jax.random.permutation(key, FRAMES) % SUBNETS).astype(jnp.int32)


def draw_width_of(key, part):
    return ((jax.random.permutation(key, SUBNETS) + 1) * (MID // SUBNETS)).astype(jnp.int32)


def shard_levels(rng, shape, shards, low, largest):
    level = 1.0
    for position, blocks in shards:
        draws = jax.random.uniform(jax.random.fold_in(jax.random.fold_in(rng, 6), position), (blocks,), jnp.float32, low / len(shards), largest / len(shards))
        level = level * jnp.repeat(jnp.exp(draws), shape[position] // blocks).reshape((-1,) + (1,) * (len(shape) - 1 - position))
    return level


def centred(stream_key, dims, deviation, most, cuts=(), held_as=jnp.bfloat16):
    values = jax.random.normal(stream_key, dims, jnp.float32) * deviation
    if len(cuts) > 0:
        values = shard_levels(stream_key, dims, cuts, -0.22, 0.18) * values
    return jnp.clip(values, min=-most, max=most).astype(held_as)


def setup_inputs(seed: int = 0) -> dict:
    arg_keys = jax.random.split(jax.random.key(seed), 15)
    features = draw_features(jax.random.fold_in(arg_keys[14], 71), 0)
    cotangent = draw_cotangent(jax.random.fold_in(arg_keys[14], 71), 0)
    reduce_a = centred(arg_keys[2], (CIN, MID), CIN ** -0.5, 0.1875, ((0, 4), (1, 8)))
    spatial_a = centred(arg_keys[3], (9, MID, MID), (9 * MID) ** -0.5, 0.09375, ((1, 4), (2, 8)))
    expand_a = centred(arg_keys[4], (MID, COUT), MID ** -0.5, 0.25, ((0, 8), (1, 4)))
    shortcut = centred(arg_keys[5], (CIN, COUT), CIN ** -0.5, 0.1875, ((0, 8), (1, 4)))
    reduce_b = centred(arg_keys[6], (COUT, MID), COUT ** -0.5, 0.125, ((0, 4), (1, 8)))
    spatial_b = centred(arg_keys[7], (9, MID, MID), (9 * MID) ** -0.5, 0.09375, ((1, 4), (2, 8)))
    expand_b = centred(arg_keys[8], (MID, COUT), MID ** -0.5, 0.25, ((0, 8), (1, 4)))
    norms_mid = jnp.clip(jax.random.uniform(arg_keys[9], (4, 2, MID), jnp.float32, 0.4, 1.6), 0.4, 1.6)
    norms_out = jnp.clip(0.4 + 1.2 * jax.random.uniform(arg_keys[10], (3, 2, COUT), jnp.float32) ** shard_levels(arg_keys[10], (3, 2, COUT), ((2, 4),), -0.2, 0.2), 0.4, 1.6)
    crop_side = draw_crop_side(jax.random.fold_in(arg_keys[14], 71), 0)
    subnet_of = draw_subnet_of(jax.random.fold_in(arg_keys[14], 71), 0)
    width_of = draw_width_of(jax.random.fold_in(arg_keys[14], 71), 0)
    return {"features": features, "cotangent": cotangent, "reduce_a": reduce_a, "spatial_a": spatial_a, "expand_a": expand_a, "shortcut": shortcut, "reduce_b": reduce_b, "spatial_b": spatial_b, "expand_b": expand_b, "norms_mid": norms_mid, "norms_out": norms_out, "crop_side": crop_side, "subnet_of": subnet_of, "width_of": width_of}


EPSILON = 1e-05
PRECISE = lax.Precision.HIGHEST

@jax.custom_vjp
def low(v):
    return lax.optimization_barrier(v.astype(jnp.bfloat16)).astype(jnp.float32)

@jax.custom_vjp
def low_back(v):
    return v

def low_keep(v):
    return (low(v), None)

def low_pass(kept, grad):
    return (grad,)

def back_keep(v):
    return (v, None)

def back_low(kept, grad):
    return (low(grad),)
low.defvjp(low_keep, low_pass)
low_back.defvjp(back_keep, back_low)

def grid_mask(limit, extent):
    period = jnp.where(limit > extent // 2, extent, extent // 2).astype(jnp.int32)
    inside = jnp.arange(extent, dtype=jnp.int32)[None, :] % period[:, None] < limit[:, None]
    return (inside[:, :, None] & inside[:, None, :]).astype(jnp.float32)[..., None]

def pointwise(inputs, weight):
    return jnp.einsum('fhwc,cd->fhwd', inputs, weight, precision=PRECISE)

def spatial(inputs, weight, stride):
    kernel = weight.reshape(3, 3, weight.shape[1], weight.shape[2])
    return lax.conv_general_dilated(inputs, kernel, (stride, stride), ((1, 1), (1, 1)), dimension_numbers=('NHWC', 'HWIO', 'NHWC'), precision=PRECISE)

def batch_norm(values, mask, member, counts, params):
    first = jnp.dot(member.T, lax.optimization_barrier(jnp.sum(values * mask, axis=(1, 2))), precision=PRECISE)
    second = jnp.dot(member.T, lax.optimization_barrier(jnp.sum(values * values * mask, axis=(1, 2))), precision=PRECISE)
    average = first / counts[:, None]
    variance = second / counts[:, None] - average * average
    inverse = lax.rsqrt(variance + EPSILON)
    frame_mean = jnp.dot(member, average, precision=PRECISE)[:, None, None, :]
    frame_inverse = jnp.dot(member, inverse, precision=PRECISE)[:, None, None, :]
    centered = (values - frame_mean) * frame_inverse
    return (params[0] * centered + params[1], jnp.stack([average, variance]))

def reference(features, cotangent, reduce_a, spatial_a, expand_a, shortcut, reduce_b, spatial_b, expand_b, norms_mid, norms_out, crop_side, subnet_of, width_of):
    member = (subnet_of[:, None] == jnp.arange(SUBNETS)[None, :]).astype(jnp.float32)
    width_frame = lax.optimization_barrier(jnp.sum(jnp.where(member > 0, width_of[None, :], 0), axis=1))
    channel_keep = (jnp.arange(MID)[None, :] < width_frame[:, None]).astype(jnp.float32)[:, None, None, :]
    mask_full = grid_mask(crop_side, FRAME)
    mask_half = grid_mask((crop_side + 1) // 2, FRAME // 2)
    count_full = jnp.dot(member.T, lax.optimization_barrier(jnp.sum(mask_full, axis=(1, 2, 3))), precision=PRECISE)
    count_half = jnp.dot(member.T, lax.optimization_barrier(jnp.sum(mask_half, axis=(1, 2, 3))), precision=PRECISE)

    def norm_act(values, mask, counts, params, keep):
        pre, stats = batch_norm(values, mask, member, counts, params)
        return (jax.nn.silu(pre) * keep, stats)
    checked = jax.checkpoint(norm_act)

    def forward(features, reduce_a, spatial_a, expand_a, shortcut, reduce_b, spatial_b, expand_b, norms_mid, norms_out):
        masked = features * mask_full
        z_one = low_back(pointwise(masked, reduce_a))
        act_one, stat_one = checked(z_one, mask_full, count_full, norms_mid[0], mask_full * channel_keep)
        act_one = low(act_one)
        z_two = low_back(spatial(act_one, spatial_a, 2))
        act_two, stat_two = checked(z_two, mask_half, count_half, norms_mid[1], mask_half * channel_keep)
        act_two = low(act_two)
        z_three = low_back(pointwise(act_two, expand_a))
        z_proj = low_back(pointwise(masked[:, ::2, ::2, :], shortcut))
        pre_three, stat_three = batch_norm(z_three, mask_half, member, count_half, norms_out[0])
        pre_proj, stat_proj = batch_norm(z_proj, mask_half, member, count_half, norms_out[1])
        out_a = jax.nn.silu(pre_three + pre_proj) * mask_half
        z_four = low_back(pointwise(low(out_a), reduce_b))
        act_four, stat_four = checked(z_four, mask_half, count_half, norms_mid[2], mask_half * channel_keep)
        act_four = low(act_four)
        z_five = low_back(spatial(act_four, spatial_b, 1))
        act_five, stat_five = checked(z_five, mask_half, count_half, norms_mid[3], mask_half * channel_keep)
        act_five = low(act_five)
        z_six = low_back(pointwise(act_five, expand_b))
        pre_six, stat_six = batch_norm(z_six, mask_half, member, count_half, norms_out[2])
        output = jax.nn.silu(pre_six + out_a) * mask_half
        return (output, (jnp.stack([stat_one, stat_two, stat_four, stat_five]), jnp.stack([stat_three, stat_proj, stat_six])))
    output, pullback, stats = jax.vjp(forward, features.astype(jnp.float32), reduce_a.astype(jnp.float32), spatial_a.astype(jnp.float32), expand_a.astype(jnp.float32), shortcut.astype(jnp.float32), reduce_b.astype(jnp.float32), spatial_b.astype(jnp.float32), expand_b.astype(jnp.float32), norms_mid.astype(jnp.float32), norms_out.astype(jnp.float32), has_aux=True)
    grads = pullback(cotangent.astype(jnp.float32))
    return (output, grads[0], grads[1], grads[2], grads[3], grads[4], grads[5], grads[6], grads[7], grads[8], grads[9], stats[0], stats[1])
```

```python
import jax
import jax.numpy as jnp
from jax import lax
from jax.experimental import pallas as pl
from jax.experimental.pallas import tpu as pltpu
from jax.sharding import PartitionSpec as P

EPSILON = 1e-05
BF = jnp.bfloat16
F32 = jnp.float32
FR = 8
RP = 7
QP = 8
PX = RP * QP
NP = FR * PX
LB = 128
NB = 4


def f3(value):
    return value.reshape(FR, PX, value.shape[-1])


def f2(value):
    return value.reshape(NP, value.shape[-1])


def wide(value, lanes):
    count = lanes // value.shape[-1]
    return value if count == 1 else jnp.concatenate([value] * count, axis=-1)


def dot_nn(left, right):
    return lax.dot_general(left, right, (((1,), (0,)), ((), ())), preferred_element_type=F32)


def dot_nt(left, right):
    return lax.dot_general(left, right, (((1,), (1,)), ((), ())), preferred_element_type=F32)


def dot_tn(left, right):
    return lax.dot_general(left, right, (((0,), (0,)), ((), ())), preferred_element_type=F32)


def crop_mask(info, half, row_scale, row_off, col_scale, col_off):
    at = lax.broadcasted_iota(jnp.int32, (PX, LB), 0)
    row = (at >> 3) * row_scale + row_off
    col = (at & 7) * col_scale + col_off
    parts = []
    for frame in range(FR):
        side = info[1 + frame]
        if half:
            side = (side + 1) >> 1
        full = 8 if half else 16
        period = jnp.where(side > full // 2, full, full // 2)
        inside = ((row & (period - 1)) < side) & ((col & (period - 1)) < side)
        parts.append(jnp.where(inside, 1.0, 0.0).astype(F32))
    return jnp.concatenate(parts, axis=0)


def plane_mask(info, plane):
    return crop_mask(info, 0, 2, plane // 2, 2, plane % 2)


def half_mask(info):
    return crop_mask(info, 1, 1, 0, 1, 0)


def by_subnet(frames, member):
    lanes = frames.shape[-1]
    return jnp.concatenate(
        [jnp.sum(frames * wide(member[s], lanes), axis=0, keepdims=True) for s in range(4)], axis=0
    )


def by_frame(table, member):
    lanes = table.shape[-1]
    total = None
    for s in range(4):
        term = wide(member[s], lanes) * table[s : s + 1, :]
        total = term if total is None else total + term
    return total[:, None, :]


def sum_px(value):
    return jnp.sum(f3(value), axis=1)


def stat_table(totals, inv_count):
    inv_n = wide(inv_count, totals.shape[-1])
    mean = totals[0:4] * inv_n
    var = totals[4:8] * inv_n - mean * mean
    return jnp.concatenate([mean, lax.rsqrt(var + EPSILON)], axis=0), jnp.concatenate([mean, var], axis=0)


def centre(value, table, member):
    return (f3(value) - by_frame(table[0:4], member)) * by_frame(table[4:8], member)


def affine(vhat, prm):
    return prm[0:1][None] * vhat + prm[1:2][None]


def slope(pre):
    sig = jax.nn.sigmoid(pre)
    return sig * (1.0 + pre * (1.0 - sig))


def norm_back(grads, vhat, table, totals, inv_count, member, gain):
    inv_n = wide(inv_count, totals.shape[-1])
    along = by_frame(totals[0:4] * inv_n, member)
    offset = by_frame(totals[4:8] * inv_n, member)
    factor = by_frame(table[4:8], member) * gain[None]
    return factor * (grads - offset - vhat * along)


def param_grads(totals):
    return jnp.concatenate(
        [jnp.sum(totals[0:4], axis=0, keepdims=True), jnp.sum(totals[4:8], axis=0, keepdims=True)], axis=0
    )


def rows_down(value):
    cube = f3(value)
    return f2(jnp.concatenate([jnp.zeros((FR, QP, cube.shape[-1]), F32), cube[:, : PX - QP]], axis=1))


def rows_up(value):
    cube = f3(value)
    return f2(jnp.concatenate([cube[:, QP:], jnp.zeros((FR, QP, cube.shape[-1]), F32)], axis=1))


def cols_right(value, first):
    return jnp.where(first, 0.0, pltpu.roll(value, 1, 0))


def cols_left(value, last):
    return jnp.where(last, 0.0, pltpu.roll(value, NP - 1, 0))


def edge_cols():
    at = lax.broadcasted_iota(jnp.int32, (NP, LB), 0) & 7
    return at == 0, at == 7


def block(ref, index, size):
    return ref[pl.ds(pl.multiple_of(index * size, size), size), :]


def sums_all(ref):
    count = ref.shape[0] // NB
    out = []
    for j in range(NB):
        total = ref[j]
        for d in range(1, count):
            total = total + ref[NB * d + j]
        out.append(total)
    return out


def sums_dp(ref):
    total = ref[0]
    for d in range(1, ref.shape[0]):
        total = total + ref[d]
    return total


def spread(ref, value):
    for d in range(ref.shape[0]):
        ref[d] = value


def k_first(info, feat, rat, xm, small, own, near, far):
    q = info[0]
    at = lax.broadcasted_iota(jnp.int32, (4 * PX, 256), 0)
    source = lax.broadcasted_iota(jnp.int32, (4 * PX, 256), 1)
    plane = (
        (at >= PX).astype(jnp.int32) + (at >= 2 * PX).astype(jnp.int32) + (at >= 3 * PX).astype(jnp.int32)
    )
    inner = at - PX * plane
    row = (inner >> 3) * 2 + (plane >> 1)
    col = (inner & 7) * 2 + (plane & 1)
    hit = source == row * 16 + col
    for pair in range(FR // 2):
        picked = []
        for frame in (2 * pair, 2 * pair + 1):
            side = info[1 + frame]
            period = jnp.where(side > 8, 16, 8)
            inside = ((row & (period - 1)) < side) & ((col & (period - 1)) < side)
            select = jnp.where(hit & inside, 1.0, 0.0).astype(BF)
            picked.append(dot_nn(select, feat[frame]))
        for p in range(4):
            both = jnp.concatenate([x[p * PX : (p + 1) * PX] for x in picked], axis=0)
            xm[p, pair * 2 * PX : (pair + 1) * 2 * PX, :] = both.astype(BF)
    small[...] = xm[0]
    weights = [block(rat, q ^ k, LB) for k in range(4)]
    for p in range(4):
        x = xm[p]
        own[p] = dot_nt(x, weights[0])
        near[0, p] = dot_nt(x, weights[1]).astype(BF)
        near[1, p] = dot_nt(x, weights[3]).astype(BF)
        far[p] = dot_nt(x, weights[2])


def k_stat_first(info, own, near, far, member, counts, zb, st):
    sums = None
    squares = None
    for p in range(4):
        low = (own[p] + near[0, p].astype(F32) + far[p].astype(F32)).astype(BF)
        zb[p] = low
        z = low.astype(F32)
        a, b = sum_px(z), sum_px(z * z)
        sums = a if sums is None else sums + a
        squares = b if squares is None else squares + b
    total = jnp.concatenate([by_subnet(x, member) for x in (sums, squares, counts[0], counts[1])], axis=0)
    spread(st, total)


def k_down(info, st, zb, member, keep, prm, sa, im, own, s1, s2, s3, table, inv_count, stats):
    q = info[0]
    totals = sums_all(st)
    inv16 = 1.0 / totals[0][8:12]
    inv_count[0:4] = inv16
    inv_count[4:8] = 1.0 / totals[0][12:16]
    for j in range(NB):
        table[j], stats[j] = stat_table(totals[j][0:8], inv16)
    tab = table[q]
    kept = keep[q][:, None, :]
    par = prm[0, q]
    first, _ = edge_cols()
    planes = []
    for p in range(4):
        pre = affine(centre(zb[p].astype(F32), tab, member), par)
        planes.append(f2(pre * jax.nn.sigmoid(pre) * f3(plane_mask(info, p)) * kept))
    moved = {}
    for t in range(3):
        for u in range(3):
            key = (0 if t == 1 else 2) + (0 if u == 1 else 1)
            x = planes[key]
            if t == 0:
                x = rows_down(x)
            if u == 0:
                x = cols_right(x, first)
            at = (3 * t + u) * LB
            im[:, at : at + LB] = x.astype(BF)
    taps = im[...]
    own[...] = dot_nt(taps, block(sa, q, LB))
    for k, ref in ((1, s1), (2, s2), (3, s3)):
        ref[...] = dot_nt(taps, block(sa, q ^ k, LB)).astype(BF)


def k_stat(info, own, r1, r2, r3, member, zb, st):
    low = (own[...] + r1[...].astype(F32) + r2[...].astype(F32) + r3[...].astype(F32)).astype(BF)
    zb[...] = low
    z = low.astype(F32)
    m = half_mask(info)
    zm = z * m
    total = jnp.concatenate([by_subnet(sum_px(zm), member), by_subnet(sum_px(zm * z), member)], axis=0)
    spread(st, total)


def act_all(info, st, blocks, member, keep, prm, norm, inv8, act, table, stats):
    q = info[0]
    totals = sums_all(st)
    for j in range(NB):
        table[j], stats[j] = stat_table(totals[j], inv8)
    m = f3(half_mask(info))
    for k in range(NB):
        j = q ^ k
        pre = affine(centre(blocks[k][...].astype(F32), table[j], member), prm[norm, j])
        a = pre * jax.nn.sigmoid(pre) * m * keep[j][:, None, :]
        act[:, pl.ds(pl.multiple_of(j * LB, LB), LB)] = f2(a).astype(BF)


def k_proj(info, x0, x1, x2, x3, sc, member, every, zp, st):
    q = info[0]
    for k, ref in enumerate((x0, x1, x2, x3)):
        every[:, pl.ds(pl.multiple_of((q ^ k) * 256, 256), 256)] = ref[...]
    z = dot_nn(every[...], sc[...])
    zp[...] = z
    st[...] = jnp.concatenate([by_subnet(sum_px(z), member), by_subnet(sum_px(z * z), member)], axis=0)


def k_expand_a(info, st, b0, b1, b2, b3, member, keep, prm, inv_count, ea, stp, act, z3, st3, table, stats):
    act_all(info, st, (b0, b1, b2, b3), member, keep, prm, 1, inv_count[4:8], act, table, stats)
    z = dot_nn(act[...], ea[...])
    z3[...] = z
    total = jnp.concatenate(
        [by_subnet(sum_px(z), member), by_subnet(sum_px(z * z), member), stp[...]], axis=0
    )
    spread(st3, total)


def k_join(info, st3, z3, zp, member, prm, inv_count, rbt, out_a, sum_a, low_a, own, s1, s2, s3, tab3, tabp, stat3, statp):
    q = info[0]
    totals = sums_dp(st3)
    inv8 = inv_count[4:8]
    tab3[...], stat3[...] = stat_table(totals[0:8], inv8)
    tabp[...], statp[...] = stat_table(totals[8:16], inv8)
    pre = affine(centre(z3[...], tab3[...], member), prm[0]) + affine(
        centre(zp[...], tabp[...], member), prm[1]
    )
    sum_a[...] = f2(pre)
    out = f2(pre * jax.nn.sigmoid(pre) * wide(f3(half_mask(info)), pre.shape[-1]))
    out_a[...] = out
    low = out.astype(BF)
    low_a[...] = low
    own[...] = dot_nt(low, block(rbt, q, LB))
    for k, ref in ((1, s1), (2, s2), (3, s3)):
        ref[...] = dot_nt(low, block(rbt, q ^ k, LB)).astype(BF)


def k_flat(info, st, zb, member, keep, prm, inv_count, sb, im, own, s1, s2, s3, table, stats):
    q = info[0]
    totals = sums_all(st)
    inv8 = inv_count[4:8]
    for j in range(NB):
        table[j], stats[j] = stat_table(totals[j], inv8)
    pre = affine(centre(zb[...].astype(F32), table[q], member), prm[2, q])
    act = f2(pre * jax.nn.sigmoid(pre) * f3(half_mask(info)) * keep[q][:, None, :])
    first, last = edge_cols()
    for t in range(3):
        shifted = rows_down(act) if t == 0 else (act if t == 1 else rows_up(act))
        for u in range(3):
            x = cols_right(shifted, first) if u == 0 else (shifted if u == 1 else cols_left(shifted, last))
            at = (3 * t + u) * LB
            im[:, at : at + LB] = x.astype(BF)
    taps = im[...]
    own[...] = dot_nt(taps, block(sb, q, LB))
    for k, ref in ((1, s1), (2, s2), (3, s3)):
        ref[...] = dot_nt(taps, block(sb, q ^ k, LB)).astype(BF)


def k_expand_b(info, st, b0, b1, b2, b3, member, keep, prm, inv_count, eb, act, z6, st6, table, stats):
    act_all(info, st, (b0, b1, b2, b3), member, keep, prm, 3, inv_count[4:8], act, table, stats)
    z = dot_nn(act[...], eb[...])
    z6[...] = z
    spread(st6, jnp.concatenate([by_subnet(sum_px(z), member), by_subnet(sum_px(z * z), member)], axis=0))


def k_output(info, st6, z6, out_a, cot, member, prm, inv_count, output, gb, st, tab6, stat6):
    totals = sums_dp(st6)
    tab6[...], stat6[...] = stat_table(totals, inv_count[4:8])
    vhat = centre(z6[...], tab6[...], member)
    pre = affine(vhat, prm[2]) + f3(out_a[...])
    m = wide(f3(half_mask(info)), pre.shape[-1])
    sig = jax.nn.sigmoid(pre)
    output[:, 0:PX, :] = pre * sig * m
    output[:, PX:, :] = jnp.zeros((FR, 64 - PX, pre.shape[-1]), F32)
    g = cot[...].astype(F32)[:, 0:PX, :] * m * (sig * (1.0 + pre * (1.0 - sig)))
    gb[...] = f2(g)
    along = by_subnet(jnp.sum(g * vhat, axis=1), member)
    offset = by_subnet(jnp.sum(g, axis=1), member)
    spread(st, jnp.concatenate([along, offset], axis=0))


def k_back_six(info, st, z6, gb, tab6, member, prm, inv_count, eb, gz6, own, s1, s2, s3, pg):
    q = info[0]
    totals = sums_dp(st)
    pg[...] = param_grads(totals)
    vhat = centre(z6[...], tab6[...], member)
    m = wide(f3(half_mask(info)), vhat.shape[-1])
    g = m * norm_back(f3(gb[...]), vhat, tab6[...], totals, inv_count[4:8], member, prm[2, 0:1])
    low = f2(g).astype(BF)
    gz6[...] = low
    own[...] = dot_nt(low, block(eb, q, LB))
    for k, ref in ((1, s1), (2, s2), (3, s3)):
        ref[...] = dot_nt(low, block(eb, q ^ k, LB)).astype(BF)


def back_stat(g, vhat, member, gl, st):
    low = f2(g).astype(BF)
    gl[...] = low
    g = f3(low.astype(F32))
    along = by_subnet(jnp.sum(g * vhat, axis=1), member)
    offset = by_subnet(jnp.sum(g, axis=1), member)
    spread(st, jnp.concatenate([along, offset], axis=0))


def k_back_stat(norm):
    def body(info, own, r1, r2, r3, zb, table, member, keep, prm, gl, st):
        q = info[0]
        part = own[...] + r1[...].astype(F32) + r2[...].astype(F32) + r3[...].astype(F32)
        vhat = centre(zb[...].astype(F32), table[q], member)
        g = f3(part * half_mask(info)) * keep[q][:, None, :] * slope(affine(vhat, prm[norm, q]))
        back_stat(g, vhat, member, gl, st)

    return body


def gz_all(info, st, grads, values, table, member, prm, norm, inv8, gz, pg):
    q = info[0]
    totals = sums_all(st)
    for j in range(NB):
        pg[j] = param_grads(totals[j])
    m = f3(half_mask(info))

    def one(k, total_ref):
        j = q ^ k
        vhat = centre(values[k][...].astype(F32), table[j], member)
        g = norm_back(
            f3(grads[k][...].astype(F32)), vhat, table[j], total_ref[j], inv8, member, prm[norm, j][0:1]
        )
        gz[:, pl.ds(pl.multiple_of(j * LB, LB), LB)] = f2(m * g).astype(BF)

    return totals, one


def k_back_five(info, st, g0, g1, g2, g3, v0, v1, v2, v3, tab5, member, keep, prm, inv_count, sb, zb4, tab4, gz5, gl, st4, pg, hold):
    q = info[0]
    totals, one = gz_all(
        info, st, (g0, g1, g2, g3), (v0, v1, v2, v3), tab5, member, prm, 3, inv_count[4:8], gz5, pg
    )
    for j in range(NB):
        hold[j] = totals[j]
    for k in range(NB):
        one(k, hold)
    terms = dot_nn(gz5[...], sb[...])
    first, last = edge_cols()
    total = None
    for t in range(3):
        for u in range(3):
            at = (3 * t + u) * LB
            x = terms[:, at : at + LB]
            x = cols_left(x, last) if u == 0 else (x if u == 1 else cols_right(x, first))
            x = rows_up(x) if t == 0 else (x if t == 1 else rows_down(x))
            total = x if total is None else total + x
    vhat = centre(zb4[...].astype(F32), tab4[q], member)
    g = f3(total * half_mask(info)) * keep[q][:, None, :] * slope(affine(vhat, prm[2, q]))
    back_stat(g, vhat, member, gl, st4)


def k_back_four(info, st, g0, g1, g2, g3, v0, v1, v2, v3, tab4, member, prm, inv_count, rbt, gb, sum_a, z3, zp, tab3, tabp, gz4, ga, st3, pg, hold):
    totals, one = gz_all(
        info, st, (g0, g1, g2, g3), (v0, v1, v2, v3), tab4, member, prm, 2, inv_count[4:8], gz4, pg
    )
    for j in range(NB):
        hold[j] = totals[j]
    for k in range(NB):
        one(k, hold)
    back = dot_nn(gz4[...], rbt[...])
    pre = sum_a[...]
    g = f3((gb[...] + back) * wide(half_mask(info), pre.shape[-1]) * slope(pre))
    ga[...] = f2(g)
    parts = [
        by_subnet(jnp.sum(g * centre(z3[...], tab3[...], member), axis=1), member),
        by_subnet(jnp.sum(g, axis=1), member),
        by_subnet(jnp.sum(g * centre(zp[...], tabp[...], member), axis=1), member),
        jnp.zeros((4, pre.shape[-1]), F32),
    ]
    spread(st3, jnp.concatenate(parts, axis=0))


def k_back_join(info, st, ga, z3, zp, tab3, tabp, member, prm, inv_count, ea, gz3, gzp, own, s1, s2, s3, pg3, pgp):
    q = info[0]
    totals = sums_dp(st)
    tot3 = totals[0:8]
    totp = jnp.concatenate([totals[8:12], totals[4:8]], axis=0)
    pg3[...] = param_grads(tot3)
    pgp[...] = param_grads(totp)
    inv8 = inv_count[4:8]
    g = f3(ga[...])
    m = wide(f3(half_mask(info)), g.shape[-1])
    low = f2(m * norm_back(g, centre(z3[...], tab3[...], member), tab3[...], tot3, inv8, member, prm[0, 0:1]))
    low = low.astype(BF)
    gz3[...] = low
    own[...] = dot_nt(low, block(ea, q, LB))
    for k, ref in ((1, s1), (2, s2), (3, s3)):
        ref[...] = dot_nt(low, block(ea, q ^ k, LB)).astype(BF)
    g = m * norm_back(g, centre(zp[...], tabp[...], member), tabp[...], totp, inv8, member, prm[1, 0:1])
    gzp[...] = f2(g).astype(BF)


def k_back_small(info, gzp, sc, own, s1, s2, s3):
    q = info[0]
    low = gzp[...]
    own[...] = dot_nt(low, block(sc, q, 256))
    for k, ref in ((1, s1), (2, s2), (3, s3)):
        ref[...] = dot_nt(low, block(sc, q ^ k, 256)).astype(BF)


def k_back_two(info, st, g0, g1, g2, g3, v0, v1, v2, v3, tab2, member, keep, prm, inv_count, sa, zb1, tab1, gz2, gl, st1, pg, hold):
    q = info[0]
    totals, one = gz_all(
        info, st, (g0, g1, g2, g3), (v0, v1, v2, v3), tab2, member, prm, 1, inv_count[4:8], gz2, pg
    )
    for j in range(NB):
        hold[j] = totals[j]
    for k in range(NB):
        one(k, hold)
    terms = dot_nn(gz2[...], sa[...])
    _, last = edge_cols()
    y = [terms[:, tap * LB : (tap + 1) * LB] for tap in range(9)]
    planes = [
        y[4],
        cols_left(y[3], last) + y[5],
        rows_up(y[1]) + y[7],
        rows_up(cols_left(y[0], last) + y[2]) + cols_left(y[6], last) + y[8],
    ]
    kept = keep[q][:, None, :]
    along = None
    offset = None
    for p in range(4):
        vhat = centre(zb1[p].astype(F32), tab1[q], member)
        g = f3(planes[p] * plane_mask(info, p)) * kept * slope(affine(vhat, prm[0, q]))
        low = f2(g).astype(BF)
        gl[p] = low
        g = f3(low.astype(F32))
        a, b = jnp.sum(g * vhat, axis=1), jnp.sum(g, axis=1)
        along = a if along is None else along + a
        offset = b if offset is None else offset + b
    spread(st1, jnp.concatenate([by_subnet(along, member), by_subnet(offset, member)], axis=0))


def k_last(info, st, g0, g1, g2, g3, v0, v1, v2, v3, tab1, member, prm, inv_count, rat, o0, o1, o2, o3, gz1, gf, pg, hold, nat):
    q = info[0]
    totals = sums_all(st)
    inv16 = inv_count[0:4]
    for j in range(NB):
        pg[j] = param_grads(totals[j])
        hold[j] = totals[j]
    for p in range(4):
        m = f3(plane_mask(info, p))
        for k, (gref, vref) in enumerate(((g0, v0), (g1, v1), (g2, v2), (g3, v3))):
            j = q ^ k
            vhat = centre(vref[p].astype(F32), tab1[j], member)
            g = norm_back(
                f3(gref[p].astype(F32)), vhat, tab1[j], hold[j], inv16, member, prm[0, j][0:1]
            )
            gz1[p, :, pl.ds(pl.multiple_of(j * LB, LB), LB)] = f2(m * g).astype(BF)
    for p in range(4):
        back = dot_nn(gz1[p], rat[...])
        if p == 0:
            back = back + o0[...] + o1[...].astype(F32) + o2[...].astype(F32) + o3[...].astype(F32)
        back = back * wide(plane_mask(info, p), back.shape[-1])
        high = back.astype(BF)
        nat[0, p] = high.astype(F32)
        nat[1, p] = back - high.astype(F32)
    at = lax.broadcasted_iota(jnp.int32, (256, 4 * PX), 1)
    target = lax.broadcasted_iota(jnp.int32, (256, 4 * PX), 0)
    plane = (
        (at >= PX).astype(jnp.int32) + (at >= 2 * PX).astype(jnp.int32) + (at >= 3 * PX).astype(jnp.int32)
    )
    inner = at - PX * plane
    row = (inner >> 3) * 2 + (plane >> 1)
    col = (inner & 7) * 2 + (plane & 1)
    select = jnp.where(target == row * 16 + col, 1.0, 0.0).astype(BF)
    for frame in range(FR):
        out = None
        for part in range(2):
            x = jnp.concatenate(
                [nat[part, p, frame * PX : (frame + 1) * PX, :] for p in range(4)], axis=0
            ).astype(BF)
            y = dot_nn(select, x)
            out = y if out is None else out + y
        gf[frame] = out


def call(body, outs, info, *args, scratch=(), name):
    total = sum(a.size * a.dtype.itemsize for a in args) + sum(
        jax.ShapeDtypeStruct(s, d).size * jnp.dtype(d).itemsize for s, d in outs
    )
    return pl.pallas_call(
        body,
        out_shape=[jax.ShapeDtypeStruct(shape, dtype) for shape, dtype in outs],
        in_specs=[pl.BlockSpec(memory_space=pltpu.SMEM)] + [pl.BlockSpec(memory_space=pltpu.VMEM)] * len(args),
        out_specs=[pl.BlockSpec(memory_space=pltpu.VMEM)] * len(outs),
        scratch_shapes=list(scratch),
        compiler_params=pltpu.CompilerParams(vmem_limit_bytes=48 << 20),
        cost_estimate=pl.CostEstimate(flops=400_000_000, bytes_accessed=total, transcendentals=0),
        name=name,
    )(info, *args)


def swap(value, k):
    return lax.ppermute(value, "chan", [(i, i ^ k) for i in range(NB)])


def partners(value):
    return [value] + [swap(value, k) for k in (1, 2, 3)]


def everywhere(value):
    return lax.all_to_all(value, ("dp", "chan"), 0, 0, tiled=True)


def along_dp(value):
    return lax.all_to_all(value, "dp", 0, 0, tiled=True)


def gather_rows(value):
    return lax.all_gather(value, "dp", axis=0, tiled=True)


def scatter_rows(value):
    return lax.psum_scatter(value, "dp", scatter_dimension=0, tiled=True)


def shards(
    features,
    cotangent,
    reduce_a,
    spatial_a,
    expand_a,
    shortcut,
    reduce_b,
    spatial_b,
    expand_b,
    norms_mid,
    norms_out,
    crop_side,
    subnet_of,
    width_of,
):
    ndp = lax.axis_size("dp")
    nall = ndp * NB
    hidden = norms_mid.shape[-1]
    taps = 9 * LB
    cin = features.shape[-1]
    cout = cotangent.shape[-1]
    rows = reduce_a.shape[1]
    position = lax.axis_index("chan").astype(jnp.int32)
    info = jnp.concatenate([position[None], crop_side])

    ra_t = reduce_a.T
    rat = along_dp(jnp.broadcast_to(ra_t[None], (ndp,) + ra_t.shape)).reshape(hidden, cin)
    sa = gather_rows(jnp.transpose(spatial_a, (2, 0, 1)).reshape(rows, taps))
    pack_mid = jnp.concatenate([expand_a, shortcut, reduce_b.T], axis=0)
    mid = lax.all_gather(pack_mid, "dp", axis=0)
    er = expand_a.shape[0]
    sr = shortcut.shape[0]
    ea = mid[:, :er].reshape(hidden, cout)
    sc = mid[:, er : er + sr].reshape(ndp * sr, cout)
    rbt = mid[:, er + sr :].reshape(hidden, cout)
    pack_end = jnp.concatenate(
        [jnp.transpose(spatial_b, (2, 0, 1)).reshape(rows, taps), expand_b], axis=1
    )
    end = gather_rows(pack_end)
    sb = end[:, :taps]
    eb = end[:, taps:]

    onehot = (subnet_of[None, :] == jnp.arange(4, dtype=jnp.int32)[:, None]).astype(F32)
    member = jnp.broadcast_to(onehot[:, :, None], (4, FR, LB))
    width = jnp.sum(onehot * width_of.astype(F32)[:, None], axis=0)
    channel = jnp.arange(hidden, dtype=F32).reshape(NB, 1, LB)
    keep = (channel < width[None, :, None]).astype(F32)
    half = (crop_side + 1) // 2
    per16 = jnp.where(crop_side > 8, crop_side * crop_side, 4 * crop_side * crop_side)
    per8 = jnp.where(half > 4, half * half, 4 * half * half)
    counts = jnp.broadcast_to(jnp.stack([per16, per8]).astype(F32)[:, :, None], (2, FR, LB))
    prm = jnp.transpose(norms_mid.reshape(4, 2, NB, LB), (0, 2, 1, 3))
    small_table = ((NB, 8, LB), F32)
    one_block = ((NP, LB), F32)
    send = ((NP, LB), BF)
    stat_all = ((nall, 8, LB), F32)
    map_out = ((NP, cout), F32)
    map_low = ((NP, hidden), BF)
    tab_out = ((8, cout), F32)

    feat = features.reshape(FR, 256, cin)
    xm, small, own, near, far = call(
        k_first,
        [((4, NP, cin), BF), ((NP, cin), BF), ((4, NP, LB), F32), ((2, 4, NP, LB), BF), ((4, NP, LB), F32)],
        info, feat, rat, name="first",
    )
    near = swap(near, 1)
    far = swap((far + near[1].astype(F32)).astype(BF), 2)
    smalls = partners(small)
    zb1, st = call(
        k_stat_first, [((4, NP, LB), BF), ((nall, 16, LB), F32)], info, own, near, far, member, counts,
        name="stat_one",
    )
    st = everywhere(st)
    zs1 = partners(zb1)
    im1, own, s1, s2, s3, tab1, inv_count, stat1 = call(
        k_down,
        [((NP, taps), BF), one_block, send, send, send, small_table, ((8, LB), F32), small_table],
        info, st, zb1, member, keep, prm, sa, name="down",
    )
    zb, st = call(
        k_stat, [send, stat_all], info, own, swap(s1, 1), swap(s2, 2), swap(s3, 3), member, name="stat_two"
    )
    zs2 = partners(zb)
    st = everywhere(st)
    every, zp, stp = call(
        k_proj, [((NP, NB * cin), BF), map_out, tab_out], info, *smalls, sc, member, name="proj"
    )
    act2, z3, st3, tab2, stat2 = call(
        k_expand_a, [map_low, map_out, ((ndp, 16, cout), F32), small_table, small_table],
        info, st, *zs2, member, keep, prm, inv_count, ea, stp, name="expand_a",
    )
    st3 = along_dp(st3)
    out_a, sum_a, low_a, own, s1, s2, s3, tab3, tabp, stat3, statp = call(
        k_join,
        [map_out, map_out, ((NP, cout), BF), one_block, send, send, send, tab_out, tab_out, tab_out, tab_out],
        info, st3, z3, zp, member, norms_out, inv_count, rbt, name="join",
    )
    zb4, st = call(
        k_stat, [send, stat_all], info, own, swap(s1, 1), swap(s2, 2), swap(s3, 3), member, name="stat_four"
    )
    st = everywhere(st)
    zs4 = partners(zb4)
    im4, own, s1, s2, s3, tab4, stat4 = call(
        k_flat, [((NP, taps), BF), one_block, send, send, send, small_table, small_table],
        info, st, zb4, member, keep, prm, inv_count, sb, name="flat",
    )
    zb5, st = call(
        k_stat, [send, stat_all], info, own, swap(s1, 1), swap(s2, 2), swap(s3, 3), member, name="stat_five"
    )
    zs5 = partners(zb5)
    st = everywhere(st)
    act5, z6, st6, tab5, stat5 = call(
        k_expand_b, [map_low, map_out, ((ndp, 8, cout), F32), small_table, small_table],
        info, st, *zs5, member, keep, prm, inv_count, eb, name="expand_b",
    )
    st6 = along_dp(st6)
    output, gb, st, tab6, stat6 = call(
        k_output, [((FR, 64, cout), F32), map_out, ((ndp, 8, cout), F32), tab_out, tab_out],
        info, st6, z6, out_a, cotangent.reshape(FR, 64, cout), member, norms_out, inv_count, name="output",
    )

    st = along_dp(st)
    gz6, own, s1, s2, s3, pg6 = call(
        k_back_six, [((NP, cout), BF), one_block, send, send, send, ((2, cout), F32)],
        info, st, z6, gb, tab6, member, norms_out, inv_count, eb, name="back_six",
    )
    gl, st = call(
        k_back_stat(3), [send, stat_all],
        info, own, swap(s1, 1), swap(s2, 2), swap(s3, 3), zb5, tab5, member, keep, prm, name="back_stat_five",
    )
    gs5 = partners(gl)
    st = everywhere(st)
    grad_eb = dot_tn(act5, gz6).astype(BF)
    hold = [pltpu.VMEM((NB, 8, LB), F32)]
    pair_mid = ((NB, 2, LB), F32)
    gz5, gl, st, pg5 = call(
        k_back_five, [map_low, send, stat_all, pair_mid],
        info, st, *gs5, *zs5, tab5, member, keep, prm, inv_count, sb, zb4, tab4, scratch=hold, name="back_five",
    )
    gs4 = partners(gl)
    st = everywhere(st)
    grad_sb = dot_tn(gz5, im4).astype(BF)
    end_grad = scatter_rows(jnp.concatenate([grad_sb, grad_eb], axis=1))
    gz4, ga, st, pg4 = call(
        k_back_four, [map_low, map_out, ((ndp, 16, cout), F32), pair_mid],
        info, st, *gs4, *zs4, tab4, member, prm, inv_count, rbt, gb, sum_a, z3, zp, tab3, tabp,
        scratch=hold, name="back_four",
    )
    st = along_dp(st)
    grad_rbt = dot_tn(gz4, low_a).astype(BF)
    gz3, gzp, own, s1, s2, s3, pg3, pgp = call(
        k_back_join,
        [((NP, cout), BF), ((NP, cout), BF), one_block, send, send, send, ((2, cout), F32), ((2, cout), F32)],
        info, st, ga, z3, zp, tab3, tabp, member, norms_out, inv_count, ea, name="back_join",
    )
    gl, st = call(
        k_back_stat(1), [send, stat_all],
        info, own, swap(s1, 1), swap(s2, 2), swap(s3, 3), zb, tab2, member, keep, prm, name="back_stat_two",
    )
    gs2 = partners(gl)
    st = everywhere(st)
    half_send = ((NP, cin), BF)
    gown, t1, t2, t3 = call(
        k_back_small, [((NP, cin), F32), half_send, half_send, half_send], info, gzp, sc, name="back_small"
    )
    grad_ea = dot_tn(act2, gz3).astype(BF)
    grad_sc = dot_tn(every, gzp).astype(BF)
    mid_grad = scatter_rows(
        jnp.concatenate(
            [g.reshape(ndp, -1, cout) for g in (grad_ea, grad_sc, grad_rbt)], axis=1
        ).reshape(-1, cout)
    )
    gz2, gl, st, pg2 = call(
        k_back_two, [map_low, ((4, NP, LB), BF), stat_all, pair_mid],
        info, st, *gs2, *zs2, tab2, member, keep, prm, inv_count, sa, zb1, tab1, scratch=hold, name="back_two",
    )
    gs1 = partners(gl)
    st = everywhere(st)
    smalls_back = (gown, swap(t1, 1), swap(t2, 2), swap(t3, 3))
    grad_sa = scatter_rows(dot_tn(gz2, im1).astype(BF))
    gz1, gf, pg1 = call(
        k_last, [((4, NP, hidden), BF), ((FR, 256, cin), F32), pair_mid],
        info, st, *gs1, *zs1, tab1, member, prm, inv_count, rat, *smalls_back,
        scratch=hold + [pltpu.VMEM((2, 4, NP, cin), F32)], name="last",
    )
    grad_rat = dot_tn(gz1.reshape(4 * NP, hidden), xm.reshape(4 * NP, cin)).astype(BF)
    grad_rat = jnp.sum(along_dp(grad_rat.reshape(ndp, rows, cin)).astype(F32), axis=0)

    def taps_out(flat):
        return jnp.transpose(flat.astype(F32).reshape(rows, 9, LB), (1, 2, 0))

    grad_reduce_a = grad_rat.T
    grad_spatial_a = taps_out(grad_sa)
    grad_expand_a = mid_grad[:er].astype(F32)
    grad_shortcut = mid_grad[er : er + sr].astype(F32)
    grad_reduce_b = mid_grad[er + sr :].astype(F32).T
    grad_spatial_b = taps_out(end_grad[:, :taps])
    grad_expand_b = end_grad[:, taps:].astype(F32)
    grad_norms_mid = jnp.stack(
        [jnp.transpose(x, (1, 0, 2)).reshape(2, hidden) for x in (pg1, pg2, pg4, pg5)]
    )
    grad_norms_out = jnp.stack([pg3, pgp, pg6])
    stats_mid = jnp.stack(
        [
            jnp.transpose(x.reshape(NB, 2, 4, LB), (1, 2, 0, 3)).reshape(2, 4, hidden)
            for x in (stat1, stat2, stat4, stat5)
        ]
    )
    stats_out = jnp.stack([x.reshape(2, 4, cout) for x in (stat3, statp, stat6)])
    return (
        output.reshape(FR, 8, 8, cout),
        gf.reshape(FR, 16, 16, cin),
        grad_reduce_a,
        grad_spatial_a,
        grad_expand_a,
        grad_shortcut,
        grad_reduce_b,
        grad_spatial_b,
        grad_expand_b,
        grad_norms_mid,
        grad_norms_out,
        stats_mid,
        stats_out,
    )


def solution(mesh):
    in_specs = (
        P("dp", None, None, "chan"),
        P("dp", None, None, "chan"),
        P("chan", "dp"),
        P(None, "chan", "dp"),
        P("dp", "chan"),
        P("dp", "chan"),
        P("chan", "dp"),
        P(None, "chan", "dp"),
        P("dp", "chan"),
        P(),
        P(None, None, "chan"),
        P("dp"),
        P("dp"),
        P(),
    )
    out_specs = (
        P("dp", None, None, "chan"),
        P("dp", None, None, "chan"),
        P("chan", "dp"),
        P(None, "chan", "dp"),
        P("dp", "chan"),
        P("dp", "chan"),
        P("chan", "dp"),
        P(None, "chan", "dp"),
        P("dp", "chan"),
        P(),
        P(None, None, "chan"),
        P(),
        P(None, None, None, "chan"),
    )
    return jax.shard_map(shards, mesh=mesh, in_specs=in_specs, out_specs=out_specs, check_vma=False)
```

```python
import jax
import jax.numpy as jnp
from jax import lax
from jax.experimental import pallas as pl
from jax.experimental.pallas import tpu as pltpu
from jax.sharding import PartitionSpec as P

EPSILON = 1e-05
BF = jnp.bfloat16
F32 = jnp.float32
FR = 8
RP = 7
QP = 8
PX = RP * QP
NP = FR * PX
LB = 128
NB = 4
TAPS = 9 * LB


class Pinned:
    def __init__(self, array, view=None, shape=None):
        self.array = array
        self.view = view
        self.shape = array.shape if shape is None else shape


class Gathered:
    def __init__(self, pieces, rows, first, lanes):
        self.pieces = pieces
        self.rows = rows
        self.window = (slice(0, rows), slice(first, first + lanes))
        self.shape = (len(pieces) * rows, lanes)


class Late:
    def __init__(self, ref, copies):
        self.ref = ref
        self.copies = copies
        self.waiting = True

    def ready(self):
        if self.waiting:
            for copy in self.copies:
                copy.wait()
            self.waiting = False
        return self.ref

    def __getitem__(self, index):
        return self.ready()[index]

    @property
    def shape(self):
        return self.ref.shape


class Saved:
    def __init__(self, ref, copy):
        self.ref = ref
        self.copy = copy
        self.sent = False

    def __setitem__(self, index, value):
        self.ref[index] = value

    def __getitem__(self, index):
        return self.ref[index]

    @property
    def shape(self):
        return self.ref.shape

    def send(self):
        self.sent = True
        self.copy.start()


def call(body, outs, info, *args, scratch=(), name, alias=None):
    flat = []
    buffers = []
    copies = 0
    for a in args:
        if isinstance(a, Gathered):
            flat += [(p, True) for p in a.pieces]
            buffers.append(pltpu.VMEM(a.shape, a.pieces[0].dtype))
            copies += len(a.pieces)
        elif isinstance(a, Pinned):
            flat.append((a.array, True))
            buffers.append(pltpu.VMEM(a.shape, a.array.dtype))
            copies += 1
        else:
            flat.append((a, False))
    saved = [len(o) > 2 for o in outs]
    for o, s in zip(outs, saved):
        if s:
            buffers.append(pltpu.VMEM(o[4] if len(o) > 3 else o[0], o[1]))
            copies += 1
    extra = [] if alias is None else [alias[0]]
    arrays = [pltpu.with_memory_space_constraint(a, pltpu.HBM) if p else a for a, p in flat]
    arrays += [pltpu.with_memory_space_constraint(a, pltpu.HBM) for a in extra]
    vmem = pl.BlockSpec(memory_space=pltpu.VMEM)
    hbm = pl.BlockSpec(memory_space=pltpu.HBM)

    def kernel(*refs):
        refs = list(refs)
        info_ref = refs.pop(0)
        ins = refs[: len(flat)]
        refs = refs[len(flat) + len(extra) :]
        results, refs = refs[: len(outs)], refs[len(outs) :]
        bufs, refs = refs[: len(buffers)], refs[len(buffers) :]
        if copies:
            sems, refs = refs[0], refs[1:]
        used = 0
        given = []
        late = []
        for a in args:
            if not isinstance(a, (Gathered, Pinned)):
                given.append(ins.pop(0))
                continue
            buf = bufs.pop(0)
            moves = []
            if isinstance(a, Gathered):
                for i in range(len(a.pieces)):
                    source = info_ref[25] ^ (2 * (i % 4)) ^ (i // 4)
                    rows = pl.ds(pl.multiple_of(source * a.rows, a.rows), a.rows)
                    moves.append(pltpu.make_async_copy(ins.pop(0).at[a.window], buf.at[rows], sems.at[used]))
                    used += 1
            else:
                ref = ins.pop(0)
                source = ref if a.view is None else a.view(ref, info_ref)
                moves.append(pltpu.make_async_copy(source, buf, sems.at[used]))
                used += 1
            for move in moves:
                move.start()
            late.append(Late(buf, moves))
            given.append(late[-1])
        produced = []
        outgoing = []
        for o, s, ref in zip(outs, saved, results):
            if s:
                buf = bufs.pop(0)
                target = o[3](ref) if len(o) > 3 else ref
                ref = Saved(buf, pltpu.make_async_copy(buf, target, sems.at[used]))
                used += 1
                outgoing.append(ref)
            produced.append(ref)
        body(info_ref, *given, *produced, *refs)
        for one in outgoing:
            if not one.sent:
                one.send()
        for one in late:
            one.ready()
        for one in outgoing:
            one.copy.wait()

    return pl.pallas_call(
        kernel,
        out_shape=[(pltpu.HBM if s else jax.ShapeDtypeStruct)(o[0], o[1]) for o, s in zip(outs, saved)],
        in_specs=[pl.BlockSpec(memory_space=pltpu.SMEM)]
        + [hbm if p else vmem for _, p in flat]
        + [hbm] * len(extra),
        out_specs=[hbm if s else vmem for s in saved],
        scratch_shapes=buffers + ([pltpu.SemaphoreType.DMA((copies,))] if copies else []) + list(scratch),
        input_output_aliases={} if alias is None else {1 + len(flat): alias[1]},
        compiler_params=pltpu.CompilerParams(vmem_limit_bytes=40 << 20),
        cost_estimate=pl.CostEstimate(flops=1, bytes_accessed=1, transcendentals=0),
        name=name,
    )(info, *arrays)


def f3(value):
    return value.reshape(FR, PX, value.shape[-1])


def f2(value):
    return value.reshape(NP, value.shape[-1])


def wide(value, lanes):
    count = lanes // value.shape[-1]
    return value if count == 1 else jnp.concatenate([value] * count, axis=-1)


def dot_nn(left, right):
    return lax.dot_general(left, right, (((1,), (0,)), ((), ())), preferred_element_type=F32)


def dot_nt(left, right):
    return lax.dot_general(left, right, (((1,), (1,)), ((), ())), preferred_element_type=F32)


def dot_tn(left, right):
    return lax.dot_general(left, right, (((0,), (0,)), ((), ())), preferred_element_type=F32)


def frame_scalars(info, first):
    row = lax.broadcasted_iota(jnp.int32, (FR, LB), 0)
    out = jnp.zeros((FR, LB), jnp.int32)
    for frame in range(FR):
        out = jnp.where(row == frame, info[first + frame], out)
    return out


def member_of(info):
    subnet = frame_scalars(info, 9)
    return [(subnet == s).astype(F32) for s in range(4)]


def keep_of(info, j):
    lane = lax.broadcasted_iota(jnp.int32, (FR, LB), 1) + j * LB
    return (lane < frame_scalars(info, 17)).astype(F32)[:, None, :]


def crop_mask(info, half, row_scale, row_off, col_scale, col_off):
    at = lax.broadcasted_iota(jnp.int32, (PX, LB), 0)
    row = (at >> 3) * row_scale + row_off
    col = (at & 7) * col_scale + col_off
    parts = []
    for frame in range(FR):
        side = info[1 + frame]
        if half:
            side = (side + 1) >> 1
        full = 8 if half else 16
        period = jnp.where(side > full // 2, full, full // 2)
        inside = ((row & (period - 1)) < side) & ((col & (period - 1)) < side)
        parts.append(jnp.where(inside, 1.0, 0.0).astype(F32))
    return jnp.concatenate(parts, axis=0)


def plane_mask(info, plane):
    return crop_mask(info, 0, 2, plane // 2, 2, plane % 2)


def half_mask(info):
    return crop_mask(info, 1, 1, 0, 1, 0)


def by_subnet(frames, member):
    lanes = frames.shape[-1]
    return jnp.concatenate(
        [jnp.sum(frames * wide(member[s], lanes), axis=0, keepdims=True) for s in range(4)], axis=0
    )


def by_frame(table, member):
    lanes = table.shape[-1]
    total = None
    for s in range(4):
        term = wide(member[s], lanes) * table[s : s + 1, :]
        total = term if total is None else total + term
    return total[:, None, :]


def sum_px(value):
    return jnp.sum(f3(value), axis=1)


def stat_table(totals, inv_count):
    inv_n = wide(inv_count, totals.shape[-1])
    mean = totals[0:4] * inv_n
    var = totals[4:8] * inv_n - mean * mean
    return jnp.concatenate([mean, lax.rsqrt(var + EPSILON)], axis=0), jnp.concatenate([mean, var], axis=0)


def centre(value, table, member):
    return (f3(value) - by_frame(table[0:4], member)) * by_frame(table[4:8], member)


def affine(vhat, prm):
    return prm[0:1][None] * vhat + prm[1:2][None]


def silu(pre):
    return pre * jax.nn.sigmoid(pre)


def slope(pre):
    sig = jax.nn.sigmoid(pre)
    return sig * (1.0 + pre * (1.0 - sig))


def norm_back(grads, vhat, table, totals, inv_count, member, gain):
    inv_n = wide(inv_count, totals.shape[-1])
    along = by_frame(totals[0:4] * inv_n, member)
    offset = by_frame(totals[4:8] * inv_n, member)
    factor = by_frame(table[4:8], member) * gain[None]
    return factor * (grads - offset - vhat * along)


def param_grads(totals):
    return jnp.concatenate(
        [jnp.sum(totals[0:4], axis=0, keepdims=True), jnp.sum(totals[4:8], axis=0, keepdims=True)], axis=0
    )


def rows_down(value):
    cube = f3(value)
    return f2(jnp.concatenate([jnp.zeros((FR, QP, cube.shape[-1]), F32), cube[:, : PX - QP]], axis=1))


def rows_up(value):
    cube = f3(value)
    return f2(jnp.concatenate([cube[:, QP:], jnp.zeros((FR, QP, cube.shape[-1]), F32)], axis=1))


def cols_right(value, first):
    return jnp.where(first, 0.0, pltpu.roll(value, 1, 0))


def cols_left(value, last):
    return jnp.where(last, 0.0, pltpu.roll(value, NP - 1, 0))


def edge_cols():
    at = lax.broadcasted_iota(jnp.int32, (NP, LB), 0) & 7
    return at == 0, at == 7


def block(ref, index, size):
    if len(ref.shape) == 2:
        return ref[pl.ds(pl.multiple_of(index * size, size), size), :]
    step = size // ref.shape[1]
    return ref[pl.ds(index * step, step)].reshape(size, ref.shape[-1])


def matrix(ref):
    value = ref[...]
    return value if len(value.shape) == 2 else value.reshape(-1, value.shape[-1])


def lanes_of(index, size):
    return pl.ds(pl.multiple_of(index * size, size), size)


def sums_all(ref):
    count = ref.shape[0] // NB
    out = []
    for j in range(NB):
        total = ref[j]
        for d in range(1, count):
            total = total + ref[NB * d + j]
        out.append(total)
    return out


def sums_dp(ref):
    total = ref[0]
    for d in range(1, ref.shape[0]):
        total = total + ref[d]
    return total


def spread(ref, value):
    for d in range(ref.shape[0]):
        ref[d] = value


def products(low, weight, q, size, own, others):
    own[...] = dot_nt(low, block(weight, q, size))
    for k, ref in others:
        ref[...] = dot_nt(low, block(weight, q ^ k, size)).astype(BF)


def emit(info, full, outs, first=0):
    if len(outs) == 1:
        outs[0][...] = full[...].astype(BF)
        return
    away, kept = outs
    rows = full.shape[0] // 8
    here = info[25]
    to = slice(first, first + rows)
    for k in range(4):
        target = here ^ (2 * k)
        kept[k, to] = full[pl.ds(pl.multiple_of(target * rows, rows), rows), :].astype(BF)
        away[k, to] = full[pl.ds(pl.multiple_of((target ^ 1) * rows, rows), rows), :].astype(BF)


def natural_index(axis):
    shape = (4 * PX, 256) if axis == 0 else (256, 4 * PX)
    at = lax.broadcasted_iota(jnp.int32, shape, axis)
    plane = (
        (at >= PX).astype(jnp.int32) + (at >= 2 * PX).astype(jnp.int32) + (at >= 3 * PX).astype(jnp.int32)
    )
    inner = at - PX * plane
    row = (inner >> 3) * 2 + (plane >> 1)
    col = (inner & 7) * 2 + (plane & 1)
    return row, col, lax.broadcasted_iota(jnp.int32, shape, 1 - axis)


def k_prep(info, feat, xm, xs, small):
    row, col, source = natural_index(0)
    hit = source == row * 16 + col
    for pair in range(FR // 2):
        picked = []
        for frame in (2 * pair, 2 * pair + 1):
            side = info[1 + frame]
            period = jnp.where(side > 8, 16, 8)
            inside = ((row & (period - 1)) < side) & ((col & (period - 1)) < side)
            select = jnp.where(hit & inside, 1.0, 0.0).astype(BF)
            picked.append(dot_nn(select, feat[frame]))
        for p in range(4):
            both = jnp.concatenate([x[p * PX : (p + 1) * PX] for x in picked], axis=0)
            xm[p, pair * 2 * PX : (pair + 1) * 2 * PX, :] = both.astype(BF)
    xs[...] = xm[...]
    small[...] = xm[0]


def k_first(info, xm, rat, own, near, far):
    q = info[0]
    weights = [block(rat, q ^ k, LB) for k in range(4)]
    for p in range(4):
        x = xm[p]
        own[p] = dot_nt(x, weights[0])
        near[0, p] = dot_nt(x, weights[1]).astype(BF)
        near[1, p] = dot_nt(x, weights[3]).astype(BF)
        far[p] = dot_nt(x, weights[2])


def k_stat_first(info, own, near, far, zb, st):
    member = member_of(info)
    sums = None
    squares = None
    for p in range(4):
        low = (own[p] + near[0, p].astype(F32) + far[p].astype(F32)).astype(BF)
        zb[p] = low
        z = low.astype(F32)
        a, b = sum_px(z), sum_px(z * z)
        sums = a if sums is None else sums + a
        squares = b if squares is None else squares + b
    spread(st, jnp.concatenate([by_subnet(sums, member), by_subnet(squares, member)], axis=0))


def k_down(info, st, zb, prm, sa, counts, own, s1, s2, s3, im, vh, table, inv_count, stats):
    q = info[0]
    member = member_of(info)
    totals = sums_all(st)
    pixels = jnp.sum(counts[...].astype(F32), axis=0, keepdims=True)
    lane = lax.broadcasted_iota(jnp.int32, (1, LB), 1)
    for s in range(8):
        here = jnp.sum(jnp.where(lane == s, pixels, 0.0), axis=1, keepdims=True)
        inv_count[s : s + 1, :] = jnp.broadcast_to(1.0 / here, (1, LB))
    inv16 = inv_count[0:4, :]
    for j in range(NB):
        table[j], stats[j] = stat_table(totals[j][0:8], inv16)
    tab = table[q]
    kept = keep_of(info, q)
    par = prm[0, q]
    first, _ = edge_cols()
    planes = []
    for p in range(4):
        vhat = centre(zb[p].astype(F32), tab, member)
        vh[p] = f2(vhat).astype(BF)
        planes.append(f2(silu(affine(vhat, par)) * f3(plane_mask(info, p)) * kept))
    vh.send()
    for t in range(3):
        for u in range(3):
            x = planes[(0 if t == 1 else 2) + (0 if u == 1 else 1)]
            if t == 0:
                x = rows_down(x)
            if u == 0:
                x = cols_right(x, first)
            at = (3 * t + u) * LB
            im[:, at : at + LB] = x.astype(BF)
    im.send()
    products(im[...], sa, q, LB, own, ((1, s1), (2, s2), (3, s3)))


def k_stat(info, own, r1, r2, r3, zb, st):
    member = member_of(info)
    low = (own[...] + r1[...].astype(F32) + r2[...].astype(F32) + r3[...].astype(F32)).astype(BF)
    zb[...] = low
    z = low.astype(F32)
    zm = z * half_mask(info)
    total = jnp.concatenate([by_subnet(sum_px(zm), member), by_subnet(sum_px(zm * z), member)], axis=0)
    spread(st, total)


def act_all(info, st, blocks, prm, norm, inv8, act, vh, table, stats):
    q = info[0]
    member = member_of(info)
    totals = sums_all(st)
    for j in range(NB):
        table[j], stats[j] = stat_table(totals[j], inv8)
    m = f3(half_mask(info))
    for k in range(NB):
        j = q ^ k
        vhat = centre(blocks[k][...].astype(F32), table[j], member)
        vh[:, lanes_of(j, LB)] = f2(vhat).astype(BF)
        a = silu(affine(vhat, prm[norm, j])) * m * keep_of(info, j)
        act[:, lanes_of(j, LB)] = f2(a).astype(BF)
    vh.send()
    act.send()


def two_sums(z, member):
    return jnp.concatenate([by_subnet(sum_px(z), member), by_subnet(sum_px(z * z), member)], axis=0)


def k_proj(info, x0, x1, x2, x3, sc, st, every, zp):
    q = info[0]
    for k, ref in enumerate((x0, x1, x2, x3)):
        every[:, lanes_of(q ^ k, 256)] = ref[...]
    every.send()
    z = dot_nn(every[...], matrix(sc))
    zp[...] = z.astype(BF)
    zp.send()
    st[...] = two_sums(z, member_of(info))


def k_expand_a(info, st, b0, b1, b2, b3, stp, stx, prm, inv_count, ea, z3, st3, act, vh, table, stats, hold):
    act_all(info, st, (b0, b1, b2, b3), prm, 1, inv_count[4:8], act, vh, table, stats)
    z = dot_nn(act[...], matrix(ea))
    z3[...] = z
    hold[...] = stp[...] + stx[...]
    half = hold.shape[1] // 2
    part = hold[:, lanes_of(info[25] & 1, half)]
    spread(st3, jnp.concatenate([two_sums(z, member_of(info)), part], axis=1))


def k_join(info, st3, z3, zp, prm, inv_count, rbt, own, s1, s2, s3, low_a, sl, vh3, vhp, tab3, tabp, stat3, statp):
    q = info[0]
    member = member_of(info)
    inv8 = inv_count[4:8]
    lanes = z3.shape[1]
    even, odd = st3[0], st3[1]
    for d in range(2, st3.shape[0], 2):
        even = even + st3[d]
        odd = odd + st3[d + 1]
    tab3[...], stat3[...] = stat_table(even[:, :lanes] + odd[:, :lanes], inv8)
    tabp[...], statp[...] = stat_table(jnp.concatenate([even[:, lanes:], odd[:, lanes:]], axis=1), inv8)
    va = centre(z3[...], tab3[...], member)
    vb = centre(zp[...].astype(F32), tabp[...], member)
    vh3[...] = f2(va).astype(BF)
    vhp[...] = f2(vb).astype(BF)
    vh3.send()
    vhp.send()
    pre = affine(va, prm[0]) + affine(vb, prm[1])
    m = wide(f3(half_mask(info)), pre.shape[-1])
    sig = jax.nn.sigmoid(pre)
    low = f2(pre * sig * m).astype(BF)
    low_a[...] = low
    low_a.send()
    sl[...] = f2(m * (sig * (1.0 + pre * (1.0 - sig)))).astype(BF)
    sl.send()
    products(low, rbt, q, LB, own, ((1, s1), (2, s2), (3, s3)))


def k_flat(info, st, zb, prm, inv_count, sb, own, s1, s2, s3, im, vh, table, stats):
    q = info[0]
    member = member_of(info)
    totals = sums_all(st)
    inv8 = inv_count[4:8]
    for j in range(NB):
        table[j], stats[j] = stat_table(totals[j], inv8)
    vhat = centre(zb[...].astype(F32), table[q], member)
    vh[...] = f2(vhat).astype(BF)
    vh.send()
    act = f2(silu(affine(vhat, prm[2, q])) * f3(half_mask(info)) * keep_of(info, q))
    first, last = edge_cols()
    for t in range(3):
        shifted = rows_down(act) if t == 0 else (act if t == 1 else rows_up(act))
        for u in range(3):
            x = cols_right(shifted, first) if u == 0 else (shifted if u == 1 else cols_left(shifted, last))
            at = (3 * t + u) * LB
            im[:, at : at + LB] = x.astype(BF)
    im.send()
    products(im[...], sb, q, LB, own, ((1, s1), (2, s2), (3, s3)))


def k_expand_b(info, st, b0, b1, b2, b3, prm, inv_count, eb, z6, st6, act, vh, table, stats):
    act_all(info, st, (b0, b1, b2, b3), prm, 3, inv_count[4:8], act, vh, table, stats)
    z = dot_nn(act[...], matrix(eb))
    z6[...] = z
    spread(st6, two_sums(z, member_of(info)))


def k_output(info, st6, z6, low_a, cot, prm, inv_count, gb, vh6, st, output, gbs, tab6, stat6):
    member = member_of(info)
    tab6[...], stat6[...] = stat_table(sums_dp(st6), inv_count[4:8])
    vhat = centre(z6[...], tab6[...], member)
    vh6[...] = f2(vhat).astype(BF)
    pre = affine(vhat, prm[2]) + f3(low_a[...].astype(F32))
    m = wide(f3(half_mask(info)), pre.shape[-1])
    sig = jax.nn.sigmoid(pre)
    output[:, 0:PX, :] = pre * sig * m
    output[:, PX:, :] = jnp.zeros((FR, 64 - PX, pre.shape[-1]), F32)
    output.send()
    g = cot[...].astype(F32)[:, 0:PX, :] * m * (sig * (1.0 + pre * (1.0 - sig)))
    gb[...] = f2(g)
    gbs[...] = f2(g).astype(BF)
    gbs.send()
    along = by_subnet(jnp.sum(g * vhat, axis=1), member)
    offset = by_subnet(jnp.sum(g, axis=1), member)
    spread(st, jnp.concatenate([along, offset], axis=0))


def k_back_six(info, st, gb, vh6, tab6, prm, inv_count, eb, act5, own, s1, s2, s3, grad, pg):
    q = info[0]
    member = member_of(info)
    totals = sums_dp(st)
    pg[...] = param_grads(totals)
    vhat = f3(vh6[...].astype(F32))
    m = wide(f3(half_mask(info)), vhat.shape[-1])
    g = m * norm_back(f3(gb[...]), vhat, tab6[...], totals, inv_count[4:8], member, prm[2, 0:1])
    low = f2(g).astype(BF)
    products(low, eb, q, LB, own, ((1, s1), (2, s2), (3, s3)))
    grad[...] = dot_tn(act5[...], low).astype(BF)


def back_stat(g, vhat, member, gl, st):
    low = f2(g).astype(BF)
    gl[...] = low
    g = f3(low.astype(F32))
    along = by_subnet(jnp.sum(g * vhat, axis=1), member)
    offset = by_subnet(jnp.sum(g, axis=1), member)
    spread(st, jnp.concatenate([along, offset], axis=0))


def k_back_stat(norm):
    def body(info, own, r1, r2, r3, vh, prm, gl, st):
        q = info[0]
        part = own[...] + r1[...].astype(F32) + r2[...].astype(F32) + r3[...].astype(F32)
        vhat = f3(vh[...].astype(F32))
        g = f3(part * half_mask(info)) * keep_of(info, q) * slope(affine(vhat, prm[norm, q]))
        back_stat(g, vhat, member_of(info), gl, st)

    return body


def gz_all(info, st, grads, values, table, prm, norm, inv8, gz, pg, hold):
    q = info[0]
    member = member_of(info)
    totals = sums_all(st)
    for j in range(NB):
        pg[j] = param_grads(totals[j])
        hold[j] = totals[j]
    m = f3(half_mask(info))
    for k in range(NB):
        j = q ^ k
        vhat = f3(values(k, j).astype(F32))
        g = norm_back(f3(grads[k][...].astype(F32)), vhat, table[j], hold[j], inv8, member, prm[norm, j][0:1])
        gz[:, lanes_of(j, LB)] = f2(m * g).astype(BF)


def k_back_five(info, st, g0, g1, g2, g3, vh5, tab5, prm, inv_count, sb, vh4, im4, gl, st4, grad, pg, gz5, hold):
    q = info[0]
    gz_all(
        info, st, (g0, g1, g2, g3), lambda k, j: vh5[:, lanes_of(j, LB)], tab5, prm, 3, inv_count[4:8],
        gz5, pg, hold,
    )
    terms = dot_nn(gz5[...], sb[...])
    first, last = edge_cols()
    total = None
    for t in range(3):
        for u in range(3):
            at = (3 * t + u) * LB
            x = terms[:, at : at + LB]
            x = cols_left(x, last) if u == 0 else (x if u == 1 else cols_right(x, first))
            x = rows_up(x) if t == 0 else (x if t == 1 else rows_down(x))
            total = x if total is None else total + x
    vhat = f3(vh4[...].astype(F32))
    g = f3(total * half_mask(info)) * keep_of(info, q) * slope(affine(vhat, prm[2, q]))
    back_stat(g, vhat, member_of(info), gl, st4)
    grad[...] = dot_tn(gz5[...], im4[...]).astype(BF)


def k_back_four(info, st, g0, g1, g2, g3, v0, v1, v2, v3, tab4, prm, inv_count, rbt, gb, sl, vh3, vhp, low_a, ga, st3, grad, pg, gz4, hold):
    member = member_of(info)
    values = (v0, v1, v2, v3)
    gz_all(
        info, st, (g0, g1, g2, g3), lambda k, j: values[k][...], tab4, prm, 2, inv_count[4:8], gz4, pg, hold
    )
    low = gz4[...]
    back = dot_nn(low, matrix(rbt))
    g = (gb[...].astype(F32) + back) * sl[...].astype(F32)
    ga[...] = g
    g = f3(g)
    along = by_subnet(jnp.sum(g * f3(vh3[...].astype(F32)), axis=1), member)
    other = by_subnet(jnp.sum(g * f3(vhp[...].astype(F32)), axis=1), member)
    offset = by_subnet(jnp.sum(g, axis=1), member)
    half = offset.shape[-1] // 2
    tail = jnp.concatenate([offset[:, :half], offset[:, half:]], axis=0)
    spread(st3, jnp.concatenate([jnp.concatenate([along, other], axis=0), tail], axis=1))
    grad[...] = dot_tn(low, low_a[...]).astype(BF)


def k_back_join(info, st, ga, vh3, vhp, tab3, tabp, prm, inv_count, ea, act2, every, own, s1, s2, s3, gzp, *rest):
    q = info[0]
    member = member_of(info)
    grads, (pg3, pgp, full_a, full_s) = rest[:-4], rest[-4:]
    totals = sums_dp(st)
    lanes = ga.shape[-1]
    tail = totals[:, lanes:]
    offset = jnp.concatenate([tail[0:4], tail[4:8]], axis=1)
    tot3 = jnp.concatenate([totals[0:4, :lanes], offset], axis=0)
    totp = jnp.concatenate([totals[4:8, :lanes], offset], axis=0)
    pg3[...] = param_grads(tot3)
    pgp[...] = param_grads(totp)
    inv8 = inv_count[4:8]
    g = f3(ga[...])
    m = wide(f3(half_mask(info)), lanes)
    low = f2(m * norm_back(g, f3(vh3[...].astype(F32)), tab3[...], tot3, inv8, member, prm[0, 0:1])).astype(BF)
    products(low, ea, q, LB, own, ((1, s1), (2, s2), (3, s3)))
    lowp = f2(m * norm_back(g, f3(vhp[...].astype(F32)), tabp[...], totp, inv8, member, prm[1, 0:1])).astype(BF)
    gzp[...] = lowp
    full_a[...] = dot_tn(act2[...], low)
    full_s[...] = dot_tn(every[...], lowp)
    count = len(grads) // 2
    emit(info, full_a, grads[:count])
    emit(info, full_s, grads[count:])


def k_back_small(info, gzp, sc, own, near, far):
    q = info[0]
    low = gzp[...]
    own[...] = dot_nt(low, block(sc, q, 256))
    near[0] = dot_nt(low, block(sc, q ^ 1, 256)).astype(BF)
    near[1] = dot_nt(low, block(sc, q ^ 3, 256)).astype(BF)
    far[...] = dot_nt(low, block(sc, q ^ 2, 256))


def k_back_two(info, st, g0, g1, g2, g3, vh2, tab2, prm, inv_count, sa, vh1, im1, gl, st1, *rest):
    q = info[0]
    member = member_of(info)
    grads, (pg, gz2, hold, full) = rest[:-4], rest[-4:]
    gz_all(
        info, st, (g0, g1, g2, g3), lambda k, j: vh2[:, lanes_of(j, LB)], tab2, prm, 1, inv_count[4:8],
        gz2, pg, hold,
    )
    terms = dot_nn(gz2[...], sa[...])
    _, last = edge_cols()
    y = [terms[:, tap * LB : (tap + 1) * LB] for tap in range(9)]
    planes = [
        y[4],
        cols_left(y[3], last) + y[5],
        rows_up(y[1]) + y[7],
        rows_up(cols_left(y[0], last) + y[2]) + cols_left(y[6], last) + y[8],
    ]
    kept = keep_of(info, q)
    along = None
    offset = None
    for p in range(4):
        vhat = f3(vh1[p].astype(F32))
        g = f3(planes[p] * plane_mask(info, p)) * kept * slope(affine(vhat, prm[0, q]))
        low = f2(g).astype(BF)
        gl[p] = low
        g = f3(low.astype(F32))
        a, b = jnp.sum(g * vhat, axis=1), jnp.sum(g, axis=1)
        along = a if along is None else along + a
        offset = b if offset is None else offset + b
    spread(st1, jnp.concatenate([by_subnet(along, member), by_subnet(offset, member)], axis=0))
    full[...] = dot_tn(gz2[...], im1[...])
    emit(info, full, grads)


def k_last(info, st, g0, g1, g2, g3, v0, v1, v2, v3, tab1, prm, inv_count, xm, gz1, *rest):
    q = info[0]
    member = member_of(info)
    grads, (pg, hold, full) = rest[:-3], rest[-3:]
    totals = sums_all(st)
    inv16 = inv_count[0:4]
    for j in range(NB):
        pg[j] = param_grads(totals[j])
        hold[j] = totals[j]
    total = None
    for p in range(4):
        m = f3(plane_mask(info, p))
        for k, (gref, vref) in enumerate(((g0, v0), (g1, v1), (g2, v2), (g3, v3))):
            j = q ^ k
            vhat = f3(vref[p].astype(F32))
            g = norm_back(f3(gref[p].astype(F32)), vhat, tab1[j], hold[j], inv16, member, prm[0, j][0:1])
            gz1[p, :, lanes_of(j, LB)] = f2(m * g).astype(BF)
        term = dot_tn(gz1[p], xm[p])
        total = term if total is None else total + term
    full[...] = total
    emit(info, full, grads)


def k_features(info, gz1, rat, own, near, far, gf, nat):
    for p in range(4):
        back = dot_nn(gz1[p], rat[...])
        if p == 0:
            back = back + own[...] + near[0].astype(F32) + far[...].astype(F32)
        back = back * wide(plane_mask(info, p), back.shape[-1])
        high = back.astype(BF)
        nat[0, p] = high.astype(F32)
        nat[1, p] = back - high.astype(F32)
    row, col, target = natural_index(1)
    select = jnp.where(target == row * 16 + col, 1.0, 0.0).astype(BF)
    for frame in range(FR):
        out = None
        for part in range(2):
            x = jnp.concatenate(
                [nat[part, p, frame * PX : (frame + 1) * PX, :] for p in range(4)], axis=0
            ).astype(BF)
            y = dot_nn(select, x)
            out = y if out is None else out + y
        gf[frame] = out


def k_tables(info, *refs):
    mids, pairs, outs, gains = refs[0:4], refs[4:8], refs[8:11], refs[11:14]
    stats_mid, grads_mid, stats_out, grads_out = refs[14:]
    for i in range(4):
        for j in range(NB):
            at = slice(j * LB, (j + 1) * LB)
            stats_mid[i, 0, :, at] = mids[i][j, 0:4]
            stats_mid[i, 1, :, at] = mids[i][j, 4:8]
            grads_mid[i, :, at] = pairs[i][j]
    for i in range(3):
        stats_out[i, 0] = outs[i][0:4]
        stats_out[i, 1] = outs[i][4:8]
        grads_out[i] = gains[i][...]


def k_end_grads(info, grad, spatial, expand, reduce):
    value = grad[...].astype(F32)
    for tap in range(9):
        spatial[tap] = value[:, tap * LB : (tap + 1) * LB]
    lanes = expand.shape[-1]
    expand[...] = value[:, TAPS : TAPS + lanes]
    reduce[...] = value[:, TAPS + lanes :]


def k_taps_grad(info, *refs):
    total = refs[0][...].astype(F32)
    for ref in refs[1:-1]:
        total = total + ref[...].astype(F32)
    for tap in range(9):
        refs[-1][tap] = total[:, tap * LB : (tap + 1) * LB]


def swap(value, k):
    return lax.ppermute(value, "chan", [(i, i ^ k) for i in range(NB)])


def partners(value):
    return [value] + [swap(value, k) for k in (1, 2, 3)]


def partners_two_hops(value):
    far = swap(value, 2)
    return [value, swap(value, 1), far, swap(far, 1)]


def everywhere(value):
    return lax.all_to_all(value, ("dp", "chan"), 0, 0, tiled=True)


def along_dp(value):
    return lax.all_to_all(value, "dp", 0, 0, tiled=True)


def after(value, *others):
    return lax.optimization_barrier((value,) + others)[0]


def swap_dp(value, k):
    return lax.ppermute(value, "dp", [(i, i ^ k) for i in range(lax.axis_size("dp"))])


def hops_of(value, first, second):
    line = [value] + [swap_dp(after(value, *first), 2 * k) for k in (1, 2, 3)]
    return line + [swap_dp(after(v, *second), 1) for v in line]


def add_near(kept, away):
    return [(kept[k].astype(F32) + away[k].astype(F32)).astype(F32 if k == 0 else BF) for k in range(4)]


def add_far(parts):
    return parts[0] + parts[1].astype(F32) + parts[2].astype(F32) + parts[3].astype(F32)


def shards(
    features,
    cotangent,
    reduce_a,
    spatial_a,
    expand_a,
    shortcut,
    reduce_b,
    spatial_b,
    expand_b,
    norms_mid,
    norms_out,
    crop_side,
    subnet_of,
    width_of,
):
    ndp = lax.axis_size("dp")
    nall = ndp * NB
    hops = ndp == 8
    hidden = norms_mid.shape[-1]
    cin = features.shape[-1]
    cout = cotangent.shape[-1]
    rows = reduce_a.shape[1]
    er = expand_a.shape[0]
    sr = shortcut.shape[0]
    position = lax.axis_index("chan").astype(jnp.int32)
    place = lax.axis_index("dp").astype(jnp.int32)
    width = jnp.sum(
        jnp.where(subnet_of[:, None] == jnp.arange(4, dtype=jnp.int32)[None, :], width_of[None, :], 0), axis=1
    )
    info = jnp.concatenate([position[None], crop_side, subnet_of, width, place[None]])

    ra_t = reduce_a.T
    sa_t = jnp.transpose(spatial_a, (2, 0, 1)).reshape(rows, TAPS)
    half = (crop_side + 1) // 2
    per16 = jnp.where(crop_side > 8, crop_side * crop_side, 4 * crop_side * crop_side)
    per8 = jnp.where(half > 4, half * half, 4 * half * half)
    lane = jnp.arange(LB, dtype=jnp.int32)[None, :]
    pixels = jnp.where(lane == subnet_of[:, None], per16[:, None], 0)
    pixels = pixels + jnp.where(lane == subnet_of[:, None] + 4, per8[:, None], 0)
    pixels = jnp.concatenate([pixels.astype(F32), jnp.zeros((rows, LB), F32)], axis=0)[: max(rows, FR)]
    prm = Pinned(jnp.transpose(norms_mid.reshape(4, 2, NB, LB), (0, 2, 1, 3)))
    prm_out = Pinned(norms_out)
    table = ((NB, 8, LB), F32, "hbm")
    one_block = ((NP, LB), F32)
    send = ((NP, LB), BF)
    sends = [one_block, send, send, send]
    stat_all = ((nall, 8, LB), F32)
    stat_own = ((ndp, 8, cout), F32)
    stat_wide = ((ndp, 8, cout + cout // 2), F32)
    map_out = ((NP, cout), F32)
    low_out = ((NP, cout), BF, "hbm")
    low_mid = ((NP, hidden), BF, "hbm")
    tab_out = ((8, cout), F32, "hbm")

    xm, xs, small = call(
        k_prep, [((4, NP, cin), BF), ((4, NP, cin), BF, "hbm"), ((NP, cin), BF)],
        info, Pinned(features.reshape(FR, 256, cin)), name="prep",
    )
    if hops:
        pieces = hops_of(jnp.concatenate([sa_t, ra_t, pixels.astype(BF)], axis=1), (), (small,))
        sa = Gathered(pieces, rows, 0, TAPS)
        rat = Gathered(pieces, rows, TAPS, cin)
        counts = Gathered(pieces, 16, TAPS + cin, LB)
    else:
        rat = Pinned(lax.all_gather(ra_t, "dp", axis=0, tiled=True))
        sa = Pinned(lax.all_gather(sa_t, "dp", axis=0, tiled=True))
        counts = Pinned(lax.psum(pixels, "dp"))
    own, near, far = call(
        k_first, [((4, NP, LB), F32), ((2, 4, NP, LB), BF), ((4, NP, LB), F32)], info, xm, rat, name="first"
    )
    near = swap(near, 1)
    far = (far + near[1].astype(F32)).astype(BF)
    pack_mid = after(jnp.concatenate([expand_a, shortcut, after(reduce_b, small).T], axis=0), own)
    mid = lax.all_gather(pack_mid, "dp", axis=0)

    def mid_rows(first, size):
        if size % 16 == 0:
            return Pinned(mid, lambda ref, info: ref.at[:, first : first + size, :], (ndp, size, cout))
        return Pinned(mid[:, first : first + size].reshape(ndp * size, cout))

    ea = mid_rows(0, er)
    sc = mid_rows(er, sr)
    rbt = mid_rows(er + sr, rows)
    pack_end = jnp.concatenate(
        [jnp.transpose(spatial_b, (2, 0, 1)).reshape(rows, TAPS), expand_b], axis=1
    )
    end = lax.all_gather(pack_end, "dp", axis=0, tiled=True)
    sb = Pinned(end, lambda ref, info: ref.at[:, 0:TAPS], (hidden, TAPS))
    eb = Pinned(end, lambda ref, info: ref.at[:, TAPS : TAPS + cout], (hidden, cout))

    far = swap(far, 2)
    zb1, st = call(
        k_stat_first, [((4, NP, LB), BF), stat_all], info, own, near, far, name="stat_one"
    )
    smalls = partners_two_hops(after(small, st))
    st = after(everywhere(st), *smalls[1:])
    own, s1, s2, s3, im1, vh1, tab1, inv_count, stat1 = call(
        k_down,
        sends + [((NP, TAPS), BF, "hbm"), ((4, NP, LB), BF, "hbm"), table, ((8, LB), F32, "hbm"), table],
        info, st, zb1, prm, sa, counts, name="down",
    )
    inv_count = Pinned(inv_count)
    zb, st = call(k_stat, [send, stat_all], info, own, swap(s1, 1), swap(s2, 2), swap(s3, 3), name="stat_two")
    zs = partners(zb)
    smalls = lax.optimization_barrier(tuple(smalls) + (st,))[:4]
    stp, every, zp = call(
        k_proj, [((8, cout), F32), ((NP, NB * cin), BF, "hbm"), low_out], info, *smalls, sc, name="proj"
    )
    st = after(everywhere(st), stp)
    stx = swap_dp(stp, 1)
    z3, st3, act2, vh2, tab2, stat2 = call(
        k_expand_a, [map_out, stat_wide, low_mid, low_mid, table, table],
        info, st, *zs, stp, stx, prm, inv_count, ea, scratch=[pltpu.VMEM((8, cout), F32)], name="expand_a",
    )
    st3 = along_dp(st3)
    own, s1, s2, s3, low_a, sl, vh3, vhp, tab3, tabp, stat3, statp = call(
        k_join, sends + [low_out, low_out, low_out, low_out, tab_out, tab_out, tab_out, tab_out],
        info, st3, z3, Pinned(zp), prm_out, inv_count, rbt, name="join",
    )
    zb, st = call(k_stat, [send, stat_all], info, own, swap(s1, 1), swap(s2, 2), swap(s3, 3), name="stat_four")
    st = everywhere(st)
    own, s1, s2, s3, im4, vh4, tab4, stat4 = call(
        k_flat, sends + [((NP, TAPS), BF, "hbm"), ((NP, LB), BF, "hbm"), table, table],
        info, st, zb, prm, inv_count, sb, name="flat",
    )
    zb, st = call(k_stat, [send, stat_all], info, own, swap(s1, 1), swap(s2, 2), swap(s3, 3), name="stat_five")
    zs = partners(zb)
    st = everywhere(st)
    z6, st6, act5, vh5, tab5, stat5 = call(
        k_expand_b, [map_out, stat_own, low_mid, low_mid, table, table],
        info, st, *zs, prm, inv_count, eb, name="expand_b",
    )
    vhs4 = partners(after(vh4, st6))
    st6 = after(along_dp(st6), *vhs4[1:])
    gb, vh6, st, output, gbs, tab6, stat6 = call(
        k_output,
        [map_out, ((NP, cout), BF), stat_own, ((FR, 64, cout), F32, "hbm"), low_out, tab_out, tab_out],
        info, st6, z6, Pinned(low_a), Pinned(cotangent.reshape(FR, 64, cout)), prm_out, inv_count, name="output",
    )

    wide_grad = TAPS + 2 * cout

    def into(first, size, dtype=BF):
        return ((hidden, wide_grad), dtype, "hbm", lambda ref: ref.at[:, first : first + size], (hidden, size))

    def reduced(size, width_):
        if hops:
            return [((4, size, width_), BF, "hbm")] * 2
        return [((ndp * size, width_), BF, "hbm")]

    def own_lanes(array):
        return Pinned(array, lambda ref, info: ref.at[:, lanes_of(info[0], LB)], (NP, LB))

    vh1_in = after(vh1, st)
    vhs1 = [vh1, swap(vh1_in, 1), swap(vh1_in, 2)]
    st = after(along_dp(st), *vhs1[1:])
    own, s1, s2, s3, end_grad, pg6 = call(
        k_back_six, sends + [into(TAPS, cout), ((2, cout), F32, "hbm")],
        info, st, gb, vh6, Pinned(tab6), prm_out, inv_count, eb, Pinned(act5), name="back_six",
    )
    gl, st = call(
        k_back_stat(3), [send, stat_all],
        info, own, swap(s1, 1), swap(s2, 2), swap(s3, 3), own_lanes(vh5), prm, name="back_stat_five",
    )
    gs = partners(gl)
    st = everywhere(st)
    hold = pltpu.VMEM((NB, 8, LB), F32)
    pair_mid = ((NB, 2, LB), F32, "hbm")
    gl, st, end_grad, pg5 = call(
        k_back_five, [send, stat_all, into(0, TAPS), pair_mid],
        info, st, *gs, Pinned(vh5), Pinned(tab5), prm, inv_count, sb, Pinned(vh4), Pinned(im4),
        scratch=[pltpu.VMEM((NP, hidden), BF), hold], alias=(end_grad, 2), name="back_five",
    )
    gs = partners(gl)
    st = everywhere(st)
    ga, st, end_grad, pg4 = call(
        k_back_four, [map_out, stat_wide, into(TAPS + cout, cout), pair_mid],
        info, st, *gs, *[Pinned(v) for v in vhs4], Pinned(tab4), prm, inv_count, rbt, Pinned(gbs), Pinned(sl),
        Pinned(vh3), Pinned(vhp), Pinned(low_a),
        scratch=[pltpu.VMEM((NP, hidden), BF), hold], alias=(end_grad, 2), name="back_four",
    )
    vhs1.append(swap(after(vhs1[2], st), 1))
    st = after(along_dp(st), vhs1[3])
    end_grad = lax.psum_scatter(after(end_grad, st), "dp", scatter_dimension=0, tiled=True)
    grad_as = reduced(er, cout) + reduced(sr, cout)
    own, s1, s2, s3, gzp, *rest = call(
        k_back_join,
        sends + [((NP, cout), BF)] + grad_as + [((2, cout), F32, "hbm")] * 2,
        info, st, ga, Pinned(vh3), Pinned(vhp), Pinned(tab3), Pinned(tabp), prm_out, inv_count, ea,
        Pinned(act2), Pinned(every),
        scratch=[pltpu.VMEM((hidden, cout), F32), pltpu.VMEM((ndp * sr, cout), F32)], name="back_join",
    )
    grad_as, (pg3, pgp) = rest[:-2], rest[-2:]
    r1, r2, r3 = swap(s1, 1), swap(s2, 2), swap(s3, 3)
    if hops:
        away_a = swap_dp(grad_as[0], 1)
        own = after(own, away_a)
    sown, near, far = call(
        k_back_small, [((NP, cin), F32), ((2, NP, cin), BF), ((NP, cin), F32)],
        info, after(gzp, r1), sc, name="back_small",
    )
    own = after(own, sown)
    gl, st = call(
        k_back_stat(1), [send, stat_all],
        info, own, r1, r2, r3, own_lanes(vh2), prm, name="back_stat_two",
    )
    gs = partners(gl)
    if hops:
        away_s = swap_dp(after(grad_as[2], gs[1]), 1)
        sums = add_near(after(grad_as[1], gs[1]), away_a)
        grad_a = [sums[0]] + [swap_dp(sums[k], 2 * k) for k in (1, 2, 3)]
    st = everywhere(st)
    if hops:
        st = after(st, away_s, *grad_a[1:])
    near = swap(near, 1)
    far = (far + near[1].astype(F32)).astype(BF)
    grad_sa = reduced(rows, TAPS)
    gl, st, *rest = call(
        k_back_two, [((4, NP, LB), BF), stat_all] + grad_sa + [pair_mid],
        info, st, *gs, Pinned(vh2), Pinned(tab2), prm, inv_count, sa, Pinned(vh1), Pinned(im1),
        scratch=[pltpu.VMEM((NP, hidden), BF), hold, pltpu.VMEM((hidden, TAPS), F32)], name="back_two",
    )
    grad_sa, pg2 = rest[:-1], rest[-1]
    gs = [gl, swap(gl, 1), swap(gl, 2)]
    if hops:
        st = after(st, far)
    st = everywhere(st)
    gs.append(swap(after(gs[2], st), 1))
    far = swap(after(far, gs[3]), 2)
    if hops:
        away_sa = swap_dp(after(grad_sa[0], gs[1]), 1)
        sums = add_near(after(grad_as[3], gs[1]), away_s)
        st = after(st, *sums, away_sa)
        grad_s = [sums[0]] + [swap_dp(sums[k], 2 * k) for k in (1, 2, 3)]
    grad_rat = reduced(rows, cin)
    gz1, *rest = call(
        k_last, [((4, NP, hidden), BF)] + grad_rat + [pair_mid],
        info, st, *gs, *[Pinned(v) for v in vhs1], Pinned(tab1), prm, inv_count, Pinned(xs),
        scratch=[hold, pltpu.VMEM((hidden, cin), F32)], name="last",
    )
    grad_rat, pg1 = rest[:-1], rest[-1]
    if hops:
        sums_sa = add_near(after(grad_sa[1], gz1), away_sa)
        parts_sa = [sums_sa[0]] + [swap_dp(sums_sa[k], 2 * k) for k in (1, 2, 3)]
        kept = after(grad_rat[1], *sums_sa)
        sums_ra = add_near(kept, swap_dp(grad_rat[0], 1))
        parts_ra = [sums_ra[0]] + [swap_dp(sums_ra[k], 2 * k) for k in (1, 2, 3)]
        gz1 = after(gz1, sums_ra[0])
        pg1 = after(pg1, sums_ra[0])
    spatial, expand, reduce = call(
        k_end_grads,
        [((9, rows, LB), F32, "hbm"), ((er, cout), F32, "hbm"), ((rows, cout), F32, "hbm")],
        info, Pinned(after(end_grad, gz1)), name="end_grads",
    )
    stats_mid, grad_norms_mid, stats_out, grad_norms_out = call(
        k_tables,
        [
            ((4, 2, 4, hidden), F32, "hbm"), ((4, 2, hidden), F32, "hbm"),
            ((3, 2, 4, cout), F32, "hbm"), ((3, 2, cout), F32, "hbm"),
        ],
        info,
        *[Pinned(x) for x in (stat1, stat2, stat4, stat5, pg1, pg2, pg4, pg5, stat3, statp, stat6, pg3, pgp, pg6)],
        name="tables",
    )
    gf = call(
        k_features, [((FR, 256, cin), F32, "hbm")],
        info, gz1, rat, Pinned(sown), near, far,
        scratch=[pltpu.VMEM((2, 4, NP, cin), F32)], name="features",
    )[0]
    if hops:
        grad_rat = add_far([after(x, gf) for x in parts_ra])
        grad_a = add_far([after(x, gf) for x in grad_a])
        grad_s = add_far([after(x, gf) for x in grad_s])
        parts_sa = [after(x, gf) for x in parts_sa]
    else:
        grad_a, grad_s, grad_sa, grad_rat = [
            lax.psum_scatter(g, "dp", scatter_dimension=0, tiled=True).astype(F32)
            for g in (*grad_as, grad_sa[0], grad_rat[0])
        ]
        parts_sa = [grad_sa]
    spatial_sa = call(k_taps_grad, [((9, rows, LB), F32, "hbm")], info, *parts_sa, name="taps_grad")[0]
    grad_reduce_a = grad_rat.T
    grad_spatial_a = jnp.transpose(spatial_sa, (0, 2, 1))
    grad_spatial_b = jnp.transpose(spatial, (0, 2, 1))
    grad_expand_b = expand
    grad_reduce_b = reduce.T
    return (
        output.reshape(FR, 8, 8, cout),
        gf.reshape(FR, 16, 16, cin),
        grad_reduce_a,
        grad_spatial_a,
        grad_a,
        grad_s,
        grad_reduce_b,
        grad_spatial_b,
        grad_expand_b,
        grad_norms_mid,
        grad_norms_out,
        stats_mid,
        stats_out,
    )


def solution(mesh):
    in_specs = (
        P("dp", None, None, "chan"),
        P("dp", None, None, "chan"),
        P("chan", "dp"),
        P(None, "chan", "dp"),
        P("dp", "chan"),
        P("dp", "chan"),
        P("chan", "dp"),
        P(None, "chan", "dp"),
        P("dp", "chan"),
        P(),
        P(None, None, "chan"),
        P("dp"),
        P("dp"),
        P(),
    )
    out_specs = (
        P("dp", None, None, "chan"),
        P("dp", None, None, "chan"),
        P("chan", "dp"),
        P(None, "chan", "dp"),
        P("dp", "chan"),
        P("dp", "chan"),
        P("chan", "dp"),
        P(None, "chan", "dp"),
        P("dp", "chan"),
        P(),
        P(None, None, "chan"),
        P(),
        P(None, None, None, "chan"),
    )
    return jax.shard_map(shards, mesh=mesh, in_specs=in_specs, out_specs=out_specs, check_vma=False)
```

```python
import jax
import jax.numpy as jnp
from jax import lax
from jax.experimental import pallas as pl
from jax.experimental.pallas import tpu as pltpu
from jax.sharding import PartitionSpec as P

EPSILON = 1e-05
BF = jnp.bfloat16
F32 = jnp.float32
FR = 8
RP = 7
QP = 8
PX = RP * QP
NP = FR * PX
LB = 128
NB = 4
TAPS = 9 * LB


class Pinned:
    def __init__(self, array, view=None, shape=None):
        self.array = array
        self.view = view
        self.shape = array.shape if shape is None else shape


class Gathered:
    def __init__(self, pieces, rows, first, lanes):
        self.pieces = pieces
        self.rows = rows
        self.window = (slice(0, rows), slice(first, first + lanes))
        self.shape = (8 * rows, lanes)


class Late:
    def __init__(self, ref, copies):
        self.ref = ref
        self.copies = copies
        self.waiting = True

    def ready(self):
        if self.waiting:
            for copy in self.copies:
                copy.wait()
            self.waiting = False
        return self.ref

    def __getitem__(self, index):
        return self.ready()[index]

    @property
    def shape(self):
        return self.ref.shape


class Saved:
    def __init__(self, ref, copy):
        self.ref = ref
        self.copy = copy
        self.sent = False

    def __setitem__(self, index, value):
        self.ref[index] = value

    def __getitem__(self, index):
        return self.ref[index]

    @property
    def shape(self):
        return self.ref.shape

    def send(self):
        self.sent = True
        self.copy.start()


def call(body, outs, info, *args, scratch=(), name, alias=None):
    flat = []
    buffers = []
    copies = 0
    for a in args:
        if isinstance(a, Gathered):
            flat += [(p, True) for p in a.pieces]
            buffers.append(pltpu.VMEM(a.shape, a.pieces[0].dtype))
            copies += 8
        elif isinstance(a, Pinned):
            flat.append((a.array, True))
            buffers.append(pltpu.VMEM(a.shape, a.array.dtype))
            copies += 1
        else:
            flat.append((a, False))
    saved = [len(o) > 2 for o in outs]
    for o, s in zip(outs, saved):
        if s:
            buffers.append(pltpu.VMEM(o[4] if len(o) > 3 else o[0], o[1]))
            copies += 1
    extra = [] if alias is None else [alias[0]]
    arrays = [pltpu.with_memory_space_constraint(a, pltpu.HBM) if p else a for a, p in flat]
    arrays += [pltpu.with_memory_space_constraint(a, pltpu.HBM) for a in extra]
    vmem = pl.BlockSpec(memory_space=pltpu.VMEM)
    hbm = pl.BlockSpec(memory_space=pltpu.HBM)

    def kernel(*refs):
        refs = list(refs)
        info_ref = refs.pop(0)
        ins = refs[: len(flat)]
        refs = refs[len(flat) + len(extra) :]
        results, refs = refs[: len(outs)], refs[len(outs) :]
        bufs, refs = refs[: len(buffers)], refs[len(buffers) :]
        if copies:
            sems, refs = refs[0], refs[1:]
        used = 0
        given = []
        late = []
        for a in args:
            if not isinstance(a, (Gathered, Pinned)):
                given.append(ins.pop(0))
                continue
            buf = bufs.pop(0)
            moves = []
            if isinstance(a, Gathered):
                blocks = []
                for piece in a.pieces:
                    ref = ins.pop(0)
                    blocks += [ref] if len(piece.shape) == 2 else [ref.at[k] for k in range(4)]
                for i in range(8):
                    source = info_ref[25] ^ (2 * (i % 4)) ^ (i // 4)
                    rows = pl.ds(pl.multiple_of(source * a.rows, a.rows), a.rows)
                    moves.append(pltpu.make_async_copy(blocks[i].at[a.window], buf.at[rows], sems.at[used]))
                    used += 1
            else:
                ref = ins.pop(0)
                source = ref if a.view is None else a.view(ref, info_ref)
                moves.append(pltpu.make_async_copy(source, buf, sems.at[used]))
                used += 1
            for move in moves:
                move.start()
            late.append(Late(buf, moves))
            given.append(late[-1])
        produced = []
        outgoing = []
        for o, s, ref in zip(outs, saved, results):
            if s:
                buf = bufs.pop(0)
                target = o[3](ref) if len(o) > 3 else ref
                ref = Saved(buf, pltpu.make_async_copy(buf, target, sems.at[used]))
                used += 1
                outgoing.append(ref)
            produced.append(ref)
        body(info_ref, *given, *produced, *refs)
        for one in outgoing:
            if not one.sent:
                one.send()
        for one in late:
            one.ready()
        for one in outgoing:
            one.copy.wait()

    return pl.pallas_call(
        kernel,
        out_shape=[(pltpu.HBM if s else jax.ShapeDtypeStruct)(o[0], o[1]) for o, s in zip(outs, saved)],
        in_specs=[pl.BlockSpec(memory_space=pltpu.SMEM)]
        + [hbm if p else vmem for _, p in flat]
        + [hbm] * len(extra),
        out_specs=[hbm if s else vmem for s in saved],
        scratch_shapes=buffers + ([pltpu.SemaphoreType.DMA((copies,))] if copies else []) + list(scratch),
        input_output_aliases={} if alias is None else {1 + len(flat): alias[1]},
        compiler_params=pltpu.CompilerParams(vmem_limit_bytes=40 << 20),
        cost_estimate=pl.CostEstimate(flops=1, bytes_accessed=1, transcendentals=0),
        name=name,
    )(info, *arrays)


def f3(value):
    return value.reshape(FR, PX, value.shape[-1])


def f2(value):
    return value.reshape(NP, value.shape[-1])


def wide(value, lanes):
    count = lanes // value.shape[-1]
    return value if count == 1 else jnp.concatenate([value] * count, axis=-1)


def dot_nn(left, right):
    return lax.dot_general(left, right, (((1,), (0,)), ((), ())), preferred_element_type=F32)


def dot_nt(left, right):
    return lax.dot_general(left, right, (((1,), (1,)), ((), ())), preferred_element_type=F32)


def dot_tn(left, right):
    return lax.dot_general(left, right, (((0,), (0,)), ((), ())), preferred_element_type=F32)


def frame_scalars(info, first):
    row = lax.broadcasted_iota(jnp.int32, (FR, LB), 0)
    out = jnp.zeros((FR, LB), jnp.int32)
    for frame in range(FR):
        out = jnp.where(row == frame, info[first + frame], out)
    return out


def member_of(info):
    subnet = frame_scalars(info, 9)
    return [(subnet == s).astype(F32) for s in range(4)]


def keep_of(info, j):
    lane = lax.broadcasted_iota(jnp.int32, (FR, LB), 1) + j * LB
    return (lane < frame_scalars(info, 17)).astype(F32)[:, None, :]


def crop_mask(info, half, row_scale, row_off, col_scale, col_off):
    at = lax.broadcasted_iota(jnp.int32, (PX, LB), 0)
    row = (at >> 3) * row_scale + row_off
    col = (at & 7) * col_scale + col_off
    parts = []
    for frame in range(FR):
        side = info[1 + frame]
        if half:
            side = (side + 1) >> 1
        full = 8 if half else 16
        period = jnp.where(side > full // 2, full, full // 2)
        inside = ((row & (period - 1)) < side) & ((col & (period - 1)) < side)
        parts.append(jnp.where(inside, 1.0, 0.0).astype(F32))
    return jnp.concatenate(parts, axis=0)


def plane_mask(info, plane):
    return crop_mask(info, 0, 2, plane // 2, 2, plane % 2)


def half_mask(info):
    return crop_mask(info, 1, 1, 0, 1, 0)


def by_subnet(frames, member):
    lanes = frames.shape[-1]
    return jnp.concatenate(
        [jnp.sum(frames * wide(member[s], lanes), axis=0, keepdims=True) for s in range(4)], axis=0
    )


def by_frame(table, member):
    lanes = table.shape[-1]
    total = None
    for s in range(4):
        term = wide(member[s], lanes) * table[s : s + 1, :]
        total = term if total is None else total + term
    return total[:, None, :]


def sum_px(value):
    return jnp.sum(f3(value), axis=1)


def stat_table(totals, inv_count):
    inv_n = wide(inv_count, totals.shape[-1])
    mean = totals[0:4] * inv_n
    var = totals[4:8] * inv_n - mean * mean
    return jnp.concatenate([mean, lax.rsqrt(var + EPSILON)], axis=0), jnp.concatenate([mean, var], axis=0)


def centre(value, table, member):
    return (f3(value) - by_frame(table[0:4], member)) * by_frame(table[4:8], member)


def affine(vhat, prm):
    return prm[0:1][None] * vhat + prm[1:2][None]


def silu(pre):
    return pre * jax.nn.sigmoid(pre)


def slope(pre):
    sig = jax.nn.sigmoid(pre)
    return sig * (1.0 + pre * (1.0 - sig))


def norm_back(grads, vhat, table, totals, inv_count, member, gain):
    inv_n = wide(inv_count, totals.shape[-1])
    along = by_frame(totals[0:4] * inv_n, member)
    offset = by_frame(totals[4:8] * inv_n, member)
    factor = by_frame(table[4:8], member) * gain[None]
    return factor * (grads - offset - vhat * along)


def param_grads(totals):
    return jnp.concatenate(
        [jnp.sum(totals[0:4], axis=0, keepdims=True), jnp.sum(totals[4:8], axis=0, keepdims=True)], axis=0
    )


def rows_down(value):
    cube = f3(value)
    return f2(jnp.concatenate([jnp.zeros((FR, QP, cube.shape[-1]), F32), cube[:, : PX - QP]], axis=1))


def rows_up(value):
    cube = f3(value)
    return f2(jnp.concatenate([cube[:, QP:], jnp.zeros((FR, QP, cube.shape[-1]), F32)], axis=1))


def cols_right(value, first):
    return jnp.where(first, 0.0, pltpu.roll(value, 1, 0))


def cols_left(value, last):
    return jnp.where(last, 0.0, pltpu.roll(value, NP - 1, 0))


def edge_cols():
    at = lax.broadcasted_iota(jnp.int32, (NP, LB), 0) & 7
    return at == 0, at == 7


def block(ref, index, size):
    if len(ref.shape) == 2:
        return ref[pl.ds(pl.multiple_of(index * size, size), size), :]
    step = size // ref.shape[1]
    return ref[pl.ds(index * step, step)].reshape(size, ref.shape[-1])


def matrix(ref):
    value = ref[...]
    return value if len(value.shape) == 2 else value.reshape(-1, value.shape[-1])


def lanes_of(index, size):
    return pl.ds(pl.multiple_of(index * size, size), size)


def sums_all(ref):
    count = ref.shape[0] // NB
    out = []
    for j in range(NB):
        total = ref[j]
        for d in range(1, count):
            total = total + ref[NB * d + j]
        out.append(total)
    return out


def sums_dp(ref):
    total = ref[0]
    for d in range(1, ref.shape[0]):
        total = total + ref[d]
    return total


def spread(ref, value):
    for d in range(ref.shape[0]):
        ref[d] = value


def products(low, weight, q, size, own, others):
    own[...] = dot_nt(low, block(weight, q, size))
    for k, ref in others:
        ref[...] = dot_nt(low, block(weight, q ^ k, size)).astype(BF)


def by_x_first(value, count):
    if count != 8:
        return value
    rows = value.shape[0] // 8
    return jnp.concatenate(
        [value[(2 * z + x) * rows : (2 * z + x + 1) * rows] for x in range(2) for z in range(4)], axis=0
    )


def emit(info, full, outs, first=0):
    if len(outs) == 1:
        outs[0][...] = full[...].astype(BF)
        return
    away, kept = outs
    rows = full.shape[0] // 8
    here = info[25]
    to = slice(first, first + rows)
    for k in range(4):
        target = here ^ (2 * k)
        kept[k, to] = full[pl.ds(pl.multiple_of(target * rows, rows), rows), :].astype(BF)
        away[k, to] = full[pl.ds(pl.multiple_of((target ^ 1) * rows, rows), rows), :].astype(BF)


def natural_index(axis):
    shape = (4 * PX, 256) if axis == 0 else (256, 4 * PX)
    at = lax.broadcasted_iota(jnp.int32, shape, axis)
    plane = (
        (at >= PX).astype(jnp.int32) + (at >= 2 * PX).astype(jnp.int32) + (at >= 3 * PX).astype(jnp.int32)
    )
    inner = at - PX * plane
    row = (inner >> 3) * 2 + (plane >> 1)
    col = (inner & 7) * 2 + (plane & 1)
    return row, col, lax.broadcasted_iota(jnp.int32, shape, 1 - axis)


def k_prep(info, feat, xm, xs, small):
    row, col, source = natural_index(0)
    hit = source == row * 16 + col
    for pair in range(FR // 2):
        picked = []
        for frame in (2 * pair, 2 * pair + 1):
            side = info[1 + frame]
            period = jnp.where(side > 8, 16, 8)
            inside = ((row & (period - 1)) < side) & ((col & (period - 1)) < side)
            select = jnp.where(hit & inside, 1.0, 0.0).astype(BF)
            picked.append(dot_nn(select, feat[frame]))
        for p in range(4):
            both = jnp.concatenate([x[p * PX : (p + 1) * PX] for x in picked], axis=0)
            xm[p, pair * 2 * PX : (pair + 1) * 2 * PX, :] = both.astype(BF)
    xs[...] = xm[...]
    small[...] = xm[0]


def k_first(info, xm, rat, *refs):
    q = info[0]
    own, near, far = refs[-3:] if len(refs) == 3 else refs[4:7]
    if len(refs) > 3:
        for k in range(4):
            refs[7][k] = refs[k][...]
        refs[7].send()
    weights = [block(rat, q ^ k, LB) for k in range(4)]
    for p in range(4):
        x = xm[p]
        own[p] = dot_nt(x, weights[0])
        near[0, p] = dot_nt(x, weights[1]).astype(BF)
        near[1, p] = dot_nt(x, weights[3]).astype(BF)
        far[p] = dot_nt(x, weights[2])


def k_stat_first(info, own, near, far, zb, st):
    member = member_of(info)
    sums = None
    squares = None
    for p in range(4):
        low = (own[p] + near[0, p].astype(F32) + far[p].astype(F32)).astype(BF)
        zb[p] = low
        z = low.astype(F32)
        a, b = sum_px(z), sum_px(z * z)
        sums = a if sums is None else sums + a
        squares = b if squares is None else squares + b
    spread(st, jnp.concatenate([by_subnet(sums, member), by_subnet(squares, member)], axis=0))


def k_down(info, st, zb, prm, sa, counts, own, s1, s2, s3, im, vh, table, inv_count, stats):
    q = info[0]
    member = member_of(info)
    totals = sums_all(st)
    pixels = jnp.sum(counts[...].astype(F32), axis=0, keepdims=True)
    lane = lax.broadcasted_iota(jnp.int32, (1, LB), 1)
    for s in range(8):
        here = jnp.sum(jnp.where(lane == s, pixels, 0.0), axis=1, keepdims=True)
        inv_count[s : s + 1, :] = jnp.broadcast_to(1.0 / here, (1, LB))
    inv16 = inv_count[0:4, :]
    for j in range(NB):
        table[j], stats[j] = stat_table(totals[j][0:8], inv16)
    tab = table[q]
    kept = keep_of(info, q)
    par = prm[0, q]
    first, _ = edge_cols()
    planes = []
    for p in range(4):
        vhat = centre(zb[p].astype(F32), tab, member)
        vh[p] = f2(vhat).astype(BF)
        planes.append(f2(silu(affine(vhat, par)) * f3(plane_mask(info, p)) * kept))
    vh.send()
    for t in range(3):
        for u in range(3):
            x = planes[(0 if t == 1 else 2) + (0 if u == 1 else 1)]
            if t == 0:
                x = rows_down(x)
            if u == 0:
                x = cols_right(x, first)
            at = (3 * t + u) * LB
            im[:, at : at + LB] = x.astype(BF)
    im.send()
    products(im[...], sa, q, LB, own, ((1, s1), (2, s2), (3, s3)))


def k_stat(info, own, r1, r2, r3, zb, st):
    member = member_of(info)
    low = (own[...] + r1[...].astype(F32) + r2[...].astype(F32) + r3[...].astype(F32)).astype(BF)
    zb[...] = low
    z = low.astype(F32)
    zm = z * half_mask(info)
    total = jnp.concatenate([by_subnet(sum_px(zm), member), by_subnet(sum_px(zm * z), member)], axis=0)
    spread(st, total)


def act_all(info, st, blocks, prm, norm, inv8, act, vh, table, stats):
    q = info[0]
    member = member_of(info)
    totals = sums_all(st)
    for j in range(NB):
        table[j], stats[j] = stat_table(totals[j], inv8)
    m = f3(half_mask(info))
    for k in range(NB):
        j = q ^ k
        vhat = centre(blocks[k][...].astype(F32), table[j], member)
        vh[:, lanes_of(j, LB)] = f2(vhat).astype(BF)
        a = silu(affine(vhat, prm[norm, j])) * m * keep_of(info, j)
        act[:, lanes_of(j, LB)] = f2(a).astype(BF)
    vh.send()
    act.send()


def two_sums(z, member):
    return jnp.concatenate([by_subnet(sum_px(z), member), by_subnet(sum_px(z * z), member)], axis=0)


def k_proj(info, x0, x1, x2, x3, sc, st, every, zp):
    q = info[0]
    for k, ref in enumerate((x0, x1, x2, x3)):
        every[:, lanes_of(q ^ k, 256)] = ref[...]
    every.send()
    z = dot_nn(every[...], matrix(sc))
    zp[...] = z.astype(BF)
    zp.send()
    st[...] = two_sums(z, member_of(info))


def k_expand_a(info, st, b0, b1, b2, b3, stp, stx, prm, inv_count, ea, z3, st3, act, vh, table, stats, hold):
    act_all(info, st, (b0, b1, b2, b3), prm, 1, inv_count[4:8], act, vh, table, stats)
    z = dot_nn(act[...], matrix(ea))
    z3[...] = z
    hold[...] = stp[...] + stx[...]
    half = hold.shape[1] // 2
    part = hold[:, lanes_of(info[25] & 1, half)]
    spread(st3, jnp.concatenate([two_sums(z, member_of(info)), part], axis=1))


def k_join(info, st3, z3, zp, prm, inv_count, rbt, own, s1, s2, s3, low_a, sl, vh3, vhp, tab3, tabp, stat3, statp):
    q = info[0]
    member = member_of(info)
    inv8 = inv_count[4:8]
    lanes = z3.shape[1]
    even, odd = st3[0], st3[1]
    for d in range(2, st3.shape[0], 2):
        even = even + st3[d]
        odd = odd + st3[d + 1]
    tab3[...], stat3[...] = stat_table(even[:, :lanes] + odd[:, :lanes], inv8)
    tabp[...], statp[...] = stat_table(jnp.concatenate([even[:, lanes:], odd[:, lanes:]], axis=1), inv8)
    va = centre(z3[...], tab3[...], member)
    vb = centre(zp[...].astype(F32), tabp[...], member)
    vh3[...] = f2(va).astype(BF)
    vhp[...] = f2(vb).astype(BF)
    vh3.send()
    vhp.send()
    pre = affine(va, prm[0]) + affine(vb, prm[1])
    m = wide(f3(half_mask(info)), pre.shape[-1])
    sig = jax.nn.sigmoid(pre)
    low = f2(pre * sig * m).astype(BF)
    low_a[...] = low
    low_a.send()
    sl[...] = f2(m * (sig * (1.0 + pre * (1.0 - sig)))).astype(BF)
    sl.send()
    products(low, rbt, q, LB, own, ((1, s1), (2, s2), (3, s3)))


def k_flat(info, st, zb, prm, inv_count, sb, own, s1, s2, s3, im, vh, table, stats):
    q = info[0]
    member = member_of(info)
    totals = sums_all(st)
    inv8 = inv_count[4:8]
    for j in range(NB):
        table[j], stats[j] = stat_table(totals[j], inv8)
    vhat = centre(zb[...].astype(F32), table[q], member)
    vh[...] = f2(vhat).astype(BF)
    vh.send()
    act = f2(silu(affine(vhat, prm[2, q])) * f3(half_mask(info)) * keep_of(info, q))
    first, last = edge_cols()
    for t in range(3):
        shifted = rows_down(act) if t == 0 else (act if t == 1 else rows_up(act))
        for u in range(3):
            x = cols_right(shifted, first) if u == 0 else (shifted if u == 1 else cols_left(shifted, last))
            at = (3 * t + u) * LB
            im[:, at : at + LB] = x.astype(BF)
    im.send()
    products(im[...], sb, q, LB, own, ((1, s1), (2, s2), (3, s3)))


def k_expand_b(info, st, b0, b1, b2, b3, prm, inv_count, eb, z6, st6, act, vh, table, stats):
    act_all(info, st, (b0, b1, b2, b3), prm, 3, inv_count[4:8], act, vh, table, stats)
    z = dot_nn(act[...], matrix(eb))
    z6[...] = z
    spread(st6, two_sums(z, member_of(info)))


def k_output(info, st6, z6, low_a, cot, prm, inv_count, gb, vh6, st, output, gbs, tab6, stat6):
    member = member_of(info)
    tab6[...], stat6[...] = stat_table(sums_dp(st6), inv_count[4:8])
    vhat = centre(z6[...], tab6[...], member)
    vh6[...] = f2(vhat).astype(BF)
    pre = affine(vhat, prm[2]) + f3(low_a[...].astype(F32))
    m = wide(f3(half_mask(info)), pre.shape[-1])
    sig = jax.nn.sigmoid(pre)
    output[:, 0:PX, :] = pre * sig * m
    output[:, PX:, :] = jnp.zeros((FR, 64 - PX, pre.shape[-1]), F32)
    output.send()
    g = cot[...].astype(F32)[:, 0:PX, :] * m * (sig * (1.0 + pre * (1.0 - sig)))
    gb[...] = f2(g)
    gbs[...] = f2(g).astype(BF)
    gbs.send()
    along = by_subnet(jnp.sum(g * vhat, axis=1), member)
    offset = by_subnet(jnp.sum(g, axis=1), member)
    spread(st, jnp.concatenate([along, offset], axis=0))


def k_back_six(info, st, gb, vh6, tab6, prm, inv_count, eb, act5, own, s1, s2, s3, pg, grad):
    q = info[0]
    member = member_of(info)
    totals = sums_dp(st)
    pg[...] = param_grads(totals)
    vhat = f3(vh6[...].astype(F32))
    m = wide(f3(half_mask(info)), vhat.shape[-1])
    g = m * norm_back(f3(gb[...]), vhat, tab6[...], totals, inv_count[4:8], member, prm[2, 0:1])
    low = f2(g).astype(BF)
    products(low, eb, q, LB, own, ((1, s1), (2, s2), (3, s3)))
    grad[...] = by_x_first(dot_tn(act5[...], low), st.shape[0]).astype(BF)


def back_stat(g, vhat, member, gl, st):
    low = f2(g).astype(BF)
    gl[...] = low
    g = f3(low.astype(F32))
    along = by_subnet(jnp.sum(g * vhat, axis=1), member)
    offset = by_subnet(jnp.sum(g, axis=1), member)
    spread(st, jnp.concatenate([along, offset], axis=0))


def k_back_stat(norm):
    def body(info, own, r1, r2, r3, vh, prm, gl, st):
        q = info[0]
        part = own[...] + r1[...].astype(F32) + r2[...].astype(F32) + r3[...].astype(F32)
        vhat = f3(vh[...].astype(F32))
        g = f3(part * half_mask(info)) * keep_of(info, q) * slope(affine(vhat, prm[norm, q]))
        back_stat(g, vhat, member_of(info), gl, st)

    return body


def gz_all(info, st, grads, values, table, prm, norm, inv8, gz, pg, hold):
    q = info[0]
    member = member_of(info)
    totals = sums_all(st)
    for j in range(NB):
        pg[j] = param_grads(totals[j])
        hold[j] = totals[j]
    m = f3(half_mask(info))
    for k in range(NB):
        j = q ^ k
        vhat = f3(values(k, j).astype(F32))
        g = norm_back(f3(grads[k][...].astype(F32)), vhat, table[j], hold[j], inv8, member, prm[norm, j][0:1])
        gz[:, lanes_of(j, LB)] = f2(m * g).astype(BF)


def k_back_five(info, st, g0, g1, g2, g3, vh5, tab5, prm, inv_count, sb, vh4, im4, gl, st4, pg, grad, gz5, hold):
    q = info[0]
    gz_all(
        info, st, (g0, g1, g2, g3), lambda k, j: vh5[:, lanes_of(j, LB)], tab5, prm, 3, inv_count[4:8],
        gz5, pg, hold,
    )
    terms = dot_nn(gz5[...], sb[...])
    first, last = edge_cols()
    total = None
    for t in range(3):
        for u in range(3):
            at = (3 * t + u) * LB
            x = terms[:, at : at + LB]
            x = cols_left(x, last) if u == 0 else (x if u == 1 else cols_right(x, first))
            x = rows_up(x) if t == 0 else (x if t == 1 else rows_down(x))
            total = x if total is None else total + x
    vhat = f3(vh4[...].astype(F32))
    g = f3(total * half_mask(info)) * keep_of(info, q) * slope(affine(vhat, prm[2, q]))
    back_stat(g, vhat, member_of(info), gl, st4)
    grad[...] = by_x_first(dot_tn(gz5[...], im4[...]), st.shape[0] // NB).astype(BF)


def k_back_four(info, st, g0, g1, g2, g3, v0, v1, v2, v3, tab4, prm, inv_count, rbt, gb, sl, vh3, vhp, low_a, ga, st3, pg, grad, gz4, hold):
    member = member_of(info)
    values = (v0, v1, v2, v3)
    gz_all(
        info, st, (g0, g1, g2, g3), lambda k, j: values[k][...], tab4, prm, 2, inv_count[4:8], gz4, pg, hold
    )
    low = gz4[...]
    back = dot_nn(low, matrix(rbt))
    g = (gb[...].astype(F32) + back) * sl[...].astype(F32)
    ga[...] = g
    g = f3(g)
    along = by_subnet(jnp.sum(g * f3(vh3[...].astype(F32)), axis=1), member)
    other = by_subnet(jnp.sum(g * f3(vhp[...].astype(F32)), axis=1), member)
    offset = by_subnet(jnp.sum(g, axis=1), member)
    half = offset.shape[-1] // 2
    tail = jnp.concatenate([offset[:, :half], offset[:, half:]], axis=0)
    spread(st3, jnp.concatenate([jnp.concatenate([along, other], axis=0), tail], axis=1))
    grad[...] = dot_tn(low, low_a[...]).astype(BF)


def add_hop(kept, away, sums):
    for k in range(4):
        total = kept[k].astype(F32) + away[k].astype(F32)
        sums[k][...] = total if k == 0 else total.astype(BF)
        sums[k].send()


def line_sum(parts):
    total = parts[0][...]
    for part in parts[1:]:
        total = total + part[...].astype(F32)
    return total


def taps_apart(ref, value):
    for tap in range(9):
        ref[tap] = value[:, tap * LB : (tap + 1) * LB]
    ref.send()


def emit_line(info, full, outs, first, part=0, parts=1):
    kept, away = outs
    rows = kept.shape[1]
    here = info[25] & 1
    lanes = full.shape[1]
    for z in range(4):
        for ref, x in ((kept, here), (away, here ^ 1)):
            at = ((2 * z + x) * parts + part) * rows
            ref[z, :, first : first + lanes] = full[pl.ds(pl.multiple_of(at, rows), rows), :].astype(BF)


def k_back_join(info, st, ga, vh3, vhp, tab3, tabp, prm, inv_count, ea, act2, every, grad_r, *refs):
    q = info[0]
    member = member_of(info)
    own, s1, s2, s3, gzp, pg3, pgp, *grads, full_a, full_s = refs
    totals = sums_dp(st)
    lanes = ga.shape[-1]
    tail = totals[:, lanes:]
    offset = jnp.concatenate([tail[0:4], tail[4:8]], axis=1)
    tot3 = jnp.concatenate([totals[0:4, :lanes], offset], axis=0)
    totp = jnp.concatenate([totals[4:8, :lanes], offset], axis=0)
    pg3[...] = param_grads(tot3)
    pgp[...] = param_grads(totp)
    inv8 = inv_count[4:8]
    g = f3(ga[...])
    m = wide(f3(half_mask(info)), lanes)
    low = f2(m * norm_back(g, f3(vh3[...].astype(F32)), tab3[...], tot3, inv8, member, prm[0, 0:1])).astype(BF)
    products(low, ea, q, LB, own, ((1, s1), (2, s2), (3, s3)))
    lowp = f2(m * norm_back(g, f3(vhp[...].astype(F32)), tabp[...], totp, inv8, member, prm[1, 0:1])).astype(BF)
    gzp[...] = lowp
    full_a[...] = dot_tn(act2[...], low)
    full_s[...] = dot_tn(every[...], lowp)
    if len(grads) == 2:
        emit_line(info, grad_r, grads, 0)
        emit_line(info, full_a, grads, lanes)
        for part in range(2):
            emit_line(info, full_s, grads, (2 + part) * lanes, part, 2)
        return
    grad = grads[0]
    count = st.shape[0]
    rows = full_s.shape[0] // count // 2
    grad[:, 0:lanes] = grad_r[...]
    grad[:, lanes : 2 * lanes] = full_a[...].astype(BF)
    for part in range(2):
        picked = [full_s[(2 * d + part) * rows : (2 * d + part + 1) * rows, :] for d in range(count)]
        at = (2 + part) * lanes
        grad[:, at : at + lanes] = jnp.concatenate(picked, axis=0).astype(BF)


def k_back_small(info, gzp, sc, own, s1, s2, s3):
    q = info[0]
    low = gzp[...]
    products(low, sc, q, 256, own, ((1, s1), (2, s2), (3, s3)))


def k_back_two(info, st, g0, g1, g2, g3, vh2, tab2, prm, inv_count, sa, vh1, im1, *refs):
    q = info[0]
    member = member_of(info)
    refs, (gz2, hold, full) = refs[:-3], refs[-3:]
    if len(refs) > 5:
        rows = refs[0].shape[1]
        for z in range(4):
            refs[6][z * rows : (z + 1) * rows, :] = (refs[0][z].astype(F32) + refs[1][z].astype(F32)).astype(BF)
        refs[6].send()
        (gl, st1, pg, saved), grads = refs[2:6], refs[7:]
    else:
        (gl, st1, pg, saved), grads = refs[0:4], refs[4:]
    gz_all(
        info, st, (g0, g1, g2, g3), lambda k, j: vh2[:, lanes_of(j, LB)], tab2, prm, 1, inv_count[4:8],
        gz2, pg, hold,
    )
    terms = dot_nn(gz2[...], sa[...])
    _, last = edge_cols()
    y = [terms[:, tap * LB : (tap + 1) * LB] for tap in range(9)]
    planes = [
        y[4],
        cols_left(y[3], last) + y[5],
        rows_up(y[1]) + y[7],
        rows_up(cols_left(y[0], last) + y[2]) + cols_left(y[6], last) + y[8],
    ]
    kept = keep_of(info, q)
    along = None
    offset = None
    for p in range(4):
        vhat = f3(vh1[p].astype(F32))
        g = f3(planes[p] * plane_mask(info, p)) * kept * slope(affine(vhat, prm[0, q]))
        low = f2(g).astype(BF)
        gl[p] = low
        saved[p] = low
        g = f3(low.astype(F32))
        a, b = jnp.sum(g * vhat, axis=1), jnp.sum(g, axis=1)
        along = a if along is None else along + a
        offset = b if offset is None else offset + b
    saved.send()
    spread(st1, jnp.concatenate([by_subnet(along, member), by_subnet(offset, member)], axis=0))
    full[...] = dot_tn(gz2[...], im1[...])
    emit(info, full, grads)


def k_last(info, st, g0, g1, g2, g3, v0, v1, v2, v3, tab1, prm, inv_count, xm, *refs):
    q = info[0]
    member = member_of(info)
    refs, hold = refs[:-1], refs[-1]
    if len(refs) > 3:
        add_hop(refs[0], refs[1], refs[5:9])
        refs = refs[2:5]
    gz1, pg, grad = refs
    totals = sums_all(st)
    inv16 = inv_count[0:4]
    for j in range(NB):
        pg[j] = param_grads(totals[j])
        hold[j] = totals[j]
    total = None
    for p in range(4):
        m = f3(plane_mask(info, p))
        for k, (gref, vref) in enumerate(((g0, v0), (g1, v1), (g2, v2), (g3, v3))):
            j = q ^ k
            vhat = f3(vref[p].astype(F32))
            g = norm_back(f3(gref[p].astype(F32)), vhat, tab1[j], hold[j], inv16, member, prm[0, j][0:1])
            gz1[p, :, lanes_of(j, LB)] = f2(m * g).astype(BF)
        term = dot_tn(gz1[p], xm[p])
        total = term if total is None else total + term
    grad[...] = total.astype(BF)


def k_features(info, gz1, rat, own, r1, r2, r3, gf, nat):
    for p in range(4):
        back = dot_nn(gz1[p], rat[...])
        if p == 0:
            back = back + own[...] + r1[...].astype(F32) + r2[...].astype(F32) + r3[...].astype(F32)
        back = back * wide(plane_mask(info, p), back.shape[-1])
        high = back.astype(BF)
        nat[0, p] = high.astype(F32)
        nat[1, p] = back - high.astype(F32)
    row, col, target = natural_index(1)
    select = jnp.where(target == row * 16 + col, 1.0, 0.0).astype(BF)
    for frame in range(FR):
        out = None
        for part in range(2):
            x = jnp.concatenate(
                [nat[part, p, frame * PX : (frame + 1) * PX, :] for p in range(4)], axis=0
            ).astype(BF)
            y = dot_nn(select, x)
            out = y if out is None else out + y
        gf[frame] = out


def k_tables(info, *refs):
    mids, pairs, outs, gains = refs[0:4], refs[4:8], refs[8:11], refs[11:14]
    stats_mid, grads_mid, stats_out, grads_out = refs[14:]
    for i in range(4):
        for j in range(NB):
            at = slice(j * LB, (j + 1) * LB)
            stats_mid[i, 0, :, at] = mids[i][j, 0:4]
            stats_mid[i, 1, :, at] = mids[i][j, 4:8]
            grads_mid[i, :, at] = pairs[i][j]
    for i in range(3):
        stats_out[i, 0] = outs[i][0:4]
        stats_out[i, 1] = outs[i][4:8]
        grads_out[i] = gains[i][...]


def k_end_grads(info, early, grad, spatial, expand, reduce, other, shortcut):
    value = early[...].astype(F32)
    taps_apart(spatial, value)
    expand[...] = value[:, TAPS:]
    value = grad[...].astype(F32)
    lanes = expand.shape[-1]
    reduce[...] = value[:, :lanes]
    other[...] = value[:, lanes : 2 * lanes]
    shortcut[...] = jnp.concatenate([value[:, 2 * lanes : 3 * lanes], value[:, 3 * lanes :]], axis=0)


def k_hop(info, kept, away, *sums):
    add_hop(kept, away, sums)


def k_final(info, *refs):
    parts, others, spatial, reduce = refs[:-3], refs[-3], refs[-2], refs[-1]
    taps_apart(spatial, line_sum(parts))
    total = others[0].astype(F32)
    for d in range(1, others.shape[0]):
        total = total + others[d].astype(F32)
    reduce[...] = total


def swap(value, k):
    return lax.ppermute(value, "chan", [(i, i ^ k) for i in range(NB)])


def partners(value):
    return [value] + [swap(value, k) for k in (1, 2, 3)]


def partners_two_hops(value):
    far = swap(value, 2)
    return [value, swap(value, 1), far, swap(far, 1)]


def everywhere(value):
    return lax.all_to_all(value, ("dp", "chan"), 0, 0, tiled=True)


def along_dp(value):
    return lax.all_to_all(value, "dp", 0, 0, tiled=True)


def after(value, *others):
    return lax.optimization_barrier((value,) + others)[0]


def swap_dp(value, k):
    return lax.ppermute(value, "dp", [(i, i ^ k) for i in range(lax.axis_size("dp"))])


def along_z(value):
    return [value] + [swap_dp(value, 2 * k) for k in (1, 2, 3)]


def across_x(line, *others):
    return line + [swap_dp(after(v, *others), 1) for v in line]


def add_near(kept, away):
    return [(kept[k].astype(F32) + away[k].astype(F32)).astype(F32 if k == 0 else BF) for k in range(4)]


def add_far(parts):
    return parts[0] + parts[1].astype(F32) + parts[2].astype(F32) + parts[3].astype(F32)


def reduce_pairs(value):
    if lax.axis_size("dp") != 8:
        return lax.psum_scatter(value, "dp", scatter_dimension=0, tiled=True)
    groups = [[2 * z, 2 * z + 1] for z in range(4)]
    return lax.psum_scatter(value, "dp", scatter_dimension=0, tiled=True, axis_index_groups=groups)


def reduce_lines(value):
    if lax.axis_size("dp") != 8:
        return value
    groups = [[2 * z + x for z in range(4)] for x in range(2)]
    return lax.psum_scatter(value, "dp", scatter_dimension=0, tiled=True, axis_index_groups=groups)


def shards(
    features,
    cotangent,
    reduce_a,
    spatial_a,
    expand_a,
    shortcut,
    reduce_b,
    spatial_b,
    expand_b,
    norms_mid,
    norms_out,
    crop_side,
    subnet_of,
    width_of,
):
    ndp = lax.axis_size("dp")
    nall = ndp * NB
    hops = ndp == 8
    hidden = norms_mid.shape[-1]
    cin = features.shape[-1]
    cout = cotangent.shape[-1]
    rows = reduce_a.shape[1]
    er = expand_a.shape[0]
    sr = shortcut.shape[0]
    position = lax.axis_index("chan").astype(jnp.int32)
    place = lax.axis_index("dp").astype(jnp.int32)
    width = jnp.sum(
        jnp.where(subnet_of[:, None] == jnp.arange(4, dtype=jnp.int32)[None, :], width_of[None, :], 0), axis=1
    )
    info = jnp.concatenate([position[None], crop_side, subnet_of, width, place[None]])

    ra_t = reduce_a.T
    sa_t = jnp.transpose(spatial_a, (2, 0, 1)).reshape(rows, TAPS)
    half = (crop_side + 1) // 2
    per16 = jnp.where(crop_side > 8, crop_side * crop_side, 4 * crop_side * crop_side)
    per8 = jnp.where(half > 4, half * half, 4 * half * half)
    lane = jnp.arange(LB, dtype=jnp.int32)[None, :]
    pixels = jnp.where(lane == subnet_of[:, None], per16[:, None], 0)
    pixels = pixels + jnp.where(lane == subnet_of[:, None] + 4, per8[:, None], 0)
    pixels = jnp.concatenate([pixels.astype(F32), jnp.zeros((rows, LB), F32)], axis=0)[: max(rows, FR)]
    prm = Pinned(jnp.transpose(norms_mid.reshape(4, 2, NB, LB), (0, 2, 1, 3)))
    prm_out = Pinned(norms_out)
    table = ((NB, 8, LB), F32, "hbm")
    one_block = ((NP, LB), F32)
    send = ((NP, LB), BF)
    sends = [one_block, send, send, send]
    stat_all = ((nall, 8, LB), F32)
    stat_own = ((ndp, 8, cout), F32)
    stat_wide = ((ndp, 8, cout + cout // 2), F32)
    map_out = ((NP, cout), F32)
    low_out = ((NP, cout), BF, "hbm")
    low_mid = ((NP, hidden), BF, "hbm")
    tab_out = ((8, cout), F32, "hbm")

    xm, xs, small = call(
        k_prep, [((4, NP, cin), BF), ((4, NP, cin), BF, "hbm"), ((NP, cin), BF)],
        info, Pinned(features.reshape(FR, 256, cin)), name="prep",
    )
    pack_mid = jnp.concatenate([expand_a, shortcut, after(reduce_b, small).T], axis=0)
    pack_end = jnp.concatenate(
        [jnp.transpose(after(spatial_b, small), (2, 0, 1)).reshape(rows, TAPS), expand_b], axis=1
    )
    if hops:
        line_ra = along_z(jnp.concatenate([ra_t, pixels.astype(BF)], axis=1))
        line_sa = along_z(sa_t)
        pieces = across_x(line_ra, pack_mid, pack_end, *line_ra[1:], *line_sa[1:])
        rat = Gathered(pieces, rows, 0, cin)
        counts = Gathered(pieces, 16, cin, LB)
    else:
        rat = Pinned(lax.all_gather(ra_t, "dp", axis=0, tiled=True))
        sa = Pinned(lax.all_gather(sa_t, "dp", axis=0, tiled=True))
        counts = Pinned(lax.psum(pixels, "dp"))
    own, near, far, *stacked = call(
        k_first,
        [((4, NP, LB), F32), ((2, 4, NP, LB), BF), ((4, NP, LB), F32)]
        + ([((4, rows, TAPS), BF, "hbm")] if hops else []),
        info, xm, rat, *([Pinned(x) for x in line_sa] if hops else []), name="first",
    )
    if hops:
        sa_pieces = [stacked[0], swap_dp(stacked[0], 1)]
        sa = Gathered(sa_pieces, rows, 0, TAPS)
    near = swap(near, 1)
    far = (far + near[1].astype(F32)).astype(BF)
    mid = lax.all_gather(after(pack_mid, far), "dp", axis=0)

    def mid_rows(first, size):
        if size % 16 == 0:
            return Pinned(mid, lambda ref, info: ref.at[:, first : first + size, :], (ndp, size, cout))
        return Pinned(mid[:, first : first + size].reshape(ndp * size, cout))

    ea = mid_rows(0, er)
    sc = mid_rows(er, sr)
    rbt = mid_rows(er + sr, rows)
    end = lax.all_gather(pack_end, "dp", axis=0, tiled=True)
    sb = Pinned(end, lambda ref, info: ref.at[:, 0:TAPS], (hidden, TAPS))
    eb = Pinned(end, lambda ref, info: ref.at[:, TAPS : TAPS + cout], (hidden, cout))

    far = swap(far, 2)
    zb1, st = call(
        k_stat_first, [((4, NP, LB), BF), stat_all], info, own, near, far, name="stat_one"
    )
    smalls = partners_two_hops(after(small, st))
    st = after(everywhere(after(st, *(sa_pieces[1:] if hops else ()))), *smalls[1:])
    own, s1, s2, s3, im1, vh1, tab1, inv_count, stat1 = call(
        k_down,
        sends + [((NP, TAPS), BF, "hbm"), ((4, NP, LB), BF, "hbm"), table, ((8, LB), F32, "hbm"), table],
        info, st, zb1, prm, sa, counts, name="down",
    )
    inv_count = Pinned(inv_count)
    zb, st = call(k_stat, [send, stat_all], info, own, swap(s1, 1), swap(s2, 2), swap(s3, 3), name="stat_two")
    zs = partners(zb)
    smalls = lax.optimization_barrier(tuple(smalls) + (st,))[:4]
    stp, every, zp = call(
        k_proj, [((8, cout), F32), ((NP, NB * cin), BF, "hbm"), low_out], info, *smalls, sc, name="proj"
    )
    st = after(everywhere(st), stp)
    stx = swap_dp(stp, 1)
    z3, st3, act2, vh2, tab2, stat2 = call(
        k_expand_a, [map_out, stat_wide, low_mid, low_mid, table, table],
        info, st, *zs, stp, stx, prm, inv_count, ea, scratch=[pltpu.VMEM((8, cout), F32)], name="expand_a",
    )
    st3 = along_dp(st3)
    own, s1, s2, s3, low_a, sl, vh3, vhp, tab3, tabp, stat3, statp = call(
        k_join, sends + [low_out, low_out, low_out, low_out, tab_out, tab_out, tab_out, tab_out],
        info, st3, z3, Pinned(zp), prm_out, inv_count, rbt, name="join",
    )
    zb, st = call(k_stat, [send, stat_all], info, own, swap(s1, 1), swap(s2, 2), swap(s3, 3), name="stat_four")
    st = everywhere(st)
    own, s1, s2, s3, im4, vh4, tab4, stat4 = call(
        k_flat, sends + [((NP, TAPS), BF, "hbm"), ((NP, LB), BF, "hbm"), table, table],
        info, st, zb, prm, inv_count, sb, name="flat",
    )
    zb, st = call(k_stat, [send, stat_all], info, own, swap(s1, 1), swap(s2, 2), swap(s3, 3), name="stat_five")
    zs = partners(zb)
    st = everywhere(st)
    z6, st6, act5, vh5, tab5, stat5 = call(
        k_expand_b, [map_out, stat_own, low_mid, low_mid, table, table],
        info, st, *zs, prm, inv_count, eb, name="expand_b",
    )
    vhs4 = partners(after(vh4, st6))
    st6 = after(along_dp(st6), *vhs4[1:])
    gb, vh6, st, output, gbs, tab6, stat6 = call(
        k_output,
        [map_out, ((NP, cout), BF), stat_own, ((FR, 64, cout), F32, "hbm"), low_out, tab_out, tab_out],
        info, st6, z6, Pinned(low_a), Pinned(cotangent.reshape(FR, 64, cout)), prm_out, inv_count, name="output",
    )

    def early(first, size):
        return ((hidden, TAPS + cout), BF, "hbm", lambda ref: ref.at[:, first : first + size], (hidden, size))

    def summed(size, lanes):
        return [((size, lanes), F32, "hbm")] + [((size, lanes), BF, "hbm")] * 3

    def z_parts(sums):
        return [sums[0]] + [swap_dp(sums[k], 2 * k) for k in (1, 2, 3)]

    def reduced(size, width_):
        if hops:
            return [((4, size, width_), BF, "hbm")] * 2
        return [((ndp * size, width_), BF, "hbm")]

    def own_lanes(array):
        return Pinned(array, lambda ref, info: ref.at[:, lanes_of(info[0], LB)], (NP, LB))

    vh1_in = after(vh1, st)
    vhs1 = [vh1, swap(vh1_in, 1), swap(vh1_in, 2)]
    st = after(along_dp(st), *vhs1[1:])
    own, s1, s2, s3, pg6, grad_early = call(
        k_back_six, sends + [((2, cout), F32, "hbm"), early(TAPS, cout)],
        info, st, gb, vh6, Pinned(tab6), prm_out, inv_count, eb, Pinned(act5), name="back_six",
    )
    gl, st = call(
        k_back_stat(3), [send, stat_all],
        info, own, swap(s1, 1), swap(s2, 2), swap(s3, 3), own_lanes(vh5), prm, name="back_stat_five",
    )
    gs = partners(gl)
    st = everywhere(st)
    hold = pltpu.VMEM((NB, 8, LB), F32)
    pair_mid = ((NB, 2, LB), F32, "hbm")
    gl, st, pg5, grad_early = call(
        k_back_five, [send, stat_all, pair_mid, early(0, TAPS)],
        info, st, *gs, Pinned(vh5), Pinned(tab5), prm, inv_count, sb, Pinned(vh4), Pinned(im4),
        scratch=[pltpu.VMEM((NP, hidden), BF), hold], alias=(grad_early, 3), name="back_five",
    )
    gs = partners(gl)
    grad_early = reduce_pairs(grad_early)
    st = everywhere(st)
    ga, st, pg4, grad_r = call(
        k_back_four, [map_out, stat_wide, pair_mid, ((hidden, cout), BF, "hbm")],
        info, st, *gs, *[Pinned(v) for v in vhs4], Pinned(tab4), prm, inv_count, rbt, Pinned(gbs), Pinned(sl),
        Pinned(vh3), Pinned(vhp), Pinned(low_a),
        scratch=[pltpu.VMEM((NP, hidden), BF), hold], name="back_four",
    )
    vhs1.append(swap(after(vhs1[2], st), 1))
    st = after(along_dp(st), vhs1[3], grad_early)
    if hops:
        grads = [((4, rows, 4 * cout), BF, "hbm")] * 2
    else:
        grads = [((hidden, 4 * cout), BF, "hbm")]
    own, s1, s2, s3, gzp, pg3, pgp, *grads = call(
        k_back_join, sends + [((NP, cout), BF)] + [((2, cout), F32, "hbm")] * 2 + grads,
        info, st, ga, Pinned(vh3), Pinned(vhp), Pinned(tab3), Pinned(tabp), prm_out, inv_count, ea,
        Pinned(act2), Pinned(every), Pinned(grad_r),
        scratch=[pltpu.VMEM((hidden, cout), F32), pltpu.VMEM((ndp * sr, cout), F32)], name="back_join",
    )
    grad_early = reduce_lines(after(grad_early, grads[0]))
    extra_in, extra_out = [], []
    if hops:
        extra_in = [Pinned(grads[0]), swap_dp(grads[1], 1)]
        extra_out = [((4 * rows, 4 * cout), BF, "hbm")]
    else:
        end_grad = reduce_pairs(grads[0])
    r1, r2, r3 = swap(s1, 1), swap(s2, 2), swap(s3, 3)
    sown, *small_sends = call(
        k_back_small, [((NP, cin), F32)] + [((NP, cin), BF)] * 3,
        info, after(gzp, r1), sc, name="back_small",
    )
    own = after(own, sown)
    gl, st = call(
        k_back_stat(1), [send, stat_all],
        info, own, r1, r2, r3, own_lanes(vh2), prm, name="back_stat_two",
    )
    gs = partners(gl)
    st = everywhere(st)
    small_one = swap(small_sends[0], 1)
    st = after(st, grad_early, small_one)
    gl, st, pg2, saved, *grad_sa = call(
        k_back_two, [((4, NP, LB), BF), stat_all, pair_mid, ((4, NP, LB), BF, "hbm")] + extra_out + reduced(rows, TAPS),
        info, st, *gs, Pinned(vh2), Pinned(tab2), prm, inv_count, sa, Pinned(vh1), Pinned(im1), *extra_in,
        scratch=[pltpu.VMEM((NP, hidden), BF), hold, pltpu.VMEM((hidden, TAPS), F32)], name="back_two",
    )
    gs = [gl, swap(gl, 1), swap(gl, 2)]
    st = everywhere(st)
    gs.append(swap(after(gs[2], st), 1))
    small_back = [small_one] + [swap(after(small_sends[k - 1], gs[3]), k) for k in (2, 3)]
    extra_in, extra_out = [], []
    if hops:
        end_grad = reduce_lines(grad_sa[0])
        extra_in = [Pinned(grad_sa[2]), swap_dp(after(grad_sa[1], gs[1]), 1)]
        extra_out = summed(rows, TAPS)
    gz1, pg1, grad_rat, *sums_sa = call(
        k_last, [((4, NP, hidden), BF), pair_mid, ((hidden, cin), BF, "hbm")] + extra_out,
        info, st, Pinned(saved), Pinned(gs[1]), Pinned(gs[2]), gs[3], *[Pinned(v) for v in vhs1], Pinned(tab1), prm, inv_count, Pinned(xs), *extra_in,
        scratch=[hold], name="last",
    )
    if hops:
        parts_sa = z_parts(sums_sa)
    else:
        parts_sa = [lax.psum_scatter(grad_sa[0], "dp", scatter_dimension=0, tiled=True).astype(F32)]
    spatial, expand, reduce, grad_a, grad_s = call(
        k_end_grads,
        [
            ((9, rows, LB), F32, "hbm"), ((er, cout), F32, "hbm"), ((rows, cout), F32, "hbm"),
            ((er, cout), F32, "hbm"), ((sr, cout), F32, "hbm"),
        ],
        info, Pinned(grad_early), Pinned(end_grad), name="end_grads",
    )
    stats_mid, grad_norms_mid, stats_out, grad_norms_out = call(
        k_tables,
        [
            ((4, 2, 4, hidden), F32, "hbm"), ((4, 2, hidden), F32, "hbm"),
            ((3, 2, 4, cout), F32, "hbm"), ((3, 2, cout), F32, "hbm"),
        ],
        info,
        *[Pinned(x) for x in (stat1, stat2, stat4, stat5, pg1, pg2, pg4, pg5, stat3, statp, stat6, pg3, pgp, pg6)],
        name="tables",
    )
    parts_ra = along_dp(grad_rat.reshape(ndp, rows, cin))
    gf = call(
        k_features, [((FR, 256, cin), F32, "hbm")],
        info, gz1, rat, Pinned(sown), *small_back,
        scratch=[pltpu.VMEM((2, 4, NP, cin), F32)], name="features",
    )[0]
    spatial_sa, grad_rat = call(
        k_final, [((9, rows, LB), F32, "hbm"), ((rows, cin), F32, "hbm")],
        info, *[Pinned(after(x, gf)) for x in parts_sa], after(parts_ra, gf), name="final",
    )
    grad_reduce_a = grad_rat.T
    grad_spatial_a = jnp.transpose(spatial_sa, (0, 2, 1))
    grad_spatial_b = jnp.transpose(spatial, (0, 2, 1))
    grad_expand_b = expand
    grad_reduce_b = reduce.T
    return (
        output.reshape(FR, 8, 8, cout),
        gf.reshape(FR, 16, 16, cin),
        grad_reduce_a,
        grad_spatial_a,
        grad_a,
        grad_s,
        grad_reduce_b,
        grad_spatial_b,
        grad_expand_b,
        grad_norms_mid,
        grad_norms_out,
        stats_mid,
        stats_out,
    )


def solution(mesh):
    in_specs = (
        P("dp", None, None, "chan"),
        P("dp", None, None, "chan"),
        P("chan", "dp"),
        P(None, "chan", "dp"),
        P("dp", "chan"),
        P("dp", "chan"),
        P("chan", "dp"),
        P(None, "chan", "dp"),
        P("dp", "chan"),
        P(),
        P(None, None, "chan"),
        P("dp"),
        P("dp"),
        P(),
    )
    out_specs = (
        P("dp", None, None, "chan"),
        P("dp", None, None, "chan"),
        P("chan", "dp"),
        P(None, "chan", "dp"),
        P("dp", "chan"),
        P("dp", "chan"),
        P("chan", "dp"),
        P(None, "chan", "dp"),
        P("dp", "chan"),
        P(),
        P(None, None, "chan"),
        P(),
        P(None, None, None, "chan"),
    )
    return jax.shard_map(shards, mesh=mesh, in_specs=in_specs, out_specs=out_specs, check_vma=False)
```

```python
import jax
import jax.numpy as jnp
from jax import lax
from jax.experimental import pallas as pl
from jax.experimental.pallas import tpu as pltpu
from jax.sharding import PartitionSpec as P

EPSILON = 1e-05
BF = jnp.bfloat16
F32 = jnp.float32
FR = 8
RP = 7
QP = 8
PX = RP * QP
NP = FR * PX
LB = 128
NB = 4
TAPS = 9 * LB


class Pinned:
    def __init__(self, array, view=None, shape=None):
        self.array = array
        self.view = view
        self.shape = array.shape if shape is None else shape


class Gathered:
    def __init__(self, pieces, rows, first, lanes):
        self.pieces = pieces
        self.rows = rows
        self.window = (slice(0, rows), slice(first, first + lanes))
        self.shape = (8 * rows, lanes)


class Late:
    def __init__(self, ref, copies):
        self.ref = ref
        self.copies = copies
        self.waiting = True

    def ready(self):
        if self.waiting:
            for copy in self.copies:
                copy.wait()
            self.waiting = False
        return self.ref

    def __getitem__(self, index):
        return self.ready()[index]

    @property
    def shape(self):
        return self.ref.shape


class Saved:
    def __init__(self, ref, copy):
        self.ref = ref
        self.copy = copy
        self.sent = False

    def __setitem__(self, index, value):
        self.ref[index] = value

    def __getitem__(self, index):
        return self.ref[index]

    @property
    def shape(self):
        return self.ref.shape

    def send(self):
        self.sent = True
        self.copy.start()


PRM, INV, PRM_OUT, TAB, TAB_OUT, SLOTS = 0, 16, 17, 29, 45, 57


class Held:
    def __init__(self, kind, norm=0, ref=None):
        self.kind = kind
        self.norm = norm
        self.ref = ref

    def __getitem__(self, index):
        if self.kind == "prm":
            norm, j = index
            return self.ref[PRM + norm * NB + j][0:2]
        if self.kind == "inv":
            return self.ref[INV][index]
        if self.kind == "tab":
            return self.ref[TAB + self.norm * NB + index]
        if self.kind == "prm_out":
            norm = index[0] if isinstance(index, tuple) else index
            value = jnp.concatenate([self.ref[PRM_OUT + norm * NB + b][0:2] for b in range(NB)], axis=1)
            return value[index[1]] if isinstance(index, tuple) else value
        return jnp.concatenate([self.ref[TAB_OUT + self.norm * NB + b] for b in range(NB)], axis=1)

    def __setitem__(self, index, value):
        if self.kind == "inv":
            self.ref[(INV,) + index] = value
        elif self.kind == "tab":
            self.ref[TAB + self.norm * NB + index] = value
        else:
            for b in range(NB):
                self.ref[TAB_OUT + self.norm * NB + b] = value[:, b * LB : (b + 1) * LB]


def call(body, outs, info, *args, scratch=(), name, alias=None, state=None):
    flat = []
    buffers = []
    copies = 0
    listed, outs = outs, [o for o in outs if not isinstance(o, Held)]
    held = [] if state is None else [state]
    for a in args:
        if isinstance(a, Held):
            continue
        if isinstance(a, Gathered):
            flat += [(p, True) for p in a.pieces]
            buffers.append(pltpu.VMEM(a.shape, a.pieces[0].dtype))
            copies += 8
        elif isinstance(a, Pinned):
            flat.append((a.array, True))
            buffers.append(pltpu.VMEM(a.shape, a.array.dtype))
            copies += 1
        else:
            flat.append((a, False))
    saved = [len(o) > 2 for o in outs]
    for o, s in zip(outs, saved):
        if s:
            buffers.append(pltpu.VMEM(o[4] if len(o) > 3 else o[0], o[1]))
            copies += 1
    extra = [] if alias is None else [alias[0]]
    arrays = [pltpu.with_memory_space_constraint(a, pltpu.HBM) if p else a for a, p in flat]
    arrays += [pltpu.with_memory_space_constraint(a, pltpu.HBM) for a in extra]
    vmem = pl.BlockSpec(memory_space=pltpu.VMEM)
    hbm = pl.BlockSpec(memory_space=pltpu.HBM)

    def kernel(*refs):
        refs = list(refs)
        info_ref = refs.pop(0)
        ins = refs[: len(flat)]
        refs = refs[len(flat) + len(extra) :]
        if held:
            held_in = refs.pop(0)
        results, refs = refs[: len(outs)], refs[len(outs) :]
        if held:
            held_out = refs.pop(0)
            held_out[...] = held_in[...]
        bufs, refs = refs[: len(buffers)], refs[len(buffers) :]
        if copies:
            sems, refs = refs[0], refs[1:]
        used = 0
        given = []
        late = []
        for a in args:
            if isinstance(a, Held):
                given.append(Held(a.kind, a.norm, held_in))
                continue
            if not isinstance(a, (Gathered, Pinned)):
                given.append(ins.pop(0))
                continue
            buf = bufs.pop(0)
            moves = []
            if isinstance(a, Gathered):
                blocks = []
                for piece in a.pieces:
                    ref = ins.pop(0)
                    blocks += [ref] if len(piece.shape) == 2 else [ref.at[k] for k in range(4)]
                for i in range(8):
                    source = info_ref[25] ^ (2 * (i % 4)) ^ (i // 4)
                    rows = pl.ds(pl.multiple_of(source * a.rows, a.rows), a.rows)
                    moves.append(pltpu.make_async_copy(blocks[i].at[a.window], buf.at[rows], sems.at[used]))
                    used += 1
            else:
                ref = ins.pop(0)
                source = ref if a.view is None else a.view(ref, info_ref)
                moves.append(pltpu.make_async_copy(source, buf, sems.at[used]))
                used += 1
            for move in moves:
                move.start()
            late.append(Late(buf, moves))
            given.append(late[-1])
        produced = []
        outgoing = []
        slots = iter(zip(outs, saved, results))
        for listing in listed:
            if isinstance(listing, Held):
                produced.append(Held(listing.kind, listing.norm, held_out))
                continue
            o, s, ref = next(slots)
            if s:
                buf = bufs.pop(0)
                target = o[3](ref) if len(o) > 3 else ref
                ref = Saved(buf, pltpu.make_async_copy(buf, target, sems.at[used]))
                used += 1
                outgoing.append(ref)
            produced.append(ref)
        body(info_ref, *given, *produced, *refs)
        for one in outgoing:
            if not one.sent:
                one.send()
        for one in late:
            one.ready()
        for one in outgoing:
            one.copy.wait()

    return pl.pallas_call(
        kernel,
        out_shape=[(pltpu.HBM if s else jax.ShapeDtypeStruct)(o[0], o[1]) for o, s in zip(outs, saved)]
        + [jax.ShapeDtypeStruct(x.shape, x.dtype) for x in held],
        in_specs=[pl.BlockSpec(memory_space=pltpu.SMEM)]
        + [hbm if p else vmem for _, p in flat]
        + [hbm] * len(extra)
        + [vmem] * len(held),
        out_specs=[hbm if s else vmem for s in saved] + [vmem] * len(held),
        scratch_shapes=buffers + ([pltpu.SemaphoreType.DMA((copies,))] if copies else []) + list(scratch),
        input_output_aliases={} if alias is None else {1 + len(flat): alias[1]},
        compiler_params=pltpu.CompilerParams(vmem_limit_bytes=40 << 20),
        cost_estimate=pl.CostEstimate(flops=1, bytes_accessed=1, transcendentals=0),
        name=name,
    )(info, *arrays, *held)


def f3(value):
    return value.reshape(FR, PX, value.shape[-1])


def f2(value):
    return value.reshape(NP, value.shape[-1])


def wide(value, lanes):
    count = lanes // value.shape[-1]
    return value if count == 1 else jnp.concatenate([value] * count, axis=-1)


def dot_nn(left, right):
    return lax.dot_general(left, right, (((1,), (0,)), ((), ())), preferred_element_type=F32)


def dot_nt(left, right):
    return lax.dot_general(left, right, (((1,), (1,)), ((), ())), preferred_element_type=F32)


def dot_tn(left, right):
    return lax.dot_general(left, right, (((0,), (0,)), ((), ())), preferred_element_type=F32)


def frame_scalars(info, first):
    row = lax.broadcasted_iota(jnp.int32, (FR, LB), 0)
    out = jnp.zeros((FR, LB), jnp.int32)
    for frame in range(FR):
        out = jnp.where(row == frame, info[first + frame], out)
    return out


def member_of(info):
    subnet = frame_scalars(info, 9)
    return [(subnet == s).astype(F32) for s in range(4)]


def keep_of(info, j):
    lane = lax.broadcasted_iota(jnp.int32, (FR, LB), 1) + j * LB
    return (lane < frame_scalars(info, 17)).astype(F32)[:, None, :]


def crop_mask(info, half, row_scale, row_off, col_scale, col_off):
    at = lax.broadcasted_iota(jnp.int32, (PX, LB), 0)
    row = (at >> 3) * row_scale + row_off
    col = (at & 7) * col_scale + col_off
    parts = []
    for frame in range(FR):
        side = info[1 + frame]
        if half:
            side = (side + 1) >> 1
        full = 8 if half else 16
        period = jnp.where(side > full // 2, full, full // 2)
        inside = ((row & (period - 1)) < side) & ((col & (period - 1)) < side)
        parts.append(jnp.where(inside, 1.0, 0.0).astype(F32))
    return jnp.concatenate(parts, axis=0)


def plane_mask(info, plane):
    return crop_mask(info, 0, 2, plane // 2, 2, plane % 2)


def half_mask(info):
    return crop_mask(info, 1, 1, 0, 1, 0)


def by_subnet(frames, member):
    lanes = frames.shape[-1]
    return jnp.concatenate(
        [jnp.sum(frames * wide(member[s], lanes), axis=0, keepdims=True) for s in range(4)], axis=0
    )


def by_frame(table, member):
    lanes = table.shape[-1]
    total = None
    for s in range(4):
        term = wide(member[s], lanes) * table[s : s + 1, :]
        total = term if total is None else total + term
    return total[:, None, :]


def sum_px(value):
    return jnp.sum(f3(value), axis=1)


def stat_table(totals, inv_count):
    inv_n = wide(inv_count, totals.shape[-1])
    mean = totals[0:4] * inv_n
    var = totals[4:8] * inv_n - mean * mean
    return jnp.concatenate([mean, lax.rsqrt(var + EPSILON)], axis=0), jnp.concatenate([mean, var], axis=0)


def centre(value, table, member):
    return (f3(value) - by_frame(table[0:4], member)) * by_frame(table[4:8], member)


def affine(vhat, prm):
    return prm[0:1][None] * vhat + prm[1:2][None]


def silu(pre):
    return pre * jax.nn.sigmoid(pre)


def slope(pre):
    sig = jax.nn.sigmoid(pre)
    return sig * (1.0 + pre * (1.0 - sig))


def norm_back(grads, vhat, table, totals, inv_count, member, gain):
    inv_n = wide(inv_count, totals.shape[-1])
    along = by_frame(totals[0:4] * inv_n, member)
    offset = by_frame(totals[4:8] * inv_n, member)
    factor = by_frame(table[4:8], member) * gain[None]
    return factor * (grads - offset - vhat * along)


def param_grads(totals):
    return jnp.concatenate(
        [jnp.sum(totals[0:4], axis=0, keepdims=True), jnp.sum(totals[4:8], axis=0, keepdims=True)], axis=0
    )


def rows_down(value):
    cube = f3(value)
    return f2(jnp.concatenate([jnp.zeros((FR, QP, cube.shape[-1]), F32), cube[:, : PX - QP]], axis=1))


def rows_up(value):
    cube = f3(value)
    return f2(jnp.concatenate([cube[:, QP:], jnp.zeros((FR, QP, cube.shape[-1]), F32)], axis=1))


def cols_right(value, first):
    return jnp.where(first, 0.0, pltpu.roll(value, 1, 0))


def cols_left(value, last):
    return jnp.where(last, 0.0, pltpu.roll(value, NP - 1, 0))


def edge_cols():
    at = lax.broadcasted_iota(jnp.int32, (NP, LB), 0) & 7
    return at == 0, at == 7


def block(ref, index, size):
    if len(ref.shape) == 2:
        return ref[pl.ds(pl.multiple_of(index * size, size), size), :]
    step = size // ref.shape[1]
    return ref[pl.ds(index * step, step)].reshape(size, ref.shape[-1])


def matrix(ref):
    value = ref[...]
    return value if len(value.shape) == 2 else value.reshape(-1, value.shape[-1])


def lanes_of(index, size):
    return pl.ds(pl.multiple_of(index * size, size), size)


def sums_all(ref):
    count = ref.shape[0] // NB
    out = []
    for j in range(NB):
        total = ref[j]
        for d in range(1, count):
            total = total + ref[NB * d + j]
        out.append(total)
    return out


def sums_dp(ref):
    total = ref[0]
    for d in range(1, ref.shape[0]):
        total = total + ref[d]
    return total


def spread(ref, value):
    for d in range(ref.shape[0]):
        ref[d] = value


def pair_products(low, weight, q, size):
    both = dot_nt(low, block(weight, q >> 1, 2 * size))
    odd = (q & 1) == 1
    first, second = both[:, :size], both[:, size:]
    return jnp.where(odd, second, first), jnp.where(odd, first, second)


def products(low, weight, q, size, own, others):
    refs = dict(others)
    own[...], near = pair_products(low, weight, q, size)
    refs[1][...] = near.astype(BF)
    far, both = pair_products(low, weight, q ^ 2, size)
    refs[2][...] = far.astype(BF)
    refs[3][...] = both.astype(BF)


def by_x_first(value, count):
    if count != 8:
        return value
    rows = value.shape[0] // 8
    return jnp.concatenate(
        [value[(2 * z + x) * rows : (2 * z + x + 1) * rows] for x in range(2) for z in range(4)], axis=0
    )


def emit(info, full, outs, first=0):
    if len(outs) == 1:
        outs[0][...] = full[...].astype(BF)
        return
    away, kept = outs
    rows = full.shape[0] // 8
    here = info[25]
    to = slice(first, first + rows)
    for k in range(4):
        target = here ^ (2 * k)
        kept[k, to] = full[pl.ds(pl.multiple_of(target * rows, rows), rows), :].astype(BF)
        away[k, to] = full[pl.ds(pl.multiple_of((target ^ 1) * rows, rows), rows), :].astype(BF)


def natural_index(axis):
    shape = (4 * PX, 256) if axis == 0 else (256, 4 * PX)
    at = lax.broadcasted_iota(jnp.int32, shape, axis)
    plane = (
        (at >= PX).astype(jnp.int32) + (at >= 2 * PX).astype(jnp.int32) + (at >= 3 * PX).astype(jnp.int32)
    )
    inner = at - PX * plane
    row = (inner >> 3) * 2 + (plane >> 1)
    col = (inner & 7) * 2 + (plane & 1)
    return row, col, lax.broadcasted_iota(jnp.int32, shape, 1 - axis)


def k_prep(info, feat, xm, xs, small):
    row, col, source = natural_index(0)
    hit = source == row * 16 + col
    for pair in range(FR // 2):
        picked = []
        for frame in (2 * pair, 2 * pair + 1):
            side = info[1 + frame]
            period = jnp.where(side > 8, 16, 8)
            inside = ((row & (period - 1)) < side) & ((col & (period - 1)) < side)
            select = jnp.where(hit & inside, 1.0, 0.0).astype(BF)
            picked.append(dot_nn(select, feat[frame]))
        for p in range(4):
            both = jnp.concatenate([x[p * PX : (p + 1) * PX] for x in picked], axis=0)
            xm[p, pair * 2 * PX : (pair + 1) * 2 * PX, :] = both.astype(BF)
    xs[...] = xm[...]
    small[...] = xm[0]


def k_first(info, xm, rat, *refs):
    q = info[0]
    own, near, far = refs[-3:] if len(refs) == 3 else refs[4:7]
    if len(refs) > 3:
        for k in range(4):
            refs[7][k] = refs[k][...]
        refs[7].send()
    for p in range(4):
        x = xm[p]
        own[p], one = pair_products(x, rat, q, LB)
        near[0, p] = one.astype(BF)
        far[p], three = pair_products(x, rat, q ^ 2, LB)
        near[1, p] = three.astype(BF)


def k_stat_first(info, own, near, far, zb, st):
    member = member_of(info)
    sums = None
    squares = None
    for p in range(4):
        low = (own[p] + near[0, p].astype(F32) + far[p].astype(F32)).astype(BF)
        zb[p] = low
        z = low.astype(F32)
        a, b = sum_px(z), sum_px(z * z)
        sums = a if sums is None else sums + a
        squares = b if squares is None else squares + b
    spread(st, jnp.concatenate([by_subnet(sums, member), by_subnet(squares, member)], axis=0))


def k_down(info, st, zb, prm, sa, counts, own, s1, s2, s3, im, vh, table, inv_count, stats):
    q = info[0]
    member = member_of(info)
    totals = sums_all(st)
    pixels = jnp.sum(counts[...].astype(F32), axis=0, keepdims=True)
    lane = lax.broadcasted_iota(jnp.int32, (1, LB), 1)
    for s in range(8):
        here = jnp.sum(jnp.where(lane == s, pixels, 0.0), axis=1, keepdims=True)
        inv_count[s : s + 1, :] = jnp.broadcast_to(1.0 / here, (1, LB))
    inv16 = inv_count[0:4, :]
    for j in range(NB):
        table[j], stats[j] = stat_table(totals[j][0:8], inv16)
    stats.send()
    tab = table[q]
    kept = keep_of(info, q)
    par = prm[0, q]
    first, _ = edge_cols()
    planes = []
    for p in range(4):
        vhat = centre(zb[p].astype(F32), tab, member)
        vh[p] = f2(vhat).astype(BF)
        planes.append(f2(silu(affine(vhat, par)) * f3(plane_mask(info, p)) * kept))
    vh.send()
    for t in range(3):
        for u in range(3):
            x = planes[(0 if t == 1 else 2) + (0 if u == 1 else 1)]
            if t == 0:
                x = rows_down(x)
            if u == 0:
                x = cols_right(x, first)
            at = (3 * t + u) * LB
            im[:, at : at + LB] = x.astype(BF)
    im.send()
    products(im[...], sa, q, LB, own, ((1, s1), (2, s2), (3, s3)))


def k_stat(info, own, r1, r2, r3, zb, st):
    member = member_of(info)
    low = (own[...] + r1[...].astype(F32) + r2[...].astype(F32) + r3[...].astype(F32)).astype(BF)
    zb[...] = low
    z = low.astype(F32)
    zm = z * half_mask(info)
    total = jnp.concatenate([by_subnet(sum_px(zm), member), by_subnet(sum_px(zm * z), member)], axis=0)
    spread(st, total)


def act_all(info, st, blocks, prm, norm, inv8, act, vh, table, stats):
    q = info[0]
    member = member_of(info)
    totals = sums_all(st)
    for j in range(NB):
        table[j], stats[j] = stat_table(totals[j], inv8)
    stats.send()
    m = f3(half_mask(info))
    for k in range(NB):
        j = q ^ k
        vhat = centre(blocks[k][...].astype(F32), table[j], member)
        vh[:, lanes_of(j, LB)] = f2(vhat).astype(BF)
        a = silu(affine(vhat, prm[norm, j])) * m * keep_of(info, j)
        act[:, lanes_of(j, LB)] = f2(a).astype(BF)
    vh.send()
    act.send()


def two_sums(z, member):
    return jnp.concatenate([by_subnet(sum_px(z), member), by_subnet(sum_px(z * z), member)], axis=0)


def k_proj(info, x0, x1, x2, x3, sc, st, every, zp):
    q = info[0]
    for k, ref in enumerate((x0, x1, x2, x3)):
        every[:, lanes_of(q ^ k, 256)] = ref[...]
    every.send()
    z = dot_nn(every[...], matrix(sc))
    zp[...] = z.astype(BF)
    zp.send()
    st[...] = two_sums(z, member_of(info))


def k_expand_a(info, st, b0, b1, b2, b3, stp, stx, prm, inv_count, ea, z3, st3, act, vh, table, stats, hold):
    act_all(info, st, (b0, b1, b2, b3), prm, 1, inv_count[4:8], act, vh, table, stats)
    z = dot_nn(act[...], matrix(ea))
    z3[...] = z
    hold[...] = stp[...] + stx[...]
    half = hold.shape[1] // 2
    part = hold[:, lanes_of(info[25] & 1, half)]
    spread(st3, jnp.concatenate([two_sums(z, member_of(info)), part], axis=1))


def k_join(info, st3, z3, zp, prm, inv_count, rbt, own, s1, s2, s3, low_a, sl, vh3, vhp, tab3, tabp, stat3, statp):
    q = info[0]
    member = member_of(info)
    inv8 = inv_count[4:8]
    lanes = z3.shape[1]
    even, odd = st3[0], st3[1]
    for d in range(2, st3.shape[0], 2):
        even = even + st3[d]
        odd = odd + st3[d + 1]
    tab3[...], stat3[...] = stat_table(even[:, :lanes] + odd[:, :lanes], inv8)
    tabp[...], statp[...] = stat_table(jnp.concatenate([even[:, lanes:], odd[:, lanes:]], axis=1), inv8)
    stat3.send()
    statp.send()
    va = centre(z3[...], tab3[...], member)
    vb = centre(zp[...].astype(F32), tabp[...], member)
    vh3[...] = f2(va).astype(BF)
    vhp[...] = f2(vb).astype(BF)
    vh3.send()
    vhp.send()
    pre = affine(va, prm[0]) + affine(vb, prm[1])
    m = wide(f3(half_mask(info)), pre.shape[-1])
    sig = jax.nn.sigmoid(pre)
    low = f2(pre * sig * m).astype(BF)
    low_a[...] = low
    low_a.send()
    sl[...] = f2(m * (sig * (1.0 + pre * (1.0 - sig)))).astype(BF)
    sl.send()
    products(low, rbt, q, LB, own, ((1, s1), (2, s2), (3, s3)))


def k_flat(info, st, zb, prm, inv_count, sb, own, s1, s2, s3, im, vh, table, stats):
    q = info[0]
    member = member_of(info)
    totals = sums_all(st)
    inv8 = inv_count[4:8]
    for j in range(NB):
        table[j], stats[j] = stat_table(totals[j], inv8)
    stats.send()
    vhat = centre(zb[...].astype(F32), table[q], member)
    vh[...] = f2(vhat).astype(BF)
    vh.send()
    act = f2(silu(affine(vhat, prm[2, q])) * f3(half_mask(info)) * keep_of(info, q))
    first, last = edge_cols()
    for t in range(3):
        shifted = rows_down(act) if t == 0 else (act if t == 1 else rows_up(act))
        for u in range(3):
            x = cols_right(shifted, first) if u == 0 else (shifted if u == 1 else cols_left(shifted, last))
            at = (3 * t + u) * LB
            im[:, at : at + LB] = x.astype(BF)
    im.send()
    products(im[...], sb, q, LB, own, ((1, s1), (2, s2), (3, s3)))


def k_expand_b(info, st, b0, b1, b2, b3, prm, inv_count, eb, z6, st6, act, vh, table, stats):
    act_all(info, st, (b0, b1, b2, b3), prm, 3, inv_count[4:8], act, vh, table, stats)
    z = dot_nn(act[...], matrix(eb))
    z6[...] = z
    spread(st6, two_sums(z, member_of(info)))


def k_output(info, st6, z6, low_a, cot, prm, inv_count, gb, vh6, st, output, gbs, tab6, stat6):
    member = member_of(info)
    tab6[...], stat6[...] = stat_table(sums_dp(st6), inv_count[4:8])
    stat6.send()
    vhat = centre(z6[...], tab6[...], member)
    vh6[...] = f2(vhat).astype(BF)
    pre = affine(vhat, prm[2]) + f3(low_a[...].astype(F32))
    m = wide(f3(half_mask(info)), pre.shape[-1])
    sig = jax.nn.sigmoid(pre)
    output[:, 0:PX, :] = pre * sig * m
    output[:, PX:, :] = jnp.zeros((FR, 64 - PX, pre.shape[-1]), F32)
    output.send()
    g = cot[...].astype(F32)[:, 0:PX, :] * m * (sig * (1.0 + pre * (1.0 - sig)))
    gb[...] = f2(g)
    gbs[...] = f2(g).astype(BF)
    gbs.send()
    along = by_subnet(jnp.sum(g * vhat, axis=1), member)
    offset = by_subnet(jnp.sum(g, axis=1), member)
    spread(st, jnp.concatenate([along, offset], axis=0))


def k_back_six(info, st, gb, vh6, tab6, prm, inv_count, eb, act5, own, s1, s2, s3, pg, grad):
    q = info[0]
    member = member_of(info)
    totals = sums_dp(st)
    pg[...] = param_grads(totals)
    pg.send()
    vhat = f3(vh6[...].astype(F32))
    m = wide(f3(half_mask(info)), vhat.shape[-1])
    g = m * norm_back(f3(gb[...]), vhat, tab6[...], totals, inv_count[4:8], member, prm[2, 0:1])
    low = f2(g).astype(BF)
    products(low, eb, q, LB, own, ((1, s1), (2, s2), (3, s3)))
    grad[...] = by_x_first(dot_tn(act5[...], low), st.shape[0]).astype(BF)


def back_stat(g, vhat, member, gl, st):
    low = f2(g).astype(BF)
    gl[...] = low
    g = f3(low.astype(F32))
    along = by_subnet(jnp.sum(g * vhat, axis=1), member)
    offset = by_subnet(jnp.sum(g, axis=1), member)
    spread(st, jnp.concatenate([along, offset], axis=0))


def k_back_stat(norm):
    def body(info, own, r1, r2, r3, vh, prm, gl, st):
        q = info[0]
        part = own[...] + r1[...].astype(F32) + r2[...].astype(F32) + r3[...].astype(F32)
        vhat = f3(vh[...].astype(F32))
        g = f3(part * half_mask(info)) * keep_of(info, q) * slope(affine(vhat, prm[norm, q]))
        back_stat(g, vhat, member_of(info), gl, st)

    return body


def gz_all(info, st, grads, values, table, prm, norm, inv8, gz, pg, hold):
    q = info[0]
    member = member_of(info)
    totals = sums_all(st)
    for j in range(NB):
        pg[j] = param_grads(totals[j])
        hold[j] = totals[j]
    pg.send()
    m = f3(half_mask(info))
    for k in range(NB):
        j = q ^ k
        vhat = f3(values(k, j).astype(F32))
        g = norm_back(f3(grads[k][...].astype(F32)), vhat, table[j], hold[j], inv8, member, prm[norm, j][0:1])
        gz[:, lanes_of(j, LB)] = f2(m * g).astype(BF)


def k_back_five(info, st, g0, g1, g2, g3, vh5, tab5, prm, inv_count, sb, vh4, im4, gl, st4, pg, grad, gz5, hold):
    q = info[0]
    gz_all(
        info, st, (g0, g1, g2, g3), lambda k, j: vh5[:, lanes_of(j, LB)], tab5, prm, 3, inv_count[4:8],
        gz5, pg, hold,
    )
    terms = dot_nn(gz5[...], sb[...])
    first, last = edge_cols()
    total = None
    for t in range(3):
        for u in range(3):
            at = (3 * t + u) * LB
            x = terms[:, at : at + LB]
            x = cols_left(x, last) if u == 0 else (x if u == 1 else cols_right(x, first))
            x = rows_up(x) if t == 0 else (x if t == 1 else rows_down(x))
            total = x if total is None else total + x
    vhat = f3(vh4[...].astype(F32))
    g = f3(total * half_mask(info)) * keep_of(info, q) * slope(affine(vhat, prm[2, q]))
    back_stat(g, vhat, member_of(info), gl, st4)
    grad[...] = by_x_first(dot_tn(gz5[...], im4[...]), st.shape[0] // NB).astype(BF)


def k_back_four(info, st, g0, g1, g2, g3, v0, v1, v2, v3, tab4, prm, inv_count, rbt, gb, sl, vh3, vhp, low_a, ga, st3, pg, grad, gz4, hold):
    member = member_of(info)
    values = (v0, v1, v2, v3)
    gz_all(
        info, st, (g0, g1, g2, g3), lambda k, j: values[k][...], tab4, prm, 2, inv_count[4:8], gz4, pg, hold
    )
    low = gz4[...]
    back = dot_nn(low, matrix(rbt))
    g = (gb[...].astype(F32) + back) * sl[...].astype(F32)
    ga[...] = g
    g = f3(g)
    along = by_subnet(jnp.sum(g * f3(vh3[...].astype(F32)), axis=1), member)
    other = by_subnet(jnp.sum(g * f3(vhp[...].astype(F32)), axis=1), member)
    offset = by_subnet(jnp.sum(g, axis=1), member)
    half = offset.shape[-1] // 2
    tail = jnp.concatenate([offset[:, :half], offset[:, half:]], axis=0)
    spread(st3, jnp.concatenate([jnp.concatenate([along, other], axis=0), tail], axis=1))
    grad[...] = dot_tn(low, low_a[...]).astype(BF)


def add_hop(kept, away, sums):
    for k in range(4):
        total = kept[k].astype(F32) + away[k].astype(F32)
        sums[k][...] = total if k == 0 else total.astype(BF)
        sums[k].send()


def line_sum(parts):
    total = parts[0][...]
    for part in parts[1:]:
        total = total + part[...].astype(F32)
    return total


def taps_apart(ref, value):
    for tap in range(9):
        ref[tap] = value[:, tap * LB : (tap + 1) * LB]
    ref.send()


def emit_line(info, full, outs, first, part=0, parts=1):
    kept, away = outs
    rows = kept.shape[1]
    here = info[25] & 1
    lanes = full.shape[1]
    for z in range(4):
        for ref, x in ((kept, here), (away, here ^ 1)):
            at = ((2 * z + x) * parts + part) * rows
            ref[z, :, first : first + lanes] = full[pl.ds(pl.multiple_of(at, rows), rows), :].astype(BF)


def k_back_join(info, st, ga, vh3, vhp, tab3, tabp, prm, inv_count, ea, act2, every, grad_r, *refs):
    q = info[0]
    member = member_of(info)
    own, s1, s2, s3, gzp, pg3, pgp, *grads, full_a, full_s = refs
    totals = sums_dp(st)
    lanes = ga.shape[-1]
    tail = totals[:, lanes:]
    offset = jnp.concatenate([tail[0:4], tail[4:8]], axis=1)
    tot3 = jnp.concatenate([totals[0:4, :lanes], offset], axis=0)
    totp = jnp.concatenate([totals[4:8, :lanes], offset], axis=0)
    pg3[...] = param_grads(tot3)
    pgp[...] = param_grads(totp)
    pg3.send()
    pgp.send()
    inv8 = inv_count[4:8]
    g = f3(ga[...])
    m = wide(f3(half_mask(info)), lanes)
    low = f2(m * norm_back(g, f3(vh3[...].astype(F32)), tab3[...], tot3, inv8, member, prm[0, 0:1])).astype(BF)
    products(low, ea, q, LB, own, ((1, s1), (2, s2), (3, s3)))
    lowp = f2(m * norm_back(g, f3(vhp[...].astype(F32)), tabp[...], totp, inv8, member, prm[1, 0:1])).astype(BF)
    gzp[...] = lowp
    full_a[...] = dot_tn(act2[...], low)
    full_s[...] = dot_tn(every[...], lowp)
    if len(grads) == 2:
        emit_line(info, grad_r, grads, 0)
        emit_line(info, full_a, grads, lanes)
        for part in range(2):
            emit_line(info, full_s, grads, (2 + part) * lanes, part, 2)
        return
    grad = grads[0]
    count = st.shape[0]
    rows = full_s.shape[0] // count // 2
    grad[:, 0:lanes] = grad_r[...]
    grad[:, lanes : 2 * lanes] = full_a[...].astype(BF)
    for part in range(2):
        picked = [full_s[(2 * d + part) * rows : (2 * d + part + 1) * rows, :] for d in range(count)]
        at = (2 + part) * lanes
        grad[:, at : at + lanes] = jnp.concatenate(picked, axis=0).astype(BF)


def k_back_small(info, gzp, sc, own, s1, s2, s3):
    q = info[0]
    low = gzp[...]
    products(low, sc, q, 256, own, ((1, s1), (2, s2), (3, s3)))


def k_back_two(info, st, g0, g1, g2, g3, vh2, tab2, prm, inv_count, sa, vh1, im1, *refs):
    q = info[0]
    member = member_of(info)
    refs, (gz2, hold, full) = refs[:-3], refs[-3:]
    if len(refs) > 5:
        rows = refs[0].shape[1]
        for z in range(4):
            refs[6][z * rows : (z + 1) * rows, :] = (refs[0][z].astype(F32) + refs[1][z].astype(F32)).astype(BF)
        refs[6].send()
        (gl, st1, pg, saved), grads = refs[2:6], refs[7:]
    else:
        (gl, st1, pg, saved), grads = refs[0:4], refs[4:]
    gz_all(
        info, st, (g0, g1, g2, g3), lambda k, j: vh2[:, lanes_of(j, LB)], tab2, prm, 1, inv_count[4:8],
        gz2, pg, hold,
    )
    terms = dot_nn(gz2[...], sa[...])
    _, last = edge_cols()
    y = [terms[:, tap * LB : (tap + 1) * LB] for tap in range(9)]
    planes = [
        y[4],
        cols_left(y[3], last) + y[5],
        rows_up(y[1]) + y[7],
        rows_up(cols_left(y[0], last) + y[2]) + cols_left(y[6], last) + y[8],
    ]
    kept = keep_of(info, q)
    along = None
    offset = None
    for p in range(4):
        vhat = f3(vh1[p].astype(F32))
        g = f3(planes[p] * plane_mask(info, p)) * kept * slope(affine(vhat, prm[0, q]))
        low = f2(g).astype(BF)
        gl[p] = low
        saved[p] = low
        g = f3(low.astype(F32))
        a, b = jnp.sum(g * vhat, axis=1), jnp.sum(g, axis=1)
        along = a if along is None else along + a
        offset = b if offset is None else offset + b
    saved.send()
    spread(st1, jnp.concatenate([by_subnet(along, member), by_subnet(offset, member)], axis=0))
    full[...] = dot_tn(gz2[...], im1[...])
    emit(info, full, grads)


def k_last(info, st, g0, g1, g2, g3, v0, v1, v2, v3, tab1, prm, inv_count, xm, *refs):
    q = info[0]
    member = member_of(info)
    gz1, pg, grad, hold = refs
    totals = sums_all(st)
    inv16 = inv_count[0:4]
    for j in range(NB):
        pg[j] = param_grads(totals[j])
        hold[j] = totals[j]
    pg.send()
    total = None
    for p in range(4):
        m = f3(plane_mask(info, p))
        for k, (gref, vref) in enumerate(((g0, v0), (g1, v1), (g2, v2), (g3, v3))):
            j = q ^ k
            vhat = f3(vref[p].astype(F32))
            g = norm_back(f3(gref[p].astype(F32)), vhat, tab1[j], hold[j], inv16, member, prm[0, j][0:1])
            gz1[p, :, lanes_of(j, LB)] = f2(m * g).astype(BF)
        term = dot_tn(gz1[p], xm[p])
        total = term if total is None else total + term
    grad[...] = total.astype(BF)


def k_features(info, gz1, rat, own, r1, r2, r3, gf, nat):
    for p in range(4):
        back = dot_nn(gz1[p], rat[...])
        if p == 0:
            back = back + own[...] + r1[...].astype(F32) + r2[...].astype(F32) + r3[...].astype(F32)
        back = back * wide(plane_mask(info, p), back.shape[-1])
        high = back.astype(BF)
        nat[0, p] = high.astype(F32)
        nat[1, p] = back - high.astype(F32)
    row, col, target = natural_index(1)
    select = jnp.where(target == row * 16 + col, 1.0, 0.0).astype(BF)
    for frame in range(FR):
        out = None
        for part in range(2):
            x = jnp.concatenate(
                [nat[part, p, frame * PX : (frame + 1) * PX, :] for p in range(4)], axis=0
            ).astype(BF)
            y = dot_nn(select, x)
            out = y if out is None else out + y
        gf[frame] = out


def k_tables(info, *refs):
    mids, pairs, outs, gains = refs[0:4], refs[4:8], refs[8:11], refs[11:14]
    stats_mid, grads_mid, stats_out, grads_out = refs[14:]
    for i in range(4):
        for j in range(NB):
            at = slice(j * LB, (j + 1) * LB)
            stats_mid[i, 0, :, at] = mids[i][j, 0:4]
            stats_mid[i, 1, :, at] = mids[i][j, 4:8]
            grads_mid[i, :, at] = pairs[i][j]
    for i in range(3):
        stats_out[i, 0] = outs[i][0:4]
        stats_out[i, 1] = outs[i][4:8]
        grads_out[i] = gains[i][...]


def k_end_grads(info, early, grad, spatial, expand, reduce, other, shortcut):
    value = early[...].astype(F32)
    taps_apart(spatial, value)
    expand[...] = value[:, TAPS:]
    value = grad[...].astype(F32)
    lanes = expand.shape[-1]
    reduce[...] = value[:, :lanes]
    other[...] = value[:, lanes : 2 * lanes]
    shortcut[...] = jnp.concatenate([value[:, 2 * lanes : 3 * lanes], value[:, 3 * lanes :]], axis=0)


def k_hop(info, kept, away, *sums):
    add_hop(kept, away, sums)


def k_final(info, *refs):
    parts, others, spatial, reduce = refs[:-3], refs[-3], refs[-2], refs[-1]
    taps_apart(spatial, line_sum(parts))
    total = others[0].astype(F32)
    for d in range(1, others.shape[0]):
        total = total + others[d].astype(F32)
    reduce[...] = total


def swap(value, k):
    return lax.ppermute(value, "chan", [(i, i ^ k) for i in range(NB)])


def partners(value):
    return [value] + [swap(value, k) for k in (1, 2, 3)]


def partners_two_hops(value):
    far = swap(value, 2)
    return [value, swap(value, 1), far, swap(far, 1)]


def everywhere(value):
    return lax.all_to_all(value, ("dp", "chan"), 0, 0, tiled=True)


def along_dp(value):
    return lax.all_to_all(value, "dp", 0, 0, tiled=True)


def after(value, *others):
    return lax.optimization_barrier((value,) + others)[0]


def swap_dp(value, k):
    return lax.ppermute(value, "dp", [(i, i ^ k) for i in range(lax.axis_size("dp"))])


def along_z(value):
    return [value] + [swap_dp(value, 2 * k) for k in (1, 2, 3)]


def across_x(line, *others):
    return line + [swap_dp(after(v, *others), 1) for v in line]


def add_near(kept, away):
    return [(kept[k].astype(F32) + away[k].astype(F32)).astype(F32 if k == 0 else BF) for k in range(4)]


def add_far(parts):
    return parts[0] + parts[1].astype(F32) + parts[2].astype(F32) + parts[3].astype(F32)


def reduce_pairs(value):
    if lax.axis_size("dp") != 8:
        return lax.psum_scatter(value, "dp", scatter_dimension=0, tiled=True)
    groups = [[2 * z, 2 * z + 1] for z in range(4)]
    return lax.psum_scatter(value, "dp", scatter_dimension=0, tiled=True, axis_index_groups=groups)


def reduce_lines(value):
    if lax.axis_size("dp") != 8:
        return value
    groups = [[2 * z + x for z in range(4)] for x in range(2)]
    return lax.psum_scatter(value, "dp", scatter_dimension=0, tiled=True, axis_index_groups=groups)


def shards(
    features,
    cotangent,
    reduce_a,
    spatial_a,
    expand_a,
    shortcut,
    reduce_b,
    spatial_b,
    expand_b,
    norms_mid,
    norms_out,
    crop_side,
    subnet_of,
    width_of,
):
    ndp = lax.axis_size("dp")
    nall = ndp * NB
    hops = ndp == 8
    hidden = norms_mid.shape[-1]
    cin = features.shape[-1]
    cout = cotangent.shape[-1]
    rows = reduce_a.shape[1]
    er = expand_a.shape[0]
    sr = shortcut.shape[0]
    position = lax.axis_index("chan").astype(jnp.int32)
    place = lax.axis_index("dp").astype(jnp.int32)
    width = jnp.sum(
        jnp.where(subnet_of[:, None] == jnp.arange(4, dtype=jnp.int32)[None, :], width_of[None, :], 0), axis=1
    )
    info = jnp.concatenate([position[None], crop_side, subnet_of, width, place[None]])

    ra_t = reduce_a.T
    sa_t = jnp.transpose(spatial_a, (2, 0, 1)).reshape(rows, TAPS)
    half = (crop_side + 1) // 2
    per16 = jnp.where(crop_side > 8, crop_side * crop_side, 4 * crop_side * crop_side)
    per8 = jnp.where(half > 4, half * half, 4 * half * half)
    lane = jnp.arange(LB, dtype=jnp.int32)[None, :]
    pixels = jnp.where(lane == subnet_of[:, None], per16[:, None], 0)
    pixels = pixels + jnp.where(lane == subnet_of[:, None] + 4, per8[:, None], 0)
    pixels = jnp.concatenate([pixels.astype(F32), jnp.zeros((rows, LB), F32)], axis=0)[: max(rows, FR)]
    prm, prm_out, inv_count = Held("prm"), Held("prm_out"), Held("inv")
    tab1, tab2, tab4, tab5 = [Held("tab", i) for i in range(4)]
    tab3, tabp, tab6 = [Held("tab_out", i) for i in range(3)]
    slots = [
        jnp.transpose(x.reshape(-1, 2, NB, LB), (0, 2, 1, 3)).reshape(-1, 2, LB) for x in (norms_mid, norms_out)
    ]
    slots = [jnp.pad(x, ((0, 0), (0, 6), (0, 0))) for x in slots]
    blank = jnp.zeros((SLOTS, 8, LB), F32)
    state = jnp.concatenate([slots[0], blank[:1], slots[1], blank[TAB:]], axis=0)
    table = ((NB, 8, LB), F32, "hbm")
    one_block = ((NP, LB), F32)
    send = ((NP, LB), BF)
    sends = [one_block, send, send, send]
    stat_all = ((nall, 8, LB), F32)
    stat_own = ((ndp, 8, cout), F32)
    stat_wide = ((ndp, 8, cout + cout // 2), F32)
    map_out = ((NP, cout), F32)
    low_out = ((NP, cout), BF, "hbm")
    low_mid = ((NP, hidden), BF, "hbm")
    tab_out = ((8, cout), F32, "hbm")

    if hops:
        line_ra = along_z(ra_t)
        line_sa = along_z(after(jnp.concatenate([sa_t, pixels.astype(BF)], axis=1), line_ra[1]))
        pieces = across_x(line_ra, *line_ra[1:])
        feat = after(features.reshape(FR, 256, cin), pieces[4])
        rat = Gathered(pieces, rows, 0, cin)
    else:
        rat = Pinned(lax.all_gather(ra_t, "dp", axis=0, tiled=True))
        sa = Pinned(lax.all_gather(sa_t, "dp", axis=0, tiled=True))
        counts = Pinned(lax.psum(pixels, "dp"))
        feat = features.reshape(FR, 256, cin)
    xm, xs, small = call(
        k_prep, [((4, NP, cin), BF), ((4, NP, cin), BF, "hbm"), ((NP, cin), BF)],
        info, Pinned(feat), name="prep",
    )
    pack_mid = jnp.concatenate([expand_a, shortcut, after(reduce_b, small).T], axis=0)
    pack_end = jnp.concatenate(
        [jnp.transpose(after(spatial_b, small), (2, 0, 1)).reshape(rows, TAPS), expand_b], axis=1
    )
    own, near, far, *stacked = call(
        k_first,
        [((4, NP, LB), F32), ((2, 4, NP, LB), BF), ((4, NP, LB), F32)]
        + ([((4, rows, TAPS + LB), BF, "hbm")] if hops else []),
        info, after(xm, pack_mid, pack_end), rat, *([Pinned(x) for x in line_sa] if hops else []), name="first",
    )
    if hops:
        sa_pieces = [stacked[0], swap_dp(stacked[0], 1)]
        sa = Gathered(sa_pieces, rows, 0, TAPS)
        counts = Gathered(sa_pieces, 16, TAPS, LB)
    near = swap(near, 1)
    far = (far + near[1].astype(F32)).astype(BF)
    mid = lax.all_gather(after(pack_mid, far), "dp", axis=0)

    def mid_rows(first, size):
        if size % 16 == 0:
            return Pinned(mid, lambda ref, info: ref.at[:, first : first + size, :], (ndp, size, cout))
        return Pinned(mid[:, first : first + size].reshape(ndp * size, cout))

    ea = mid_rows(0, er)
    sc = mid_rows(er, sr)
    rbt = mid_rows(er + sr, rows)
    end = lax.all_gather(pack_end, "dp", axis=0, tiled=True)
    sb = Pinned(end, lambda ref, info: ref.at[:, 0:TAPS], (hidden, TAPS))
    eb = Pinned(end, lambda ref, info: ref.at[:, TAPS : TAPS + cout], (hidden, cout))

    far = swap(far, 2)
    zb1, st = call(
        k_stat_first, [((4, NP, LB), BF), stat_all], info, own, near, far, name="stat_one"
    )
    smalls = partners_two_hops(after(small, st))
    st = after(everywhere(after(st, *(sa_pieces[1:] if hops else ()))), *smalls[1:])
    own, s1, s2, s3, im1, vh1, stat1, state = call(
        k_down,
        sends + [((NP, TAPS), BF, "hbm"), ((4, NP, LB), BF, "hbm"), tab1, inv_count, table],
        info, st, zb1, prm, sa, counts, state=state, name="down",
    )
    zb, st = call(k_stat, [send, stat_all], info, own, swap(s1, 1), swap(s2, 2), swap(s3, 3), name="stat_two")
    zs = partners(zb)
    smalls = lax.optimization_barrier(tuple(smalls) + (st,))[:4]
    stp, every, zp = call(
        k_proj, [((8, cout), F32), ((NP, NB * cin), BF, "hbm"), low_out], info, *smalls, sc, name="proj"
    )
    st = after(everywhere(st), stp)
    stx = swap_dp(stp, 1)
    z3, st3, act2, vh2, stat2, state = call(
        k_expand_a, [map_out, stat_wide, low_mid, low_mid, tab2, table],
        info, st, *zs, stp, stx, prm, inv_count, ea, scratch=[pltpu.VMEM((8, cout), F32)], state=state, name="expand_a",
    )
    st3 = along_dp(st3)
    own, s1, s2, s3, low_a, sl, vh3, vhp, stat3, statp, state = call(
        k_join, sends + [low_out, low_out, low_out, low_out, tab3, tabp, tab_out, tab_out],
        info, st3, z3, Pinned(zp), prm_out, inv_count, rbt, state=state, name="join",
    )
    zb, st = call(k_stat, [send, stat_all], info, own, swap(s1, 1), swap(s2, 2), swap(s3, 3), name="stat_four")
    st = everywhere(st)
    own, s1, s2, s3, im4, vh4, stat4, state = call(
        k_flat, sends + [((NP, TAPS), BF, "hbm"), ((NP, LB), BF, "hbm"), tab4, table],
        info, st, zb, prm, inv_count, sb, state=state, name="flat",
    )
    zb, st = call(k_stat, [send, stat_all], info, own, swap(s1, 1), swap(s2, 2), swap(s3, 3), name="stat_five")
    zs = partners(zb)
    st = everywhere(st)
    z6, st6, act5, vh5, stat5, state = call(
        k_expand_b, [map_out, stat_own, low_mid, low_mid, tab5, table],
        info, st, *zs, prm, inv_count, eb, state=state, name="expand_b",
    )
    vhs4 = partners(after(vh4, st6))
    st6 = after(along_dp(st6), *vhs4[1:])
    gb, vh6, st, output, gbs, stat6, state = call(
        k_output,
        [map_out, ((NP, cout), BF), stat_own, ((FR, 64, cout), F32, "hbm"), low_out, tab6, tab_out],
        info, st6, z6, Pinned(low_a), Pinned(cotangent.reshape(FR, 64, cout)), prm_out, inv_count, state=state, name="output",
    )

    def early(first, size):
        return ((hidden, TAPS + cout), BF, "hbm", lambda ref: ref.at[:, first : first + size], (hidden, size))

    def summed(size, lanes):
        return [((size, lanes), F32, "hbm")] + [((size, lanes), BF, "hbm")] * 3

    def z_parts(sums):
        return [sums[0]] + [swap_dp(sums[k], 2 * k) for k in (1, 2, 3)]

    def reduced(size, width_):
        if hops:
            return [((4, size, width_), BF, "hbm")] * 2
        return [((ndp * size, width_), BF, "hbm")]

    def own_lanes(array):
        return Pinned(array, lambda ref, info: ref.at[:, lanes_of(info[0], LB)], (NP, LB))

    vh1_in = after(vh1, st)
    vhs1 = [vh1, swap(vh1_in, 1), swap(vh1_in, 2)]
    st = after(along_dp(st), *vhs1[1:])
    own, s1, s2, s3, pg6, grad_early, state = call(
        k_back_six, sends + [((2, cout), F32, "hbm"), early(TAPS, cout)],
        info, st, gb, vh6, tab6, prm_out, inv_count, eb, Pinned(act5), state=state, name="back_six",
    )
    gl, st, state = call(
        k_back_stat(3), [send, stat_all],
        info, own, swap(s1, 1), swap(s2, 2), swap(s3, 3), own_lanes(vh5), prm, state=state, name="back_stat_five",
    )
    gs = partners(gl)
    st = everywhere(st)
    hold = pltpu.VMEM((NB, 8, LB), F32)
    pair_mid = ((NB, 2, LB), F32, "hbm")
    gl, st, pg5, grad_early, state = call(
        k_back_five, [send, stat_all, pair_mid, early(0, TAPS)],
        info, st, *gs, Pinned(vh5), tab5, prm, inv_count, sb, Pinned(vh4), Pinned(im4),
        scratch=[pltpu.VMEM((NP, hidden), BF), hold], alias=(grad_early, 3), state=state, name="back_five",
    )
    gs = partners(gl)
    grad_early = reduce_pairs(grad_early)
    st = everywhere(st)
    ga, st, pg4, grad_r, state = call(
        k_back_four, [map_out, stat_wide, pair_mid, ((hidden, cout), BF, "hbm")],
        info, st, *gs, *[Pinned(v) for v in vhs4], tab4, prm, inv_count, rbt, Pinned(gbs), Pinned(sl),
        Pinned(vh3), Pinned(vhp), Pinned(low_a),
        scratch=[pltpu.VMEM((NP, hidden), BF), hold], state=state, name="back_four",
    )
    vhs1.append(swap(after(vhs1[2], st), 1))
    st = after(along_dp(st), vhs1[3], grad_early)
    if hops:
        grads = [((4, rows, 4 * cout), BF, "hbm")] * 2
    else:
        grads = [((hidden, 4 * cout), BF, "hbm")]
    own, s1, s2, s3, gzp, pg3, pgp, *grads, state = call(
        k_back_join, sends + [((NP, cout), BF)] + [((2, cout), F32, "hbm")] * 2 + grads,
        info, st, ga, Pinned(vh3), Pinned(vhp), tab3, tabp, prm_out, inv_count, ea,
        Pinned(act2), Pinned(every), Pinned(grad_r),
        scratch=[pltpu.VMEM((hidden, cout), F32), pltpu.VMEM((ndp * sr, cout), F32)], state=state, name="back_join",
    )
    grad_early = reduce_lines(after(grad_early, grads[0]))
    extra_in, extra_out = [], []
    if hops:
        extra_in = [Pinned(grads[0]), swap_dp(grads[1], 1)]
        extra_out = [((4 * rows, 4 * cout), BF, "hbm")]
    else:
        end_grad = reduce_pairs(grads[0])
    r1, r2, r3 = swap(s1, 1), swap(s2, 2), swap(s3, 3)
    sown, *small_sends = call(
        k_back_small, [((NP, cin), F32)] + [((NP, cin), BF)] * 3,
        info, after(gzp, r1), sc, name="back_small",
    )
    own = after(own, sown)
    gl, st, state = call(
        k_back_stat(1), [send, stat_all],
        info, own, r1, r2, r3, own_lanes(vh2), prm, state=state, name="back_stat_two",
    )
    gs = partners(gl)
    st = everywhere(st)
    small_one = swap(small_sends[0], 1)
    st = after(st, grad_early, small_one)
    gl, st, pg2, saved, *grad_sa, state = call(
        k_back_two, [((4, NP, LB), BF), stat_all, pair_mid, ((4, NP, LB), BF, "hbm")] + extra_out + reduced(rows, TAPS),
        info, st, *gs, Pinned(vh2), tab2, prm, inv_count, sa, Pinned(vh1), Pinned(im1), *extra_in,
        scratch=[pltpu.VMEM((NP, hidden), BF), hold, pltpu.VMEM((hidden, TAPS), F32)], state=state, name="back_two",
    )
    gs = [gl, swap(gl, 1), swap(gl, 2)]
    st = everywhere(st)
    gs.append(swap(after(gs[2], st), 1))
    small_back = [small_one] + [swap(after(small_sends[k - 1], gs[3]), k) for k in (2, 3)]
    extra_in, extra_out = [], []
    if hops:
        end_grad = reduce_lines(grad_sa[0])
        kept, away = grad_sa[2], swap_dp(grad_sa[1], 1)
    gz1, pg1, grad_rat, _ = call(
        k_last, [((4, NP, hidden), BF), pair_mid, ((hidden, cin), BF, "hbm")],
        info, st, Pinned(saved), Pinned(gs[1]), Pinned(gs[2]), gs[3], *[Pinned(v) for v in vhs1], tab1, prm, inv_count,
        Pinned(xs), scratch=[hold], state=state, name="last",
    )
    if hops:
        sums_sa = call(k_hop, summed(rows, TAPS), info, Pinned(after(kept, gz1)), away, name="hop")
        parts_sa = z_parts(sums_sa)
        grad_rat = after(grad_rat, sums_sa[0])
    else:
        parts_sa = [lax.psum_scatter(grad_sa[0], "dp", scatter_dimension=0, tiled=True).astype(F32)]
    spatial, expand, reduce, grad_a, grad_s = call(
        k_end_grads,
        [
            ((9, rows, LB), F32, "hbm"), ((er, cout), F32, "hbm"), ((rows, cout), F32, "hbm"),
            ((er, cout), F32, "hbm"), ((sr, cout), F32, "hbm"),
        ],
        info, Pinned(grad_early), Pinned(end_grad), name="end_grads",
    )
    parts_ra = along_dp(grad_rat.reshape(ndp, rows, cin))
    stats_mid, grad_norms_mid, stats_out, grad_norms_out = call(
        k_tables,
        [
            ((4, 2, 4, hidden), F32, "hbm"), ((4, 2, hidden), F32, "hbm"),
            ((3, 2, 4, cout), F32, "hbm"), ((3, 2, cout), F32, "hbm"),
        ],
        info,
        *[Pinned(x) for x in (stat1, stat2, stat4, stat5, pg1, pg2, pg4, pg5, stat3, statp, stat6, pg3, pgp, pg6)],
        name="tables",
    )
    gf = call(
        k_features, [((FR, 256, cin), F32, "hbm")],
        info, gz1, rat, Pinned(sown), *small_back,
        scratch=[pltpu.VMEM((2, 4, NP, cin), F32)], name="features",
    )[0]
    spatial_sa, grad_rat = call(
        k_final, [((9, rows, LB), F32, "hbm"), ((rows, cin), F32, "hbm")],
        info, *[Pinned(after(x, gf, spatial)) for x in parts_sa[:1]], *[after(x, gf, spatial) for x in parts_sa[1:]],
        after(parts_ra, gf, spatial), name="final",
    )
    grad_reduce_a = grad_rat.T
    grad_spatial_a = jnp.transpose(spatial_sa, (0, 2, 1))
    grad_spatial_b = jnp.transpose(spatial, (0, 2, 1))
    grad_expand_b = expand
    grad_reduce_b = reduce.T
    return (
        output.reshape(FR, 8, 8, cout),
        gf.reshape(FR, 16, 16, cin),
        grad_reduce_a,
        grad_spatial_a,
        grad_a,
        grad_s,
        grad_reduce_b,
        grad_spatial_b,
        grad_expand_b,
        grad_norms_mid,
        grad_norms_out,
        stats_mid,
        stats_out,
    )


def solution(mesh):
    in_specs = (
        P("dp", None, None, "chan"),
        P("dp", None, None, "chan"),
        P("chan", "dp"),
        P(None, "chan", "dp"),
        P("dp", "chan"),
        P("dp", "chan"),
        P("chan", "dp"),
        P(None, "chan", "dp"),
        P("dp", "chan"),
        P(),
        P(None, None, "chan"),
        P("dp"),
        P("dp"),
        P(),
    )
    out_specs = (
        P("dp", None, None, "chan"),
        P("dp", None, None, "chan"),
        P("chan", "dp"),
        P(None, "chan", "dp"),
        P("dp", "chan"),
        P("dp", "chan"),
        P("chan", "dp"),
        P(None, "chan", "dp"),
        P("dp", "chan"),
        P(),
        P(None, None, "chan"),
        P(),
        P(None, None, None, "chan"),
    )
    return jax.shard_map(shards, mesh=mesh, in_specs=in_specs, out_specs=out_specs, check_vma=False)
```

```python
import jax
import jax.numpy as jnp
from jax import lax
from jax.experimental import pallas as pl
from jax.experimental.pallas import tpu as pltpu
from jax.sharding import PartitionSpec as P

EPSILON = 1e-05
BF = jnp.bfloat16
F32 = jnp.float32
FR = 8
RP = 7
QP = 8
PX = RP * QP
NP = FR * PX
LB = 128
NB = 4
TAPS = 9 * LB


class Pinned:
    def __init__(self, array, view=None, shape=None):
        self.array = array
        self.view = view
        self.shape = array.shape if shape is None else shape


class Gathered:
    def __init__(self, pieces, rows, first, lanes):
        self.pieces = pieces
        self.rows = rows
        self.window = (slice(0, rows), slice(first, first + lanes))
        self.shape = (8 * rows, lanes)


class Late:
    def __init__(self, ref, copies):
        self.ref = ref
        self.copies = copies
        self.waiting = True

    def ready(self):
        if self.waiting:
            for copy in self.copies:
                copy.wait()
            self.waiting = False
        return self.ref

    def __getitem__(self, index):
        return self.ready()[index]

    @property
    def shape(self):
        return self.ref.shape


class Saved:
    def __init__(self, ref, copy):
        self.ref = ref
        self.copy = copy
        self.sent = False

    def __setitem__(self, index, value):
        self.ref[index] = value

    def __getitem__(self, index):
        return self.ref[index]

    @property
    def shape(self):
        return self.ref.shape

    def send(self):
        self.sent = True
        self.copy.start()


PRM, INV, PRM_OUT, TAB, TAB_OUT, SLOTS = 0, 16, 17, 29, 45, 57


class Held:
    def __init__(self, kind, norm=0, ref=None):
        self.kind = kind
        self.norm = norm
        self.ref = ref

    def __getitem__(self, index):
        if self.kind == "prm":
            norm, j = index
            return self.ref[PRM + norm * NB + j][0:2]
        if self.kind == "inv":
            return self.ref[INV][index]
        if self.kind == "tab":
            return self.ref[TAB + self.norm * NB + index]
        if self.kind == "prm_out":
            norm = index[0] if isinstance(index, tuple) else index
            value = jnp.concatenate([self.ref[PRM_OUT + norm * NB + b][0:2] for b in range(NB)], axis=1)
            return value[index[1]] if isinstance(index, tuple) else value
        return jnp.concatenate([self.ref[TAB_OUT + self.norm * NB + b] for b in range(NB)], axis=1)

    def __setitem__(self, index, value):
        if self.kind == "inv":
            self.ref[(INV,) + index] = value
        elif self.kind == "tab":
            self.ref[TAB + self.norm * NB + index] = value
        else:
            for b in range(NB):
                self.ref[TAB_OUT + self.norm * NB + b] = value[:, b * LB : (b + 1) * LB]


def call(body, outs, info, *args, scratch=(), name, alias=None, state=None):
    flat = []
    buffers = []
    copies = 0
    listed, outs = outs, [o for o in outs if not isinstance(o, Held)]
    held = [] if state is None else [state]
    for a in args:
        if isinstance(a, Held):
            continue
        if isinstance(a, Gathered):
            flat += [(p, True) for p in a.pieces]
            buffers.append(pltpu.VMEM(a.shape, a.pieces[0].dtype))
            copies += 8
        elif isinstance(a, Pinned):
            flat.append((a.array, True))
            buffers.append(pltpu.VMEM(a.shape, a.array.dtype))
            copies += 1
        else:
            flat.append((a, False))
    saved = [len(o) > 2 for o in outs]
    for o, s in zip(outs, saved):
        if s:
            buffers.append(pltpu.VMEM(o[4] if len(o) > 3 else o[0], o[1]))
            copies += 1
    extra = [] if alias is None else [alias[0]]
    arrays = [pltpu.with_memory_space_constraint(a, pltpu.HBM) if p else a for a, p in flat]
    arrays += [pltpu.with_memory_space_constraint(a, pltpu.HBM) for a in extra]
    vmem = pl.BlockSpec(memory_space=pltpu.VMEM)
    hbm = pl.BlockSpec(memory_space=pltpu.HBM)

    def kernel(*refs):
        refs = list(refs)
        info_ref = refs.pop(0)
        ins = refs[: len(flat)]
        refs = refs[len(flat) + len(extra) :]
        if held:
            held_in = refs.pop(0)
        results, refs = refs[: len(outs)], refs[len(outs) :]
        if held:
            held_out = refs.pop(0)
            held_out[...] = held_in[...]
        bufs, refs = refs[: len(buffers)], refs[len(buffers) :]
        if copies:
            sems, refs = refs[0], refs[1:]
        used = 0
        given = []
        late = []
        for a in args:
            if isinstance(a, Held):
                given.append(Held(a.kind, a.norm, held_in))
                continue
            if not isinstance(a, (Gathered, Pinned)):
                given.append(ins.pop(0))
                continue
            buf = bufs.pop(0)
            moves = []
            if isinstance(a, Gathered):
                blocks = []
                for piece in a.pieces:
                    ref = ins.pop(0)
                    blocks += [ref] if len(piece.shape) == 2 else [ref.at[k] for k in range(4)]
                for i in range(8):
                    source = info_ref[25] ^ (2 * (i % 4)) ^ (i // 4)
                    rows = pl.ds(pl.multiple_of(source * a.rows, a.rows), a.rows)
                    moves.append(pltpu.make_async_copy(blocks[i].at[a.window], buf.at[rows], sems.at[used]))
                    used += 1
            else:
                ref = ins.pop(0)
                source = ref if a.view is None else a.view(ref, info_ref)
                moves.append(pltpu.make_async_copy(source, buf, sems.at[used]))
                used += 1
            for move in moves:
                move.start()
            late.append(Late(buf, moves))
            given.append(late[-1])
        produced = []
        outgoing = []
        slots = iter(zip(outs, saved, results))
        for listing in listed:
            if isinstance(listing, Held):
                produced.append(Held(listing.kind, listing.norm, held_out))
                continue
            o, s, ref = next(slots)
            if s:
                buf = bufs.pop(0)
                target = o[3](ref) if len(o) > 3 else ref
                ref = Saved(buf, pltpu.make_async_copy(buf, target, sems.at[used]))
                used += 1
                outgoing.append(ref)
            produced.append(ref)
        body(info_ref, *given, *produced, *refs)
        for one in outgoing:
            if not one.sent:
                one.send()
        for one in late:
            one.ready()
        for one in outgoing:
            one.copy.wait()

    return pl.pallas_call(
        kernel,
        out_shape=[(pltpu.HBM if s else jax.ShapeDtypeStruct)(o[0], o[1]) for o, s in zip(outs, saved)]
        + [jax.ShapeDtypeStruct(x.shape, x.dtype) for x in held],
        in_specs=[pl.BlockSpec(memory_space=pltpu.SMEM)]
        + [hbm if p else vmem for _, p in flat]
        + [hbm] * len(extra)
        + [vmem] * len(held),
        out_specs=[hbm if s else vmem for s in saved] + [vmem] * len(held),
        scratch_shapes=buffers + ([pltpu.SemaphoreType.DMA((copies,))] if copies else []) + list(scratch),
        input_output_aliases={} if alias is None else {1 + len(flat): alias[1]},
        compiler_params=pltpu.CompilerParams(vmem_limit_bytes=40 << 20),
        cost_estimate=pl.CostEstimate(flops=1, bytes_accessed=1, transcendentals=0),
        name=name,
    )(info, *arrays, *held)


def f3(value):
    return value.reshape(FR, PX, value.shape[-1])


def f2(value):
    return value.reshape(NP, value.shape[-1])


def wide(value, lanes):
    count = lanes // value.shape[-1]
    return value if count == 1 else jnp.concatenate([value] * count, axis=-1)


def dot_nn(left, right):
    return lax.dot_general(left, right, (((1,), (0,)), ((), ())), preferred_element_type=F32)


def dot_nt(left, right):
    return lax.dot_general(left, right, (((1,), (1,)), ((), ())), preferred_element_type=F32)


def dot_tn(left, right):
    return lax.dot_general(left, right, (((0,), (0,)), ((), ())), preferred_element_type=F32)


def frame_scalars(info, first):
    row = lax.broadcasted_iota(jnp.int32, (FR, LB), 0)
    out = jnp.zeros((FR, LB), jnp.int32)
    for frame in range(FR):
        out = jnp.where(row == frame, info[first + frame], out)
    return out


def member_of(info):
    subnet = frame_scalars(info, 9)
    return [(subnet == s).astype(F32) for s in range(4)]


def keep_of(info, j):
    lane = lax.broadcasted_iota(jnp.int32, (FR, LB), 1) + j * LB
    return (lane < frame_scalars(info, 17)).astype(F32)[:, None, :]


def crop_mask(info, half, row_scale, row_off, col_scale, col_off):
    at = lax.broadcasted_iota(jnp.int32, (PX, LB), 0)
    row = (at >> 3) * row_scale + row_off
    col = (at & 7) * col_scale + col_off
    parts = []
    for frame in range(FR):
        side = info[1 + frame]
        if half:
            side = (side + 1) >> 1
        full = 8 if half else 16
        period = jnp.where(side > full // 2, full, full // 2)
        inside = ((row & (period - 1)) < side) & ((col & (period - 1)) < side)
        parts.append(jnp.where(inside, 1.0, 0.0).astype(F32))
    return jnp.concatenate(parts, axis=0)


def plane_mask(info, plane):
    return crop_mask(info, 0, 2, plane // 2, 2, plane % 2)


def half_mask(info):
    return crop_mask(info, 1, 1, 0, 1, 0)


def by_subnet(frames, member):
    lanes = frames.shape[-1]
    return jnp.concatenate(
        [jnp.sum(frames * wide(member[s], lanes), axis=0, keepdims=True) for s in range(4)], axis=0
    )


def by_frame(table, member):
    lanes = table.shape[-1]
    total = None
    for s in range(4):
        term = wide(member[s], lanes) * table[s : s + 1, :]
        total = term if total is None else total + term
    return total[:, None, :]


def sum_px(value):
    return jnp.sum(f3(value), axis=1)


def stat_table(totals, inv_count):
    inv_n = wide(inv_count, totals.shape[-1])
    mean = totals[0:4] * inv_n
    var = totals[4:8] * inv_n - mean * mean
    return jnp.concatenate([mean, lax.rsqrt(var + EPSILON)], axis=0), jnp.concatenate([mean, var], axis=0)


def centre(value, table, member):
    return (f3(value) - by_frame(table[0:4], member)) * by_frame(table[4:8], member)


def affine(vhat, prm):
    return prm[0:1][None] * vhat + prm[1:2][None]


def silu(pre):
    return pre * jax.nn.sigmoid(pre)


def slope(pre):
    sig = jax.nn.sigmoid(pre)
    return sig * (1.0 + pre * (1.0 - sig))


def norm_back(grads, vhat, table, totals, inv_count, member, gain):
    inv_n = wide(inv_count, totals.shape[-1])
    along = by_frame(totals[0:4] * inv_n, member)
    offset = by_frame(totals[4:8] * inv_n, member)
    factor = by_frame(table[4:8], member) * gain[None]
    return factor * (grads - offset - vhat * along)


def param_grads(totals):
    return jnp.concatenate(
        [jnp.sum(totals[0:4], axis=0, keepdims=True), jnp.sum(totals[4:8], axis=0, keepdims=True)], axis=0
    )


def rows_down(value):
    cube = f3(value)
    return f2(jnp.concatenate([jnp.zeros((FR, QP, cube.shape[-1]), F32), cube[:, : PX - QP]], axis=1))


def rows_up(value):
    cube = f3(value)
    return f2(jnp.concatenate([cube[:, QP:], jnp.zeros((FR, QP, cube.shape[-1]), F32)], axis=1))


def cols_right(value, first):
    return jnp.where(first, 0.0, pltpu.roll(value, 1, 0))


def cols_left(value, last):
    return jnp.where(last, 0.0, pltpu.roll(value, NP - 1, 0))


def edge_cols():
    at = lax.broadcasted_iota(jnp.int32, (NP, LB), 0) & 7
    return at == 0, at == 7


def block(ref, index, size):
    if len(ref.shape) == 2:
        return ref[pl.ds(pl.multiple_of(index * size, size), size), :]
    step = size // ref.shape[1]
    return ref[pl.ds(index * step, step)].reshape(size, ref.shape[-1])


def matrix(ref):
    value = ref[...]
    return value if len(value.shape) == 2 else value.reshape(-1, value.shape[-1])


def lanes_of(index, size):
    return pl.ds(pl.multiple_of(index * size, size), size)


def sums_all(ref):
    count = ref.shape[0] // NB
    out = []
    for j in range(NB):
        total = ref[j]
        for d in range(1, count):
            total = total + ref[NB * d + j]
        out.append(total)
    return out


def sums_dp(ref):
    total = ref[0]
    for d in range(1, ref.shape[0]):
        total = total + ref[d]
    return total


def spread(ref, value):
    for d in range(ref.shape[0]):
        ref[d] = value


def pair_products(low, weight, q, size):
    both = dot_nt(low, block(weight, q >> 1, 2 * size))
    odd = (q & 1) == 1
    first, second = both[:, :size], both[:, size:]
    return jnp.where(odd, second, first), jnp.where(odd, first, second)


def products(low, weight, q, size, own, others):
    refs = dict(others)
    own[...], near = pair_products(low, weight, q, size)
    refs[1][...] = near.astype(BF)
    far, both = pair_products(low, weight, q ^ 2, size)
    refs[2][...] = far.astype(BF)
    refs[3][...] = both.astype(BF)


def by_x_first(value, count):
    if count != 8:
        return value
    rows = value.shape[0] // 8
    return jnp.concatenate(
        [value[(2 * z + x) * rows : (2 * z + x + 1) * rows] for x in range(2) for z in range(4)], axis=0
    )


def emit(info, full, outs, first=0):
    if len(outs) == 1:
        outs[0][...] = full[...].astype(BF)
        return
    away, kept = outs
    rows = full.shape[0] // 8
    here = info[25]
    to = slice(first, first + rows)
    for k in range(4):
        target = here ^ (2 * k)
        kept[k, to] = full[pl.ds(pl.multiple_of(target * rows, rows), rows), :].astype(BF)
        away[k, to] = full[pl.ds(pl.multiple_of((target ^ 1) * rows, rows), rows), :].astype(BF)


def natural_index(axis):
    shape = (4 * PX, 256) if axis == 0 else (256, 4 * PX)
    at = lax.broadcasted_iota(jnp.int32, shape, axis)
    plane = (
        (at >= PX).astype(jnp.int32) + (at >= 2 * PX).astype(jnp.int32) + (at >= 3 * PX).astype(jnp.int32)
    )
    inner = at - PX * plane
    row = (inner >> 3) * 2 + (plane >> 1)
    col = (inner & 7) * 2 + (plane & 1)
    return row, col, lax.broadcasted_iota(jnp.int32, shape, 1 - axis)


def k_prep(info, feat, xm, xs, small):
    row, col, source = natural_index(0)
    hit = source == row * 16 + col
    for pair in range(FR // 2):
        picked = []
        for frame in (2 * pair, 2 * pair + 1):
            side = info[1 + frame]
            period = jnp.where(side > 8, 16, 8)
            inside = ((row & (period - 1)) < side) & ((col & (period - 1)) < side)
            select = jnp.where(hit & inside, 1.0, 0.0).astype(BF)
            picked.append(dot_nn(select, feat[frame]))
        for p in range(4):
            both = jnp.concatenate([x[p * PX : (p + 1) * PX] for x in picked], axis=0)
            xm[p, pair * 2 * PX : (pair + 1) * 2 * PX, :] = both.astype(BF)
    xs[...] = xm[...]
    small[...] = xm[0]


def k_first(info, xm, rat, *refs):
    q = info[0]
    own, near, far = refs[-3:] if len(refs) == 3 else refs[4:7]
    if len(refs) > 3:
        for k in range(4):
            refs[7][k] = refs[k][...]
        refs[7].send()
    for p in range(4):
        x = xm[p]
        own[p], one = pair_products(x, rat, q, LB)
        near[0, p] = one.astype(BF)
        far[p], three = pair_products(x, rat, q ^ 2, LB)
        near[1, p] = three.astype(BF)


def k_stat_first(info, own, near, far, zb, st):
    member = member_of(info)
    sums = None
    squares = None
    for p in range(4):
        low = (own[p] + near[0, p].astype(F32) + far[p].astype(F32)).astype(BF)
        zb[p] = low
        z = low.astype(F32)
        a, b = sum_px(z), sum_px(z * z)
        sums = a if sums is None else sums + a
        squares = b if squares is None else squares + b
    spread(st, jnp.concatenate([by_subnet(sums, member), by_subnet(squares, member)], axis=0))


def k_down(info, st, zb, prm, sa, counts, own, s1, s2, s3, im, vh, table, inv_count, stats):
    q = info[0]
    member = member_of(info)
    totals = sums_all(st)
    pixels = jnp.sum(counts[...].astype(F32), axis=0, keepdims=True)
    lane = lax.broadcasted_iota(jnp.int32, (1, LB), 1)
    for s in range(8):
        here = jnp.sum(jnp.where(lane == s, pixels, 0.0), axis=1, keepdims=True)
        inv_count[s : s + 1, :] = jnp.broadcast_to(1.0 / here, (1, LB))
    inv16 = inv_count[0:4, :]
    for j in range(NB):
        table[j], stats[j] = stat_table(totals[j][0:8], inv16)
    stats.send()
    tab = table[q]
    kept = keep_of(info, q)
    par = prm[0, q]
    first, _ = edge_cols()
    planes = []
    for p in range(4):
        vhat = centre(zb[p].astype(F32), tab, member)
        vh[p] = f2(vhat).astype(BF)
        planes.append(f2(silu(affine(vhat, par)) * f3(plane_mask(info, p)) * kept))
    vh.send()
    for t in range(3):
        for u in range(3):
            x = planes[(0 if t == 1 else 2) + (0 if u == 1 else 1)]
            if t == 0:
                x = rows_down(x)
            if u == 0:
                x = cols_right(x, first)
            at = (3 * t + u) * LB
            im[:, at : at + LB] = x.astype(BF)
    im.send()
    products(im[...], sa, q, LB, own, ((1, s1), (2, s2), (3, s3)))


def k_stat(info, own, r1, r2, r3, zb, st):
    member = member_of(info)
    low = (own[...] + r1[...].astype(F32) + r2[...].astype(F32) + r3[...].astype(F32)).astype(BF)
    zb[...] = low
    z = low.astype(F32)
    zm = z * half_mask(info)
    total = jnp.concatenate([by_subnet(sum_px(zm), member), by_subnet(sum_px(zm * z), member)], axis=0)
    spread(st, total)


def act_all(info, st, blocks, prm, norm, inv8, act, vh, table, stats):
    q = info[0]
    member = member_of(info)
    totals = sums_all(st)
    for j in range(NB):
        table[j], stats[j] = stat_table(totals[j], inv8)
    stats.send()
    m = f3(half_mask(info))
    for k in range(NB):
        j = q ^ k
        vhat = centre(blocks[k][...].astype(F32), table[j], member)
        vh[:, lanes_of(j, LB)] = f2(vhat).astype(BF)
        a = silu(affine(vhat, prm[norm, j])) * m * keep_of(info, j)
        act[:, lanes_of(j, LB)] = f2(a).astype(BF)
    vh.send()
    act.send()


def two_sums(z, member):
    return jnp.concatenate([by_subnet(sum_px(z), member), by_subnet(sum_px(z * z), member)], axis=0)


def k_proj(info, x0, x1, x2, x3, sc, st, every, zp):
    q = info[0]
    for k, ref in enumerate((x0, x1, x2, x3)):
        every[:, lanes_of(q ^ k, 256)] = ref[...]
    every.send()
    z = dot_nn(every[...], matrix(sc))
    zp[...] = z.astype(BF)
    zp.send()
    st[...] = two_sums(z, member_of(info))


def k_expand_a(info, st, b0, b1, b2, b3, stp, stx, prm, inv_count, ea, z3, st3, act, vh, table, stats, hold):
    act_all(info, st, (b0, b1, b2, b3), prm, 1, inv_count[4:8], act, vh, table, stats)
    z = dot_nn(act[...], matrix(ea))
    z3[...] = z
    hold[...] = stp[...] + stx[...]
    half = hold.shape[1] // 2
    part = hold[:, lanes_of(info[25] & 1, half)]
    spread(st3, jnp.concatenate([two_sums(z, member_of(info)), part], axis=1))


def k_join(info, st3, z3, zp, prm, inv_count, rbt, own, s1, s2, s3, low_a, sl, vh3, vhp, tab3, tabp, stat3, statp):
    q = info[0]
    member = member_of(info)
    inv8 = inv_count[4:8]
    lanes = z3.shape[1]
    even, odd = st3[0], st3[1]
    for d in range(2, st3.shape[0], 2):
        even = even + st3[d]
        odd = odd + st3[d + 1]
    tab3[...], stat3[...] = stat_table(even[:, :lanes] + odd[:, :lanes], inv8)
    tabp[...], statp[...] = stat_table(jnp.concatenate([even[:, lanes:], odd[:, lanes:]], axis=1), inv8)
    stat3.send()
    statp.send()
    va = centre(z3[...], tab3[...], member)
    vb = centre(zp[...].astype(F32), tabp[...], member)
    vh3[...] = f2(va).astype(BF)
    vhp[...] = f2(vb).astype(BF)
    vh3.send()
    vhp.send()
    pre = affine(va, prm[0]) + affine(vb, prm[1])
    m = wide(f3(half_mask(info)), pre.shape[-1])
    sig = jax.nn.sigmoid(pre)
    low = f2(pre * sig * m).astype(BF)
    low_a[...] = low
    low_a.send()
    sl[...] = f2(m * (sig * (1.0 + pre * (1.0 - sig)))).astype(BF)
    sl.send()
    products(low, rbt, q, LB, own, ((1, s1), (2, s2), (3, s3)))


def k_flat(info, st, zb, prm, inv_count, sb, own, s1, s2, s3, im, vh, table, stats):
    q = info[0]
    member = member_of(info)
    totals = sums_all(st)
    inv8 = inv_count[4:8]
    for j in range(NB):
        table[j], stats[j] = stat_table(totals[j], inv8)
    stats.send()
    vhat = centre(zb[...].astype(F32), table[q], member)
    vh[...] = f2(vhat).astype(BF)
    vh.send()
    act = f2(silu(affine(vhat, prm[2, q])) * f3(half_mask(info)) * keep_of(info, q))
    first, last = edge_cols()
    for t in range(3):
        shifted = rows_down(act) if t == 0 else (act if t == 1 else rows_up(act))
        for u in range(3):
            x = cols_right(shifted, first) if u == 0 else (shifted if u == 1 else cols_left(shifted, last))
            at = (3 * t + u) * LB
            im[:, at : at + LB] = x.astype(BF)
    im.send()
    products(im[...], sb, q, LB, own, ((1, s1), (2, s2), (3, s3)))


def k_expand_b(info, st, b0, b1, b2, b3, prm, inv_count, eb, z6, st6, act, vh, table, stats):
    act_all(info, st, (b0, b1, b2, b3), prm, 3, inv_count[4:8], act, vh, table, stats)
    z = dot_nn(act[...], matrix(eb))
    z6[...] = z
    spread(st6, two_sums(z, member_of(info)))


def k_output(info, st6, z6, low_a, cot, prm, inv_count, gb, vh6, st, output, gbs, tab6, stat6):
    member = member_of(info)
    tab6[...], stat6[...] = stat_table(sums_dp(st6), inv_count[4:8])
    stat6.send()
    vhat = centre(z6[...], tab6[...], member)
    vh6[...] = f2(vhat).astype(BF)
    pre = affine(vhat, prm[2]) + f3(low_a[...].astype(F32))
    m = wide(f3(half_mask(info)), pre.shape[-1])
    sig = jax.nn.sigmoid(pre)
    output[:, 0:PX, :] = pre * sig * m
    output[:, PX:, :] = jnp.zeros((FR, 64 - PX, pre.shape[-1]), F32)
    output.send()
    g = cot[...].astype(F32)[:, 0:PX, :] * m * (sig * (1.0 + pre * (1.0 - sig)))
    gb[...] = f2(g)
    gbs[...] = f2(g).astype(BF)
    gbs.send()
    along = by_subnet(jnp.sum(g * vhat, axis=1), member)
    offset = by_subnet(jnp.sum(g, axis=1), member)
    spread(st, jnp.concatenate([along, offset], axis=0))


def k_back_six(info, st, gb, vh6, tab6, prm, inv_count, eb, act5, own, s1, s2, s3, pg, grad):
    q = info[0]
    member = member_of(info)
    totals = sums_dp(st)
    pg[...] = param_grads(totals)
    pg.send()
    vhat = f3(vh6[...].astype(F32))
    m = wide(f3(half_mask(info)), vhat.shape[-1])
    g = m * norm_back(f3(gb[...]), vhat, tab6[...], totals, inv_count[4:8], member, prm[2, 0:1])
    low = f2(g).astype(BF)
    products(low, eb, q, LB, own, ((1, s1), (2, s2), (3, s3)))
    grad[...] = by_x_first(dot_tn(act5[...], low), st.shape[0]).astype(BF)


def back_stat(g, vhat, member, gl, st):
    low = f2(g).astype(BF)
    gl[...] = low
    g = f3(low.astype(F32))
    along = by_subnet(jnp.sum(g * vhat, axis=1), member)
    offset = by_subnet(jnp.sum(g, axis=1), member)
    spread(st, jnp.concatenate([along, offset], axis=0))


def k_back_stat(norm):
    def body(info, own, r1, r2, r3, vh, prm, gl, st):
        q = info[0]
        part = own[...] + r1[...].astype(F32) + r2[...].astype(F32) + r3[...].astype(F32)
        vhat = f3(vh[...].astype(F32))
        g = f3(part * half_mask(info)) * keep_of(info, q) * slope(affine(vhat, prm[norm, q]))
        back_stat(g, vhat, member_of(info), gl, st)

    return body


def gz_all(info, st, grads, values, table, prm, norm, inv8, gz, pg, hold):
    q = info[0]
    member = member_of(info)
    totals = sums_all(st)
    for j in range(NB):
        pg[j] = param_grads(totals[j])
        hold[j] = totals[j]
    pg.send()
    m = f3(half_mask(info))
    for k in range(NB):
        j = q ^ k
        vhat = f3(values(k, j).astype(F32))
        g = norm_back(f3(grads[k][...].astype(F32)), vhat, table[j], hold[j], inv8, member, prm[norm, j][0:1])
        gz[:, lanes_of(j, LB)] = f2(m * g).astype(BF)


def k_back_five(info, st, g0, g1, g2, g3, vh5, tab5, prm, inv_count, sb, vh4, im4, gl, st4, pg, grad, gz5, hold):
    q = info[0]
    gz_all(
        info, st, (g0, g1, g2, g3), lambda k, j: vh5[:, lanes_of(j, LB)], tab5, prm, 3, inv_count[4:8],
        gz5, pg, hold,
    )
    terms = dot_nn(gz5[...], sb[...])
    first, last = edge_cols()
    total = None
    for t in range(3):
        for u in range(3):
            at = (3 * t + u) * LB
            x = terms[:, at : at + LB]
            x = cols_left(x, last) if u == 0 else (x if u == 1 else cols_right(x, first))
            x = rows_up(x) if t == 0 else (x if t == 1 else rows_down(x))
            total = x if total is None else total + x
    vhat = f3(vh4[...].astype(F32))
    g = f3(total * half_mask(info)) * keep_of(info, q) * slope(affine(vhat, prm[2, q]))
    back_stat(g, vhat, member_of(info), gl, st4)
    grad[...] = by_x_first(dot_tn(gz5[...], im4[...]), st.shape[0] // NB).astype(BF)


def k_back_four(info, st, g0, g1, g2, g3, v0, v1, v2, v3, tab4, prm, inv_count, rbt, gb, sl, vh3, vhp, low_a, ga, st3, pg, grad, gz4, hold):
    member = member_of(info)
    values = (v0, v1, v2, v3)
    gz_all(
        info, st, (g0, g1, g2, g3), lambda k, j: values[k][...], tab4, prm, 2, inv_count[4:8], gz4, pg, hold
    )
    low = gz4[...]
    back = dot_nn(low, matrix(rbt))
    g = (gb[...].astype(F32) + back) * sl[...].astype(F32)
    ga[...] = g
    g = f3(g)
    along = by_subnet(jnp.sum(g * f3(vh3[...].astype(F32)), axis=1), member)
    other = by_subnet(jnp.sum(g * f3(vhp[...].astype(F32)), axis=1), member)
    offset = by_subnet(jnp.sum(g, axis=1), member)
    half = offset.shape[-1] // 2
    tail = jnp.concatenate([offset[:, :half], offset[:, half:]], axis=0)
    spread(st3, jnp.concatenate([jnp.concatenate([along, other], axis=0), tail], axis=1))
    grad[...] = dot_tn(low, low_a[...]).astype(BF)


def add_hop(kept, away, sums):
    for k in range(4):
        total = kept[k].astype(F32) + away[k].astype(F32)
        sums[k][...] = total if k == 0 else total.astype(BF)
        sums[k].send()


def line_sum(parts):
    total = parts[0][...]
    for part in parts[1:]:
        total = total + part[...].astype(F32)
    return total


def taps_apart(ref, value):
    for tap in range(9):
        ref[tap] = value[:, tap * LB : (tap + 1) * LB]
    ref.send()


def emit_line(info, full, outs, first, part=0, parts=1):
    kept, away = outs
    rows = kept.shape[1]
    here = info[25] & 1
    lanes = full.shape[1]
    for z in range(4):
        for ref, x in ((kept, here), (away, here ^ 1)):
            at = ((2 * z + x) * parts + part) * rows
            ref[z, :, first : first + lanes] = full[pl.ds(pl.multiple_of(at, rows), rows), :].astype(BF)


def k_back_join(info, st, ga, vh3, vhp, tab3, tabp, prm, inv_count, ea, act2, every, grad_r, *refs):
    q = info[0]
    member = member_of(info)
    own, s1, s2, s3, gzp, pg3, pgp, *grads, full_a, full_s = refs
    totals = sums_dp(st)
    lanes = ga.shape[-1]
    tail = totals[:, lanes:]
    offset = jnp.concatenate([tail[0:4], tail[4:8]], axis=1)
    tot3 = jnp.concatenate([totals[0:4, :lanes], offset], axis=0)
    totp = jnp.concatenate([totals[4:8, :lanes], offset], axis=0)
    pg3[...] = param_grads(tot3)
    pgp[...] = param_grads(totp)
    pg3.send()
    pgp.send()
    inv8 = inv_count[4:8]
    g = f3(ga[...])
    m = wide(f3(half_mask(info)), lanes)
    low = f2(m * norm_back(g, f3(vh3[...].astype(F32)), tab3[...], tot3, inv8, member, prm[0, 0:1])).astype(BF)
    products(low, ea, q, LB, own, ((1, s1), (2, s2), (3, s3)))
    lowp = f2(m * norm_back(g, f3(vhp[...].astype(F32)), tabp[...], totp, inv8, member, prm[1, 0:1])).astype(BF)
    gzp[...] = lowp
    full_a[...] = dot_tn(act2[...], low)
    full_s[...] = dot_tn(every[...], lowp)
    if len(grads) == 2:
        emit_line(info, grad_r, grads, 0)
        emit_line(info, full_a, grads, lanes)
        for part in range(2):
            emit_line(info, full_s, grads, (2 + part) * lanes, part, 2)
        return
    grad = grads[0]
    count = st.shape[0]
    rows = full_s.shape[0] // count // 2
    grad[:, 0:lanes] = grad_r[...]
    grad[:, lanes : 2 * lanes] = full_a[...].astype(BF)
    for part in range(2):
        picked = [full_s[(2 * d + part) * rows : (2 * d + part + 1) * rows, :] for d in range(count)]
        at = (2 + part) * lanes
        grad[:, at : at + lanes] = jnp.concatenate(picked, axis=0).astype(BF)


def k_back_small(info, gzp, sc, own, s1, s2, s3):
    q = info[0]
    low = gzp[...]
    products(low, sc, q, 256, own, ((1, s1), (2, s2), (3, s3)))


def k_back_two(info, st, g0, g1, g2, g3, vh2, tab2, prm, inv_count, sa, vh1, im1, *refs):
    q = info[0]
    member = member_of(info)
    refs, (gz2, hold, full) = refs[:-3], refs[-3:]
    if len(refs) > 5:
        rows = refs[0].shape[1]
        for z in range(4):
            refs[6][z * rows : (z + 1) * rows, :] = (refs[0][z].astype(F32) + refs[1][z].astype(F32)).astype(BF)
        refs[6].send()
        (gl, st1, pg, saved), grads = refs[2:6], refs[7:]
    else:
        (gl, st1, pg, saved), grads = refs[0:4], refs[4:]
    gz_all(
        info, st, (g0, g1, g2, g3), lambda k, j: vh2[:, lanes_of(j, LB)], tab2, prm, 1, inv_count[4:8],
        gz2, pg, hold,
    )
    terms = dot_nn(gz2[...], sa[...])
    _, last = edge_cols()
    y = [terms[:, tap * LB : (tap + 1) * LB] for tap in range(9)]
    planes = [
        y[4],
        cols_left(y[3], last) + y[5],
        rows_up(y[1]) + y[7],
        rows_up(cols_left(y[0], last) + y[2]) + cols_left(y[6], last) + y[8],
    ]
    kept = keep_of(info, q)
    along = None
    offset = None
    for p in range(4):
        vhat = f3(vh1[p].astype(F32))
        g = f3(planes[p] * plane_mask(info, p)) * kept * slope(affine(vhat, prm[0, q]))
        low = f2(g).astype(BF)
        gl[p] = low
        saved[p] = low
        g = f3(low.astype(F32))
        a, b = jnp.sum(g * vhat, axis=1), jnp.sum(g, axis=1)
        along = a if along is None else along + a
        offset = b if offset is None else offset + b
    saved.send()
    spread(st1, jnp.concatenate([by_subnet(along, member), by_subnet(offset, member)], axis=0))
    full[...] = dot_tn(gz2[...], im1[...])
    emit(info, full, grads)


def k_last(info, st, g0, g1, g2, g3, v0, v1, v2, v3, tab1, prm, inv_count, xm, *refs):
    q = info[0]
    member = member_of(info)
    gz1, pg, grad, hold = refs
    totals = sums_all(st)
    inv16 = inv_count[0:4]
    for j in range(NB):
        pg[j] = param_grads(totals[j])
        hold[j] = totals[j]
    pg.send()
    total = None
    for p in range(4):
        m = f3(plane_mask(info, p))
        for k, (gref, vref) in enumerate(((g0, v0), (g1, v1), (g2, v2), (g3, v3))):
            j = q ^ k
            vhat = f3(vref[p].astype(F32))
            g = norm_back(f3(gref[p].astype(F32)), vhat, tab1[j], hold[j], inv16, member, prm[0, j][0:1])
            gz1[p, :, lanes_of(j, LB)] = f2(m * g).astype(BF)
        term = dot_tn(gz1[p], xm[p])
        total = term if total is None else total + term
    grad[...] = total.astype(BF)


def k_features(info, gz1, rat, own, r1, r2, r3, gf, nat):
    for p in range(4):
        back = dot_nn(gz1[p], rat[...])
        if p == 0:
            back = back + own[...] + r1[...].astype(F32) + r2[...].astype(F32) + r3[...].astype(F32)
        back = back * wide(plane_mask(info, p), back.shape[-1])
        high = back.astype(BF)
        nat[0, p] = high.astype(F32)
        nat[1, p] = back - high.astype(F32)
    row, col, target = natural_index(1)
    select = jnp.where(target == row * 16 + col, 1.0, 0.0).astype(BF)
    for frame in range(FR):
        out = None
        for part in range(2):
            x = jnp.concatenate(
                [nat[part, p, frame * PX : (frame + 1) * PX, :] for p in range(4)], axis=0
            ).astype(BF)
            y = dot_nn(select, x)
            out = y if out is None else out + y
        gf[frame] = out


def k_tables(info, *refs):
    mids, pairs, outs, gains = refs[0:4], refs[4:8], refs[8:11], refs[11:14]
    stats_mid, grads_mid, stats_out, grads_out = refs[14:]
    for i in range(4):
        for j in range(NB):
            at = slice(j * LB, (j + 1) * LB)
            stats_mid[i, 0, :, at] = mids[i][j, 0:4]
            stats_mid[i, 1, :, at] = mids[i][j, 4:8]
            grads_mid[i, :, at] = pairs[i][j]
    for i in range(3):
        stats_out[i, 0] = outs[i][0:4]
        stats_out[i, 1] = outs[i][4:8]
        grads_out[i] = gains[i][...]


def k_end_grads(info, early, grad, spatial, expand, reduce, other, shortcut):
    value = early[...].astype(F32)
    taps_apart(spatial, value)
    expand[...] = value[:, TAPS:]
    value = grad[...].astype(F32)
    lanes = expand.shape[-1]
    reduce[...] = value[:, :lanes]
    other[...] = value[:, lanes : 2 * lanes]
    shortcut[...] = jnp.concatenate([value[:, 2 * lanes : 3 * lanes], value[:, 3 * lanes :]], axis=0)


def k_hop(info, kept, away, *sums):
    add_hop(kept, away, sums)


def k_final(info, *refs):
    parts, others, spatial, reduce = refs[:-3], refs[-3], refs[-2], refs[-1]
    taps_apart(spatial, line_sum(parts))
    total = others[0].astype(F32)
    for d in range(1, others.shape[0]):
        total = total + others[d].astype(F32)
    reduce[...] = total


def swap(value, k):
    return lax.ppermute(value, "chan", [(i, i ^ k) for i in range(NB)])


def partners(value):
    return [value] + [swap(value, k) for k in (1, 2, 3)]


def partners_two_hops(value):
    far = swap(value, 2)
    return [value, swap(value, 1), far, swap(far, 1)]


def everywhere(value):
    return lax.all_to_all(value, ("dp", "chan"), 0, 0, tiled=True)


def along_dp(value):
    return lax.all_to_all(value, "dp", 0, 0, tiled=True)


def after(value, *others):
    return lax.optimization_barrier((value,) + others)[0]


def swap_dp(value, k):
    return lax.ppermute(value, "dp", [(i, i ^ k) for i in range(lax.axis_size("dp"))])


def along_z(value):
    return [value] + [swap_dp(value, 2 * k) for k in (1, 2, 3)]


def across_x(line, *others):
    return line + [swap_dp(after(v, *others), 1) for v in line]


def add_near(kept, away):
    return [(kept[k].astype(F32) + away[k].astype(F32)).astype(F32 if k == 0 else BF) for k in range(4)]


def add_far(parts):
    return parts[0] + parts[1].astype(F32) + parts[2].astype(F32) + parts[3].astype(F32)


def reduce_pairs(value):
    if lax.axis_size("dp") != 8:
        return lax.psum_scatter(value, "dp", scatter_dimension=0, tiled=True)
    groups = [[2 * z, 2 * z + 1] for z in range(4)]
    return lax.psum_scatter(value, "dp", scatter_dimension=0, tiled=True, axis_index_groups=groups)


def reduce_lines(value):
    if lax.axis_size("dp") != 8:
        return value
    groups = [[2 * z + x for z in range(4)] for x in range(2)]
    return lax.psum_scatter(value, "dp", scatter_dimension=0, tiled=True, axis_index_groups=groups)


def shards(
    features,
    cotangent,
    reduce_a,
    spatial_a,
    expand_a,
    shortcut,
    reduce_b,
    spatial_b,
    expand_b,
    norms_mid,
    norms_out,
    crop_side,
    subnet_of,
    width_of,
):
    ndp = lax.axis_size("dp")
    nall = ndp * NB
    hops = ndp == 8
    hidden = norms_mid.shape[-1]
    cin = features.shape[-1]
    cout = cotangent.shape[-1]
    rows = reduce_a.shape[1]
    er = expand_a.shape[0]
    sr = shortcut.shape[0]
    position = lax.axis_index("chan").astype(jnp.int32)
    place = lax.axis_index("dp").astype(jnp.int32)
    width = jnp.sum(
        jnp.where(subnet_of[:, None] == jnp.arange(4, dtype=jnp.int32)[None, :], width_of[None, :], 0), axis=1
    )
    info = jnp.concatenate([position[None], crop_side, subnet_of, width, place[None]])

    ra_t = reduce_a.T
    sa_t = jnp.transpose(spatial_a, (2, 0, 1)).reshape(rows, TAPS)
    half = (crop_side + 1) // 2
    per16 = jnp.where(crop_side > 8, crop_side * crop_side, 4 * crop_side * crop_side)
    per8 = jnp.where(half > 4, half * half, 4 * half * half)
    lane = jnp.arange(LB, dtype=jnp.int32)[None, :]
    pixels = jnp.where(lane == subnet_of[:, None], per16[:, None], 0)
    pixels = pixels + jnp.where(lane == subnet_of[:, None] + 4, per8[:, None], 0)
    pixels = jnp.concatenate([pixels.astype(F32), jnp.zeros((rows, LB), F32)], axis=0)[: max(rows, FR)]
    prm, prm_out, inv_count = Held("prm"), Held("prm_out"), Held("inv")
    tab1, tab2, tab4, tab5 = [Held("tab", i) for i in range(4)]
    tab3, tabp, tab6 = [Held("tab_out", i) for i in range(3)]
    slots = [
        jnp.transpose(x.reshape(-1, 2, NB, LB), (0, 2, 1, 3)).reshape(-1, 2, LB) for x in (norms_mid, norms_out)
    ]
    slots = [jnp.pad(x, ((0, 0), (0, 6), (0, 0))) for x in slots]
    blank = jnp.zeros((SLOTS, 8, LB), F32)
    state = jnp.concatenate([slots[0], blank[:1], slots[1], blank[TAB:]], axis=0)
    table = ((NB, 8, LB), F32, "hbm")
    one_block = ((NP, LB), F32)
    send = ((NP, LB), BF)
    sends = [one_block, send, send, send]
    stat_all = ((nall, 8, LB), F32)
    stat_own = ((ndp, 8, cout), F32)
    stat_wide = ((ndp, 8, cout + cout // 2), F32)
    map_out = ((NP, cout), F32)
    low_out = ((NP, cout), BF, "hbm")
    low_mid = ((NP, hidden), BF, "hbm")
    tab_out = ((8, cout), F32, "hbm")

    if hops:
        line_ra = along_z(ra_t)
        line_sa = along_z(after(jnp.concatenate([sa_t, pixels.astype(BF)], axis=1), line_ra[1]))
        pieces = across_x(line_ra, *line_ra[1:])
        feat = after(features.reshape(FR, 256, cin), pieces[4])
        rat = Gathered(pieces, rows, 0, cin)
    else:
        rat = Pinned(lax.all_gather(ra_t, "dp", axis=0, tiled=True))
        sa = Pinned(lax.all_gather(sa_t, "dp", axis=0, tiled=True))
        counts = Pinned(lax.psum(pixels, "dp"))
        feat = features.reshape(FR, 256, cin)
    xm, xs, small = call(
        k_prep, [((4, NP, cin), BF), ((4, NP, cin), BF, "hbm"), ((NP, cin), BF)],
        info, Pinned(feat), name="prep",
    )
    pack_mid = jnp.concatenate([expand_a, shortcut, after(reduce_b, small).T], axis=0)
    pack_end = jnp.concatenate(
        [jnp.transpose(after(spatial_b, small), (2, 0, 1)).reshape(rows, TAPS), expand_b], axis=1
    )
    own, near, far, *stacked = call(
        k_first,
        [((4, NP, LB), F32), ((2, 4, NP, LB), BF), ((4, NP, LB), F32)]
        + ([((4, rows, TAPS + LB), BF, "hbm")] if hops else []),
        info, after(xm, pack_mid, pack_end), rat, *(line_sa if hops else []), name="first",
    )
    if hops:
        sa_pieces = [stacked[0], swap_dp(stacked[0], 1)]
        sa = Gathered(sa_pieces, rows, 0, TAPS)
        counts = Gathered(sa_pieces, 16, TAPS, LB)
    near = swap(near, 1)
    far = (far + near[1].astype(F32)).astype(BF)
    mid = lax.all_gather(after(pack_mid, own), "dp", axis=0)

    def mid_rows(first, size):
        if size % 16 == 0:
            return Pinned(mid, lambda ref, info: ref.at[:, first : first + size, :], (ndp, size, cout))
        return Pinned(mid[:, first : first + size].reshape(ndp * size, cout))

    ea = mid_rows(0, er)
    sc = mid_rows(er, sr)
    rbt = mid_rows(er + sr, rows)
    end = lax.all_gather(pack_end, "dp", axis=0, tiled=True)
    sb = Pinned(end, lambda ref, info: ref.at[:, 0:TAPS], (hidden, TAPS))
    eb = Pinned(end, lambda ref, info: ref.at[:, TAPS : TAPS + cout], (hidden, cout))

    far = swap(far, 2)
    zb1, st = call(
        k_stat_first, [((4, NP, LB), BF), stat_all], info, own, near, far, name="stat_one"
    )
    smalls = partners_two_hops(after(small, st))
    st = after(everywhere(st), *smalls[1:])
    own, s1, s2, s3, im1, vh1, stat1, state = call(
        k_down,
        sends + [((NP, TAPS), BF, "hbm"), ((4, NP, LB), BF, "hbm"), tab1, inv_count, table],
        info, st, zb1, prm, sa, counts, state=state, name="down",
    )
    zb, st = call(k_stat, [send, stat_all], info, own, swap(s1, 1), swap(s2, 2), swap(s3, 3), name="stat_two")
    zs = partners(zb)
    smalls = lax.optimization_barrier(tuple(smalls) + (st,))[:4]
    stp, every, zp = call(
        k_proj, [((8, cout), F32), ((NP, NB * cin), BF, "hbm"), low_out], info, *smalls, sc, name="proj"
    )
    st = after(everywhere(st), stp)
    stx = swap_dp(stp, 1)
    z3, st3, act2, vh2, stat2, state = call(
        k_expand_a, [map_out, stat_wide, low_mid, low_mid, tab2, table],
        info, st, *zs, stp, stx, prm, inv_count, ea, scratch=[pltpu.VMEM((8, cout), F32)], state=state, name="expand_a",
    )
    st3 = along_dp(st3)
    own, s1, s2, s3, low_a, sl, vh3, vhp, stat3, statp, state = call(
        k_join, sends + [low_out, low_out, low_out, low_out, tab3, tabp, tab_out, tab_out],
        info, st3, z3, Pinned(zp), prm_out, inv_count, rbt, state=state, name="join",
    )
    zb, st = call(k_stat, [send, stat_all], info, own, swap(s1, 1), swap(s2, 2), swap(s3, 3), name="stat_four")
    st = everywhere(st)
    own, s1, s2, s3, im4, vh4, stat4, state = call(
        k_flat, sends + [((NP, TAPS), BF, "hbm"), ((NP, LB), BF, "hbm"), tab4, table],
        info, st, zb, prm, inv_count, sb, state=state, name="flat",
    )
    zb, st = call(k_stat, [send, stat_all], info, own, swap(s1, 1), swap(s2, 2), swap(s3, 3), name="stat_five")
    zs = partners(zb)
    st = everywhere(st)
    z6, st6, act5, vh5, stat5, state = call(
        k_expand_b, [map_out, stat_own, low_mid, low_mid, tab5, table],
        info, st, *zs, prm, inv_count, eb, state=state, name="expand_b",
    )
    vhs4 = partners(after(vh4, st6))
    st6 = after(along_dp(st6), *vhs4[1:])
    gb, vh6, st, output, gbs, stat6, state = call(
        k_output,
        [map_out, ((NP, cout), BF), stat_own, ((FR, 64, cout), F32, "hbm"), low_out, tab6, tab_out],
        info, st6, z6, Pinned(low_a), Pinned(cotangent.reshape(FR, 64, cout)), prm_out, inv_count, state=state, name="output",
    )

    def early(first, size):
        return ((hidden, TAPS + cout), BF, "hbm", lambda ref: ref.at[:, first : first + size], (hidden, size))

    def summed(size, lanes):
        return [((size, lanes), F32, "hbm")] + [((size, lanes), BF, "hbm")] * 3

    def z_parts(sums):
        return [sums[0]] + [swap_dp(sums[k], 2 * k) for k in (1, 2, 3)]

    def reduced(size, width_):
        if hops:
            return [((4, size, width_), BF, "hbm")] * 2
        return [((ndp * size, width_), BF, "hbm")]

    def own_lanes(array):
        return Pinned(array, lambda ref, info: ref.at[:, lanes_of(info[0], LB)], (NP, LB))

    vh1_in = after(vh1, st)
    vhs1 = [vh1, swap(vh1_in, 1), swap(vh1_in, 2)]
    st = after(along_dp(st), *vhs1[1:])
    own, s1, s2, s3, pg6, grad_early, state = call(
        k_back_six, sends + [((2, cout), F32, "hbm"), early(TAPS, cout)],
        info, st, gb, vh6, tab6, prm_out, inv_count, eb, Pinned(act5), state=state, name="back_six",
    )
    gl, st, state = call(
        k_back_stat(3), [send, stat_all],
        info, own, swap(s1, 1), swap(s2, 2), swap(s3, 3), own_lanes(vh5), prm, state=state, name="back_stat_five",
    )
    gs = partners(gl)
    st = everywhere(st)
    hold = pltpu.VMEM((NB, 8, LB), F32)
    pair_mid = ((NB, 2, LB), F32, "hbm")
    gl, st, pg5, grad_early, state = call(
        k_back_five, [send, stat_all, pair_mid, early(0, TAPS)],
        info, st, *gs, Pinned(vh5), tab5, prm, inv_count, sb, Pinned(vh4), Pinned(im4),
        scratch=[pltpu.VMEM((NP, hidden), BF), hold], alias=(grad_early, 3), state=state, name="back_five",
    )
    gs = partners(gl)
    grad_early = reduce_pairs(grad_early)
    st = everywhere(st)
    ga, st, pg4, grad_r, state = call(
        k_back_four, [map_out, stat_wide, pair_mid, ((hidden, cout), BF, "hbm")],
        info, st, *gs, *[Pinned(v) for v in vhs4], tab4, prm, inv_count, rbt, Pinned(gbs), Pinned(sl),
        Pinned(vh3), Pinned(vhp), Pinned(low_a),
        scratch=[pltpu.VMEM((NP, hidden), BF), hold], state=state, name="back_four",
    )
    vhs1.append(swap(after(vhs1[2], st), 1))
    st = after(along_dp(st), vhs1[3], grad_early)
    if hops:
        grads = [((4, rows, 4 * cout), BF, "hbm")] * 2
    else:
        grads = [((hidden, 4 * cout), BF, "hbm")]
    own, s1, s2, s3, gzp, pg3, pgp, *grads, state = call(
        k_back_join, sends + [((NP, cout), BF)] + [((2, cout), F32, "hbm")] * 2 + grads,
        info, st, ga, Pinned(vh3), Pinned(vhp), tab3, tabp, prm_out, inv_count, ea,
        Pinned(act2), Pinned(every), Pinned(grad_r),
        scratch=[pltpu.VMEM((hidden, cout), F32), pltpu.VMEM((ndp * sr, cout), F32)], state=state, name="back_join",
    )
    grad_early = reduce_lines(after(grad_early, grads[0]))
    extra_in, extra_out = [], []
    if hops:
        extra_in = [Pinned(grads[0]), swap_dp(grads[1], 1)]
        extra_out = [((4 * rows, 4 * cout), BF, "hbm")]
    else:
        end_grad = reduce_pairs(grads[0])
    r1, r2, r3 = swap(s1, 1), swap(s2, 2), swap(s3, 3)
    sown, *small_sends = call(
        k_back_small, [((NP, cin), F32)] + [((NP, cin), BF)] * 3,
        info, after(gzp, r1), sc, name="back_small",
    )
    own = after(own, sown)
    gl, st, state = call(
        k_back_stat(1), [send, stat_all],
        info, own, r1, r2, r3, own_lanes(vh2), prm, state=state, name="back_stat_two",
    )
    gs = partners(gl)
    st = everywhere(st)
    small_one = swap(small_sends[0], 1)
    st = after(st, grad_early, small_one)
    gl, st, pg2, saved, *grad_sa, state = call(
        k_back_two, [((4, NP, LB), BF), stat_all, pair_mid, ((4, NP, LB), BF, "hbm")] + extra_out + reduced(rows, TAPS),
        info, st, *gs, Pinned(vh2), tab2, prm, inv_count, sa, Pinned(vh1), Pinned(im1), *extra_in,
        scratch=[pltpu.VMEM((NP, hidden), BF), hold, pltpu.VMEM((hidden, TAPS), F32)], state=state, name="back_two",
    )
    gs = [gl, swap(gl, 1), swap(gl, 2)]
    st = everywhere(st)
    gs.append(swap(after(gs[2], st), 1))
    small_back = [small_one] + [swap(after(small_sends[k - 1], gs[3]), k) for k in (2, 3)]
    extra_in, extra_out = [], []
    if hops:
        end_grad = reduce_lines(grad_sa[0])
        kept, away = grad_sa[2], swap_dp(grad_sa[1], 1)
    gz1, pg1, grad_rat, _ = call(
        k_last, [((4, NP, hidden), BF), pair_mid, ((hidden, cin), BF, "hbm")],
        info, st, Pinned(saved), Pinned(gs[1]), Pinned(gs[2]), gs[3], *[Pinned(v) for v in vhs1], tab1, prm, inv_count,
        Pinned(xs), scratch=[hold], state=state, name="last",
    )
    if hops:
        sums_sa = call(k_hop, summed(rows, TAPS), info, Pinned(after(kept, gz1)), away, name="hop")
        parts_sa = z_parts(sums_sa)
        grad_rat = after(grad_rat, sums_sa[0])
    else:
        parts_sa = [lax.psum_scatter(grad_sa[0], "dp", scatter_dimension=0, tiled=True).astype(F32)]
    spatial, expand, reduce, grad_a, grad_s = call(
        k_end_grads,
        [
            ((9, rows, LB), F32, "hbm"), ((er, cout), F32, "hbm"), ((rows, cout), F32, "hbm"),
            ((er, cout), F32, "hbm"), ((sr, cout), F32, "hbm"),
        ],
        info, Pinned(grad_early), Pinned(end_grad), name="end_grads",
    )
    parts_ra = along_dp(grad_rat.reshape(ndp, rows, cin))
    stats_mid, grad_norms_mid, stats_out, grad_norms_out = call(
        k_tables,
        [
            ((4, 2, 4, hidden), F32, "hbm"), ((4, 2, hidden), F32, "hbm"),
            ((3, 2, 4, cout), F32, "hbm"), ((3, 2, cout), F32, "hbm"),
        ],
        info,
        *[Pinned(x) for x in (stat1, stat2, stat4, stat5, pg1, pg2, pg4, pg5, stat3, statp, stat6, pg3, pgp, pg6)],
        name="tables",
    )
    gf = call(
        k_features, [((FR, 256, cin), F32, "hbm")],
        info, gz1, rat, Pinned(sown), *small_back,
        scratch=[pltpu.VMEM((2, 4, NP, cin), F32)], name="features",
    )[0]
    spatial_sa, grad_rat = call(
        k_final, [((9, rows, LB), F32, "hbm"), ((rows, cin), F32, "hbm")],
        info, *[Pinned(after(x, gf, spatial)) for x in parts_sa[:1]], *[after(x, gf, spatial) for x in parts_sa[1:]],
        after(parts_ra, gf, spatial), name="final",
    )
    grad_reduce_a = grad_rat.T
    grad_spatial_a = jnp.transpose(spatial_sa, (0, 2, 1))
    grad_spatial_b = jnp.transpose(spatial, (0, 2, 1))
    grad_expand_b = expand
    grad_reduce_b = reduce.T
    return (
        output.reshape(FR, 8, 8, cout),
        gf.reshape(FR, 16, 16, cin),
        grad_reduce_a,
        grad_spatial_a,
        grad_a,
        grad_s,
        grad_reduce_b,
        grad_spatial_b,
        grad_expand_b,
        grad_norms_mid,
        grad_norms_out,
        stats_mid,
        stats_out,
    )


def solution(mesh):
    in_specs = (
        P("dp", None, None, "chan"),
        P("dp", None, None, "chan"),
        P("chan", "dp"),
        P(None, "chan", "dp"),
        P("dp", "chan"),
        P("dp", "chan"),
        P("chan", "dp"),
        P(None, "chan", "dp"),
        P("dp", "chan"),
        P(),
        P(None, None, "chan"),
        P("dp"),
        P("dp"),
        P(),
    )
    out_specs = (
        P("dp", None, None, "chan"),
        P("dp", None, None, "chan"),
        P("chan", "dp"),
        P(None, "chan", "dp"),
        P("dp", "chan"),
        P("dp", "chan"),
        P("chan", "dp"),
        P(None, "chan", "dp"),
        P("dp", "chan"),
        P(),
        P(None, None, "chan"),
        P(),
        P(None, None, None, "chan"),
    )
    return jax.shard_map(shards, mesh=mesh, in_specs=in_specs, out_specs=out_specs, check_vma=False)
```

```python
import jax
import jax.numpy as jnp
from jax import lax
from jax.experimental import pallas as pl
from jax.experimental.pallas import tpu as pltpu
from jax.sharding import PartitionSpec as P

EPSILON = 1e-05
BF = jnp.bfloat16
F32 = jnp.float32
FR = 8
RP = 7
QP = 8
PX = RP * QP
NP = FR * PX
LB = 128
NB = 4
TAPS = 9 * LB


class Pinned:
    def __init__(self, array, view=None, shape=None):
        self.array = array
        self.view = view
        self.shape = array.shape if shape is None else shape


class Gathered:
    def __init__(self, pieces, rows, first, lanes):
        self.pieces = pieces
        self.rows = rows
        self.window = (slice(0, rows), slice(first, first + lanes))
        self.shape = (8 * rows, lanes)


class Late:
    def __init__(self, ref, copies):
        self.ref = ref
        self.copies = copies
        self.waiting = True

    def ready(self):
        if self.waiting:
            for copy in self.copies:
                copy.wait()
            self.waiting = False
        return self.ref

    def __getitem__(self, index):
        return self.ready()[index]

    @property
    def shape(self):
        return self.ref.shape


class Saved:
    def __init__(self, ref, copy):
        self.ref = ref
        self.copy = copy
        self.sent = False

    def __setitem__(self, index, value):
        self.ref[index] = value

    def __getitem__(self, index):
        return self.ref[index]

    @property
    def shape(self):
        return self.ref.shape

    def send(self):
        self.sent = True
        self.copy.start()


PRM, INV, PRM_OUT, TAB, TAB_OUT, SLOTS = 0, 16, 17, 29, 45, 57


class Held:
    def __init__(self, kind, norm=0, ref=None):
        self.kind = kind
        self.norm = norm
        self.ref = ref

    def __getitem__(self, index):
        if self.kind == "prm":
            norm, j = index
            return self.ref[PRM + norm * NB + j][0:2]
        if self.kind == "inv":
            return self.ref[INV][index]
        if self.kind == "tab":
            return self.ref[TAB + self.norm * NB + index]
        if self.kind == "prm_out":
            norm = index[0] if isinstance(index, tuple) else index
            value = jnp.concatenate([self.ref[PRM_OUT + norm * NB + b][0:2] for b in range(NB)], axis=1)
            return value[index[1]] if isinstance(index, tuple) else value
        return jnp.concatenate([self.ref[TAB_OUT + self.norm * NB + b] for b in range(NB)], axis=1)

    def __setitem__(self, index, value):
        if self.kind == "inv":
            self.ref[(INV,) + index] = value
        elif self.kind == "tab":
            self.ref[TAB + self.norm * NB + index] = value
        else:
            for b in range(NB):
                self.ref[TAB_OUT + self.norm * NB + b] = value[:, b * LB : (b + 1) * LB]


def call(body, outs, info, *args, scratch=(), name, alias=None, state=None):
    flat = []
    buffers = []
    copies = 0
    listed, outs = outs, [o for o in outs if not isinstance(o, Held)]
    held = [] if state is None else [state]
    for a in args:
        if isinstance(a, Held):
            continue
        if isinstance(a, Gathered):
            flat += [(p, True) for p in a.pieces]
            buffers.append(pltpu.VMEM(a.shape, a.pieces[0].dtype))
            copies += 8
        elif isinstance(a, Pinned):
            flat.append((a.array, True))
            buffers.append(pltpu.VMEM(a.shape, a.array.dtype))
            copies += 1
        else:
            flat.append((a, False))
    saved = [len(o) > 2 for o in outs]
    for o, s in zip(outs, saved):
        if s:
            buffers.append(pltpu.VMEM(o[4] if len(o) > 3 else o[0], o[1]))
            copies += 1
    extra = [] if alias is None else [alias[0]]
    arrays = [pltpu.with_memory_space_constraint(a, pltpu.HBM) if p else a for a, p in flat]
    arrays += [pltpu.with_memory_space_constraint(a, pltpu.HBM) for a in extra]
    vmem = pl.BlockSpec(memory_space=pltpu.VMEM)
    hbm = pl.BlockSpec(memory_space=pltpu.HBM)

    def kernel(*refs):
        refs = list(refs)
        info_ref = refs.pop(0)
        ins = refs[: len(flat)]
        refs = refs[len(flat) + len(extra) :]
        if held:
            held_in = refs.pop(0)
        results, refs = refs[: len(outs)], refs[len(outs) :]
        if held:
            held_out = refs.pop(0)
            held_out[...] = held_in[...]
        bufs, refs = refs[: len(buffers)], refs[len(buffers) :]
        if copies:
            sems, refs = refs[0], refs[1:]
        used = 0
        given = []
        late = []
        for a in args:
            if isinstance(a, Held):
                given.append(Held(a.kind, a.norm, held_in))
                continue
            if not isinstance(a, (Gathered, Pinned)):
                given.append(ins.pop(0))
                continue
            buf = bufs.pop(0)
            moves = []
            if isinstance(a, Gathered):
                blocks = []
                for piece in a.pieces:
                    ref = ins.pop(0)
                    blocks += [ref] if len(piece.shape) == 2 else [ref.at[k] for k in range(4)]
                for i in range(8):
                    source = info_ref[25] ^ (2 * (i % 4)) ^ (i // 4)
                    rows = pl.ds(pl.multiple_of(source * a.rows, a.rows), a.rows)
                    moves.append(pltpu.make_async_copy(blocks[i].at[a.window], buf.at[rows], sems.at[used]))
                    used += 1
            else:
                ref = ins.pop(0)
                source = ref if a.view is None else a.view(ref, info_ref)
                moves.append(pltpu.make_async_copy(source, buf, sems.at[used]))
                used += 1
            for move in moves:
                move.start()
            late.append(Late(buf, moves))
            given.append(late[-1])
        produced = []
        outgoing = []
        slots = iter(zip(outs, saved, results))
        for listing in listed:
            if isinstance(listing, Held):
                produced.append(Held(listing.kind, listing.norm, held_out))
                continue
            o, s, ref = next(slots)
            if s:
                buf = bufs.pop(0)
                target = o[3](ref) if len(o) > 3 else ref
                ref = Saved(buf, pltpu.make_async_copy(buf, target, sems.at[used]))
                used += 1
                outgoing.append(ref)
            produced.append(ref)
        body(info_ref, *given, *produced, *refs)
        for one in outgoing:
            if not one.sent:
                one.send()
        for one in late:
            one.ready()
        for one in outgoing:
            one.copy.wait()

    return pl.pallas_call(
        kernel,
        out_shape=[(pltpu.HBM if s else jax.ShapeDtypeStruct)(o[0], o[1]) for o, s in zip(outs, saved)]
        + [jax.ShapeDtypeStruct(x.shape, x.dtype) for x in held],
        in_specs=[pl.BlockSpec(memory_space=pltpu.SMEM)]
        + [hbm if p else vmem for _, p in flat]
        + [hbm] * len(extra)
        + [vmem] * len(held),
        out_specs=[hbm if s else vmem for s in saved] + [vmem] * len(held),
        scratch_shapes=buffers + ([pltpu.SemaphoreType.DMA((copies,))] if copies else []) + list(scratch),
        input_output_aliases={} if alias is None else {1 + len(flat): alias[1]},
        compiler_params=pltpu.CompilerParams(vmem_limit_bytes=40 << 20),
        cost_estimate=pl.CostEstimate(flops=1, bytes_accessed=1, transcendentals=0),
        name=name,
    )(info, *arrays, *held)


def f3(value):
    return value.reshape(FR, PX, value.shape[-1])


def f2(value):
    return value.reshape(NP, value.shape[-1])


def wide(value, lanes):
    count = lanes // value.shape[-1]
    return value if count == 1 else jnp.concatenate([value] * count, axis=-1)


def dot_nn(left, right):
    return lax.dot_general(left, right, (((1,), (0,)), ((), ())), preferred_element_type=F32)


def dot_nt(left, right):
    return lax.dot_general(left, right, (((1,), (1,)), ((), ())), preferred_element_type=F32)


def dot_tn(left, right):
    return lax.dot_general(left, right, (((0,), (0,)), ((), ())), preferred_element_type=F32)


def frame_scalars(info, first):
    row = lax.broadcasted_iota(jnp.int32, (FR, LB), 0)
    out = jnp.zeros((FR, LB), jnp.int32)
    for frame in range(FR):
        out = jnp.where(row == frame, info[first + frame], out)
    return out


def member_of(info):
    subnet = frame_scalars(info, 9)
    return [(subnet == s).astype(F32) for s in range(4)]


def keep_of(info, j):
    lane = lax.broadcasted_iota(jnp.int32, (FR, LB), 1) + j * LB
    return (lane < frame_scalars(info, 17)).astype(F32)[:, None, :]


def crop_mask(info, half, row_scale, row_off, col_scale, col_off):
    at = lax.broadcasted_iota(jnp.int32, (PX, LB), 0)
    row = (at >> 3) * row_scale + row_off
    col = (at & 7) * col_scale + col_off
    parts = []
    for frame in range(FR):
        side = info[1 + frame]
        if half:
            side = (side + 1) >> 1
        full = 8 if half else 16
        period = jnp.where(side > full // 2, full, full // 2)
        inside = ((row & (period - 1)) < side) & ((col & (period - 1)) < side)
        parts.append(jnp.where(inside, 1.0, 0.0).astype(F32))
    return jnp.concatenate(parts, axis=0)


def plane_mask(info, plane):
    return crop_mask(info, 0, 2, plane // 2, 2, plane % 2)


def half_mask(info):
    return crop_mask(info, 1, 1, 0, 1, 0)


def by_subnet(frames, member):
    lanes = frames.shape[-1]
    return jnp.concatenate(
        [jnp.sum(frames * wide(member[s], lanes), axis=0, keepdims=True) for s in range(4)], axis=0
    )


def by_frame(table, member):
    lanes = table.shape[-1]
    total = None
    for s in range(4):
        term = wide(member[s], lanes) * table[s : s + 1, :]
        total = term if total is None else total + term
    return total[:, None, :]


def sum_px(value):
    return jnp.sum(f3(value), axis=1)


def stat_table(totals, inv_count):
    inv_n = wide(inv_count, totals.shape[-1])
    mean = totals[0:4] * inv_n
    var = totals[4:8] * inv_n - mean * mean
    return jnp.concatenate([mean, lax.rsqrt(var + EPSILON)], axis=0), jnp.concatenate([mean, var], axis=0)


def centre(value, table, member):
    return (f3(value) - by_frame(table[0:4], member)) * by_frame(table[4:8], member)


def affine(vhat, prm):
    return prm[0:1][None] * vhat + prm[1:2][None]


def silu(pre):
    return pre * jax.nn.sigmoid(pre)


def slope(pre):
    sig = jax.nn.sigmoid(pre)
    return sig * (1.0 + pre * (1.0 - sig))


def norm_back(grads, vhat, table, totals, inv_count, member, gain):
    inv_n = wide(inv_count, totals.shape[-1])
    along = by_frame(totals[0:4] * inv_n, member)
    offset = by_frame(totals[4:8] * inv_n, member)
    factor = by_frame(table[4:8], member) * gain[None]
    return factor * (grads - offset - vhat * along)


def param_grads(totals):
    return jnp.concatenate(
        [jnp.sum(totals[0:4], axis=0, keepdims=True), jnp.sum(totals[4:8], axis=0, keepdims=True)], axis=0
    )


def rows_down(value):
    cube = f3(value)
    return f2(jnp.concatenate([jnp.zeros((FR, QP, cube.shape[-1]), F32), cube[:, : PX - QP]], axis=1))


def rows_up(value):
    cube = f3(value)
    return f2(jnp.concatenate([cube[:, QP:], jnp.zeros((FR, QP, cube.shape[-1]), F32)], axis=1))


def cols_right(value, first):
    return jnp.where(first, 0.0, pltpu.roll(value, 1, 0))


def cols_left(value, last):
    return jnp.where(last, 0.0, pltpu.roll(value, NP - 1, 0))


def edge_cols():
    at = lax.broadcasted_iota(jnp.int32, (NP, LB), 0) & 7
    return at == 0, at == 7


def block(ref, index, size):
    if len(ref.shape) == 2:
        return ref[pl.ds(pl.multiple_of(index * size, size), size), :]
    step = size // ref.shape[1]
    return ref[pl.ds(index * step, step)].reshape(size, ref.shape[-1])


def matrix(ref):
    value = ref[...]
    return value if len(value.shape) == 2 else value.reshape(-1, value.shape[-1])


def lanes_of(index, size):
    return pl.ds(pl.multiple_of(index * size, size), size)


def sums_all(ref):
    count = ref.shape[0] // NB
    out = []
    for j in range(NB):
        total = ref[j]
        for d in range(1, count):
            total = total + ref[NB * d + j]
        out.append(total)
    return out


def sums_dp(ref):
    total = ref[0]
    for d in range(1, ref.shape[0]):
        total = total + ref[d]
    return total


def spread(ref, value):
    for d in range(ref.shape[0]):
        ref[d] = value


def pair_products(low, weight, q, size):
    both = dot_nt(low, block(weight, q >> 1, 2 * size))
    odd = (q & 1) == 1
    first, second = both[:, :size], both[:, size:]
    return jnp.where(odd, second, first), jnp.where(odd, first, second)


def products(low, weight, q, size, own, others):
    refs = dict(others)
    own[...], near = pair_products(low, weight, q, size)
    refs[1][...] = near.astype(BF)
    far, both = pair_products(low, weight, q ^ 2, size)
    refs[2][...] = far.astype(BF)
    refs[3][...] = both.astype(BF)


def by_x_first(value, count):
    if count != 8:
        return value
    rows = value.shape[0] // 8
    return jnp.concatenate(
        [value[(2 * z + x) * rows : (2 * z + x + 1) * rows] for x in range(2) for z in range(4)], axis=0
    )


def emit(info, full, outs, first=0):
    if len(outs) == 1:
        outs[0][...] = full[...].astype(BF)
        return
    away, kept = outs
    rows = full.shape[0] // 8
    here = info[25]
    to = slice(first, first + rows)
    for k in range(4):
        target = here ^ (2 * k)
        kept[k, to] = full[pl.ds(pl.multiple_of(target * rows, rows), rows), :].astype(BF)
        away[k, to] = full[pl.ds(pl.multiple_of((target ^ 1) * rows, rows), rows), :].astype(BF)


def natural_index(axis):
    shape = (4 * PX, 256) if axis == 0 else (256, 4 * PX)
    at = lax.broadcasted_iota(jnp.int32, shape, axis)
    plane = (
        (at >= PX).astype(jnp.int32) + (at >= 2 * PX).astype(jnp.int32) + (at >= 3 * PX).astype(jnp.int32)
    )
    inner = at - PX * plane
    row = (inner >> 3) * 2 + (plane >> 1)
    col = (inner & 7) * 2 + (plane & 1)
    return row, col, lax.broadcasted_iota(jnp.int32, shape, 1 - axis)


def k_prep(info, feat, xm, xs, small):
    row, col, source = natural_index(0)
    hit = source == row * 16 + col
    for pair in range(FR // 2):
        picked = []
        for frame in (2 * pair, 2 * pair + 1):
            side = info[1 + frame]
            period = jnp.where(side > 8, 16, 8)
            inside = ((row & (period - 1)) < side) & ((col & (period - 1)) < side)
            select = jnp.where(hit & inside, 1.0, 0.0).astype(BF)
            picked.append(dot_nn(select, feat[frame]))
        for p in range(4):
            both = jnp.concatenate([x[p * PX : (p + 1) * PX] for x in picked], axis=0)
            xm[p, pair * 2 * PX : (pair + 1) * 2 * PX, :] = both.astype(BF)
    xs[...] = xm[...]
    small[...] = xm[0]


def k_first(info, xm, rat, *refs):
    q = info[0]
    own, near, far = refs[-3:] if len(refs) == 3 else refs[4:7]
    if len(refs) > 3:
        for k in range(4):
            refs[7][k] = refs[k][...]
        refs[7].send()
    for p in range(4):
        x = xm[p]
        own[p], one = pair_products(x, rat, q, LB)
        near[0, p] = one.astype(BF)
        far[p], three = pair_products(x, rat, q ^ 2, LB)
        near[1, p] = three.astype(BF)


def k_stat_first(info, own, near, far, zb, st):
    member = member_of(info)
    sums = None
    squares = None
    for p in range(4):
        low = (own[p] + near[0, p].astype(F32) + far[p].astype(F32)).astype(BF)
        zb[p] = low
        z = low.astype(F32)
        a, b = sum_px(z), sum_px(z * z)
        sums = a if sums is None else sums + a
        squares = b if squares is None else squares + b
    spread(st, jnp.concatenate([by_subnet(sums, member), by_subnet(squares, member)], axis=0))


def k_down(info, st, zb, prm, sa, counts, own, s1, s2, s3, im, vh, table, inv_count, stats):
    q = info[0]
    member = member_of(info)
    totals = sums_all(st)
    pixels = jnp.sum(counts[...].astype(F32), axis=0, keepdims=True)
    lane = lax.broadcasted_iota(jnp.int32, (1, LB), 1)
    for s in range(8):
        here = jnp.sum(jnp.where(lane == s, pixels, 0.0), axis=1, keepdims=True)
        inv_count[s : s + 1, :] = jnp.broadcast_to(1.0 / here, (1, LB))
    inv16 = inv_count[0:4, :]
    for j in range(NB):
        table[j], stats[j] = stat_table(totals[j][0:8], inv16)
    stats.send()
    tab = table[q]
    kept = keep_of(info, q)
    par = prm[0, q]
    first, _ = edge_cols()
    planes = []
    for p in range(4):
        vhat = centre(zb[p].astype(F32), tab, member)
        vh[p] = f2(vhat).astype(BF)
        planes.append(f2(silu(affine(vhat, par)) * f3(plane_mask(info, p)) * kept))
    vh.send()
    for t in range(3):
        for u in range(3):
            x = planes[(0 if t == 1 else 2) + (0 if u == 1 else 1)]
            if t == 0:
                x = rows_down(x)
            if u == 0:
                x = cols_right(x, first)
            at = (3 * t + u) * LB
            im[:, at : at + LB] = x.astype(BF)
    im.send()
    products(im[...], sa, q, LB, own, ((1, s1), (2, s2), (3, s3)))


def k_stat(info, own, r1, r2, r3, zb, st):
    member = member_of(info)
    low = (own[...] + r1[...].astype(F32) + r2[...].astype(F32) + r3[...].astype(F32)).astype(BF)
    zb[...] = low
    z = low.astype(F32)
    zm = z * half_mask(info)
    total = jnp.concatenate([by_subnet(sum_px(zm), member), by_subnet(sum_px(zm * z), member)], axis=0)
    spread(st, total)


def act_all(info, st, blocks, prm, norm, inv8, act, vh, table, stats):
    q = info[0]
    member = member_of(info)
    totals = sums_all(st)
    for j in range(NB):
        table[j], stats[j] = stat_table(totals[j], inv8)
    stats.send()
    m = f3(half_mask(info))
    for k in range(NB):
        j = q ^ k
        vhat = centre(blocks[k][...].astype(F32), table[j], member)
        vh[:, lanes_of(j, LB)] = f2(vhat).astype(BF)
        a = silu(affine(vhat, prm[norm, j])) * m * keep_of(info, j)
        act[:, lanes_of(j, LB)] = f2(a).astype(BF)
    vh.send()
    act.send()


def two_sums(z, member):
    return jnp.concatenate([by_subnet(sum_px(z), member), by_subnet(sum_px(z * z), member)], axis=0)


def k_proj(info, x0, x1, x2, x3, sc, st, every, zp):
    q = info[0]
    for k, ref in enumerate((x0, x1, x2, x3)):
        every[:, lanes_of(q ^ k, 256)] = ref[...]
    every.send()
    z = dot_nn(every[...], matrix(sc))
    zp[...] = z.astype(BF)
    zp.send()
    st[...] = two_sums(z, member_of(info))


def k_expand_a(info, st, b0, b1, b2, b3, stp, prm, inv_count, ea, z3, st3, act, vh, table, stats):
    act_all(info, st, (b0, b1, b2, b3), prm, 1, inv_count[4:8], act, vh, table, stats)
    z = dot_nn(act[...], matrix(ea))
    z3[...] = z
    spread(st3, jnp.concatenate([two_sums(z, member_of(info)), stp[...]], axis=1))


def k_join(info, st3, z3, zp, prm, inv_count, rbt, own, s1, s2, s3, low_a, sl, vh3, vhp, tab3, tabp, stat3, statp):
    q = info[0]
    member = member_of(info)
    inv8 = inv_count[4:8]
    lanes = z3.shape[1]
    totals = sums_dp(st3)
    tab3[...], stat3[...] = stat_table(totals[:, :lanes], inv8)
    tabp[...], statp[...] = stat_table(totals[:, lanes:], inv8)
    stat3.send()
    statp.send()
    va = centre(z3[...], tab3[...], member)
    vb = centre(zp[...].astype(F32), tabp[...], member)
    vh3[...] = f2(va).astype(BF)
    vhp[...] = f2(vb).astype(BF)
    vh3.send()
    vhp.send()
    pre = affine(va, prm[0]) + affine(vb, prm[1])
    m = wide(f3(half_mask(info)), pre.shape[-1])
    sig = jax.nn.sigmoid(pre)
    low = f2(pre * sig * m).astype(BF)
    low_a[...] = low
    low_a.send()
    sl[...] = f2(m * (sig * (1.0 + pre * (1.0 - sig)))).astype(BF)
    sl.send()
    products(low, rbt, q, LB, own, ((1, s1), (2, s2), (3, s3)))


def k_flat(info, st, zb, prm, inv_count, sb, own, s1, s2, s3, im, vh, table, stats):
    q = info[0]
    member = member_of(info)
    totals = sums_all(st)
    inv8 = inv_count[4:8]
    for j in range(NB):
        table[j], stats[j] = stat_table(totals[j], inv8)
    stats.send()
    vhat = centre(zb[...].astype(F32), table[q], member)
    vh[...] = f2(vhat).astype(BF)
    vh.send()
    act = f2(silu(affine(vhat, prm[2, q])) * f3(half_mask(info)) * keep_of(info, q))
    first, last = edge_cols()
    for t in range(3):
        shifted = rows_down(act) if t == 0 else (act if t == 1 else rows_up(act))
        for u in range(3):
            x = cols_right(shifted, first) if u == 0 else (shifted if u == 1 else cols_left(shifted, last))
            at = (3 * t + u) * LB
            im[:, at : at + LB] = x.astype(BF)
    im.send()
    products(im[...], sb, q, LB, own, ((1, s1), (2, s2), (3, s3)))


def k_expand_b(info, st, b0, b1, b2, b3, prm, inv_count, eb, z6, st6, act, vh, table, stats):
    act_all(info, st, (b0, b1, b2, b3), prm, 3, inv_count[4:8], act, vh, table, stats)
    z = dot_nn(act[...], matrix(eb))
    z6[...] = z
    spread(st6, two_sums(z, member_of(info)))


def k_output(info, st6, z6, low_a, cot, prm, inv_count, gb, vh6, st, output, gbs, tab6, stat6):
    member = member_of(info)
    tab6[...], stat6[...] = stat_table(sums_dp(st6), inv_count[4:8])
    stat6.send()
    vhat = centre(z6[...], tab6[...], member)
    vh6[...] = f2(vhat).astype(BF)
    pre = affine(vhat, prm[2]) + f3(low_a[...].astype(F32))
    m = wide(f3(half_mask(info)), pre.shape[-1])
    sig = jax.nn.sigmoid(pre)
    output[:, 0:PX, :] = pre * sig * m
    output[:, PX:, :] = jnp.zeros((FR, 64 - PX, pre.shape[-1]), F32)
    output.send()
    g = cot[...].astype(F32)[:, 0:PX, :] * m * (sig * (1.0 + pre * (1.0 - sig)))
    gb[...] = f2(g)
    gbs[...] = f2(g).astype(BF)
    gbs.send()
    along = by_subnet(jnp.sum(g * vhat, axis=1), member)
    offset = by_subnet(jnp.sum(g, axis=1), member)
    spread(st, jnp.concatenate([along, offset], axis=0))


def k_back_six(info, st, gb, vh6, tab6, prm, inv_count, eb, act5, own, s1, s2, s3, pg, grad):
    q = info[0]
    member = member_of(info)
    totals = sums_dp(st)
    pg[...] = param_grads(totals)
    pg.send()
    vhat = f3(vh6[...].astype(F32))
    m = wide(f3(half_mask(info)), vhat.shape[-1])
    g = m * norm_back(f3(gb[...]), vhat, tab6[...], totals, inv_count[4:8], member, prm[2, 0:1])
    low = f2(g).astype(BF)
    products(low, eb, q, LB, own, ((1, s1), (2, s2), (3, s3)))
    grad[...] = by_x_first(dot_tn(act5[...], low), st.shape[0]).astype(BF)


def back_stat(g, vhat, member, gl, st):
    low = f2(g).astype(BF)
    gl[...] = low
    g = f3(low.astype(F32))
    along = by_subnet(jnp.sum(g * vhat, axis=1), member)
    offset = by_subnet(jnp.sum(g, axis=1), member)
    spread(st, jnp.concatenate([along, offset], axis=0))


def k_back_stat(norm):
    def body(info, own, r1, r2, r3, vh, prm, gl, st):
        q = info[0]
        part = own[...] + r1[...].astype(F32) + r2[...].astype(F32) + r3[...].astype(F32)
        vhat = f3(vh[...].astype(F32))
        g = f3(part * half_mask(info)) * keep_of(info, q) * slope(affine(vhat, prm[norm, q]))
        back_stat(g, vhat, member_of(info), gl, st)

    return body


def gz_all(info, st, grads, values, table, prm, norm, inv8, gz, pg, hold):
    q = info[0]
    member = member_of(info)
    totals = sums_all(st)
    for j in range(NB):
        pg[j] = param_grads(totals[j])
        hold[j] = totals[j]
    pg.send()
    m = f3(half_mask(info))
    for k in range(NB):
        j = q ^ k
        vhat = f3(values(k, j).astype(F32))
        g = norm_back(f3(grads[k][...].astype(F32)), vhat, table[j], hold[j], inv8, member, prm[norm, j][0:1])
        gz[:, lanes_of(j, LB)] = f2(m * g).astype(BF)


def k_back_five(info, st, g0, g1, g2, g3, vh5, tab5, prm, inv_count, sb, vh4, im4, gl, st4, pg, grad, gz5, hold):
    q = info[0]
    gz_all(
        info, st, (g0, g1, g2, g3), lambda k, j: vh5[:, lanes_of(j, LB)], tab5, prm, 3, inv_count[4:8],
        gz5, pg, hold,
    )
    terms = dot_nn(gz5[...], sb[...])
    first, last = edge_cols()
    total = None
    for t in range(3):
        for u in range(3):
            at = (3 * t + u) * LB
            x = terms[:, at : at + LB]
            x = cols_left(x, last) if u == 0 else (x if u == 1 else cols_right(x, first))
            x = rows_up(x) if t == 0 else (x if t == 1 else rows_down(x))
            total = x if total is None else total + x
    vhat = f3(vh4[...].astype(F32))
    g = f3(total * half_mask(info)) * keep_of(info, q) * slope(affine(vhat, prm[2, q]))
    back_stat(g, vhat, member_of(info), gl, st4)
    grad[...] = by_x_first(dot_tn(gz5[...], im4[...]), st.shape[0] // NB).astype(BF)


def k_back_four(info, st, g0, g1, g2, g3, v0, v1, v2, v3, tab4, prm, inv_count, rbt, gb, sl, vh3, vhp, low_a, ga, st3, pg, grad, gz4, hold):
    member = member_of(info)
    values = (v0, v1, v2, v3)
    gz_all(
        info, st, (g0, g1, g2, g3), lambda k, j: values[k][...], tab4, prm, 2, inv_count[4:8], gz4, pg, hold
    )
    low = gz4[...]
    back = dot_nn(low, matrix(rbt))
    g = (gb[...].astype(F32) + back) * sl[...].astype(F32)
    ga[...] = g
    g = f3(g)
    along = by_subnet(jnp.sum(g * f3(vh3[...].astype(F32)), axis=1), member)
    other = by_subnet(jnp.sum(g * f3(vhp[...].astype(F32)), axis=1), member)
    offset = by_subnet(jnp.sum(g, axis=1), member)
    half = offset.shape[-1] // 2
    tail = jnp.concatenate([offset[:, :half], offset[:, half:]], axis=0)
    spread(st3, jnp.concatenate([jnp.concatenate([along, other], axis=0), tail], axis=1))
    grad[...] = dot_tn(low, low_a[...]).astype(BF)


def add_hop(kept, away, sums):
    for k in range(4):
        total = kept[k].astype(F32) + away[k].astype(F32)
        sums[k][...] = total if k == 0 else total.astype(BF)
        sums[k].send()


def line_sum(parts):
    total = parts[0][...]
    for part in parts[1:]:
        total = total + part[...].astype(F32)
    return total


def taps_apart(ref, value):
    for tap in range(9):
        ref[tap] = value[:, tap * LB : (tap + 1) * LB]
    ref.send()


def emit_line(info, full, outs, first, part=0, parts=1):
    kept, away = outs
    rows = kept.shape[1]
    here = info[25] & 1
    lanes = full.shape[1]
    for z in range(4):
        for ref, x in ((kept, here), (away, here ^ 1)):
            at = ((2 * z + x) * parts + part) * rows
            ref[z, :, first : first + lanes] = full[pl.ds(pl.multiple_of(at, rows), rows), :].astype(BF)


def k_back_join(info, st, ga, vh3, vhp, tab3, tabp, prm, inv_count, ea, act2, every, grad_r, *refs):
    q = info[0]
    member = member_of(info)
    own, s1, s2, s3, gzp, pg3, pgp, *grads, full_a, full_s = refs
    totals = sums_dp(st)
    lanes = ga.shape[-1]
    tail = totals[:, lanes:]
    offset = jnp.concatenate([tail[0:4], tail[4:8]], axis=1)
    tot3 = jnp.concatenate([totals[0:4, :lanes], offset], axis=0)
    totp = jnp.concatenate([totals[4:8, :lanes], offset], axis=0)
    pg3[...] = param_grads(tot3)
    pgp[...] = param_grads(totp)
    pg3.send()
    pgp.send()
    inv8 = inv_count[4:8]
    g = f3(ga[...])
    m = wide(f3(half_mask(info)), lanes)
    low = f2(m * norm_back(g, f3(vh3[...].astype(F32)), tab3[...], tot3, inv8, member, prm[0, 0:1])).astype(BF)
    products(low, ea, q, LB, own, ((1, s1), (2, s2), (3, s3)))
    lowp = f2(m * norm_back(g, f3(vhp[...].astype(F32)), tabp[...], totp, inv8, member, prm[1, 0:1])).astype(BF)
    gzp[...] = lowp
    full_a[...] = dot_tn(act2[...], low)
    full_s[...] = dot_tn(every[...], lowp)
    if len(grads) == 2:
        emit_line(info, grad_r, grads, 0)
        emit_line(info, full_a, grads, lanes)
        for part in range(2):
            emit_line(info, full_s, grads, (2 + part) * lanes, part, 2)
        return
    grad = grads[0]
    count = st.shape[0]
    rows = full_s.shape[0] // count // 2
    grad[:, 0:lanes] = grad_r[...]
    grad[:, lanes : 2 * lanes] = full_a[...].astype(BF)
    for part in range(2):
        picked = [full_s[(2 * d + part) * rows : (2 * d + part + 1) * rows, :] for d in range(count)]
        at = (2 + part) * lanes
        grad[:, at : at + lanes] = jnp.concatenate(picked, axis=0).astype(BF)


def k_back_small(info, gzp, sc, own, s1, s2, s3):
    q = info[0]
    low = gzp[...]
    products(low, sc, q, 256, own, ((1, s1), (2, s2), (3, s3)))


def k_back_two(info, st, g0, g1, g2, g3, vh2, tab2, prm, inv_count, sa, vh1, im1, *refs):
    q = info[0]
    member = member_of(info)
    refs, (gz2, hold, full) = refs[:-3], refs[-3:]
    if len(refs) > 5:
        rows = refs[0].shape[1]
        for z in range(4):
            refs[6][z * rows : (z + 1) * rows, :] = (refs[0][z].astype(F32) + refs[1][z].astype(F32)).astype(BF)
        refs[6].send()
        (gl, st1, pg, saved), grads = refs[2:6], refs[7:]
    else:
        (gl, st1, pg, saved), grads = refs[0:4], refs[4:]
    gz_all(
        info, st, (g0, g1, g2, g3), lambda k, j: vh2[:, lanes_of(j, LB)], tab2, prm, 1, inv_count[4:8],
        gz2, pg, hold,
    )
    terms = dot_nn(gz2[...], sa[...])
    _, last = edge_cols()
    y = [terms[:, tap * LB : (tap + 1) * LB] for tap in range(9)]
    planes = [
        y[4],
        cols_left(y[3], last) + y[5],
        rows_up(y[1]) + y[7],
        rows_up(cols_left(y[0], last) + y[2]) + cols_left(y[6], last) + y[8],
    ]
    kept = keep_of(info, q)
    along = None
    offset = None
    for p in range(4):
        vhat = f3(vh1[p].astype(F32))
        g = f3(planes[p] * plane_mask(info, p)) * kept * slope(affine(vhat, prm[0, q]))
        low = f2(g).astype(BF)
        gl[p] = low
        saved[p] = low
        g = f3(low.astype(F32))
        a, b = jnp.sum(g * vhat, axis=1), jnp.sum(g, axis=1)
        along = a if along is None else along + a
        offset = b if offset is None else offset + b
    saved.send()
    spread(st1, jnp.concatenate([by_subnet(along, member), by_subnet(offset, member)], axis=0))
    full[...] = dot_tn(gz2[...], im1[...])
    emit(info, full, grads)


def k_last(info, st, g0, g1, g2, g3, v0, v1, v2, v3, tab1, prm, inv_count, xm, *refs):
    q = info[0]
    member = member_of(info)
    gz1, pg, grad, hold = refs
    totals = sums_all(st)
    inv16 = inv_count[0:4]
    for j in range(NB):
        pg[j] = param_grads(totals[j])
        hold[j] = totals[j]
    pg.send()
    total = None
    for p in range(4):
        m = f3(plane_mask(info, p))
        for k, (gref, vref) in enumerate(((g0, v0), (g1, v1), (g2, v2), (g3, v3))):
            j = q ^ k
            vhat = f3(vref[p].astype(F32))
            g = norm_back(f3(gref[p].astype(F32)), vhat, tab1[j], hold[j], inv16, member, prm[0, j][0:1])
            gz1[p, :, lanes_of(j, LB)] = f2(m * g).astype(BF)
        term = dot_tn(gz1[p], xm[p])
        total = term if total is None else total + term
    grad[...] = total.astype(BF)


def k_features(info, gz1, rat, own, r1, r2, r3, gf, nat):
    for p in range(4):
        back = dot_nn(gz1[p], rat[...])
        if p == 0:
            back = back + own[...] + r1[...].astype(F32) + r2[...].astype(F32) + r3[...].astype(F32)
        back = back * wide(plane_mask(info, p), back.shape[-1])
        high = back.astype(BF)
        nat[0, p] = high.astype(F32)
        nat[1, p] = back - high.astype(F32)
    row, col, target = natural_index(1)
    select = jnp.where(target == row * 16 + col, 1.0, 0.0).astype(BF)
    for frame in range(FR):
        out = None
        for part in range(2):
            x = jnp.concatenate(
                [nat[part, p, frame * PX : (frame + 1) * PX, :] for p in range(4)], axis=0
            ).astype(BF)
            y = dot_nn(select, x)
            out = y if out is None else out + y
        gf[frame] = out


def k_tables(info, *refs):
    mids, pairs, outs, gains = refs[0:4], refs[4:8], refs[8:11], refs[11:14]
    stats_mid, grads_mid, stats_out, grads_out = refs[14:]
    for i in range(4):
        for j in range(NB):
            at = slice(j * LB, (j + 1) * LB)
            stats_mid[i, 0, :, at] = mids[i][j, 0:4]
            stats_mid[i, 1, :, at] = mids[i][j, 4:8]
            grads_mid[i, :, at] = pairs[i][j]
    for i in range(3):
        stats_out[i, 0] = outs[i][0:4]
        stats_out[i, 1] = outs[i][4:8]
        grads_out[i] = gains[i][...]


def k_end_grads(info, early, grad, spatial, expand, reduce, other, shortcut):
    value = early[...].astype(F32)
    taps_apart(spatial, value)
    expand[...] = value[:, TAPS:]
    value = grad[...].astype(F32)
    lanes = expand.shape[-1]
    reduce[...] = value[:, :lanes]
    other[...] = value[:, lanes : 2 * lanes]
    shortcut[...] = jnp.concatenate([value[:, 2 * lanes : 3 * lanes], value[:, 3 * lanes :]], axis=0)


def k_hop(info, kept, away, *sums):
    add_hop(kept, away, sums)


def k_final(info, *refs):
    parts, others, spatial, reduce = refs[:-3], refs[-3], refs[-2], refs[-1]
    taps_apart(spatial, line_sum(parts))
    total = others[0].astype(F32)
    for d in range(1, others.shape[0]):
        total = total + others[d].astype(F32)
    reduce[...] = total


def swap(value, k):
    return lax.ppermute(value, "chan", [(i, i ^ k) for i in range(NB)])


def partners(value):
    return [value] + [swap(value, k) for k in (1, 2, 3)]


def partners_two_hops(value):
    far = swap(value, 2)
    return [value, swap(value, 1), far, swap(far, 1)]


def everywhere(value):
    return lax.all_to_all(value, ("dp", "chan"), 0, 0, tiled=True)


def along_dp(value):
    return lax.all_to_all(value, "dp", 0, 0, tiled=True)


def after(value, *others):
    return lax.optimization_barrier((value,) + others)[0]


def swap_dp(value, k):
    return lax.ppermute(value, "dp", [(i, i ^ k) for i in range(lax.axis_size("dp"))])


def along_z(value):
    return [value] + [swap_dp(value, 2 * k) for k in (1, 2, 3)]


def across_x(line, *others):
    return line + [swap_dp(after(v, *others), 1) for v in line]


def add_near(kept, away):
    return [(kept[k].astype(F32) + away[k].astype(F32)).astype(F32 if k == 0 else BF) for k in range(4)]


def add_far(parts):
    return parts[0] + parts[1].astype(F32) + parts[2].astype(F32) + parts[3].astype(F32)


def reduce_pairs(value):
    if lax.axis_size("dp") != 8:
        return lax.psum_scatter(value, "dp", scatter_dimension=0, tiled=True)
    groups = [[2 * z, 2 * z + 1] for z in range(4)]
    return lax.psum_scatter(value, "dp", scatter_dimension=0, tiled=True, axis_index_groups=groups)


def reduce_lines(value):
    if lax.axis_size("dp") != 8:
        return value
    groups = [[2 * z + x for z in range(4)] for x in range(2)]
    return lax.psum_scatter(value, "dp", scatter_dimension=0, tiled=True, axis_index_groups=groups)


def shards(
    features,
    cotangent,
    reduce_a,
    spatial_a,
    expand_a,
    shortcut,
    reduce_b,
    spatial_b,
    expand_b,
    norms_mid,
    norms_out,
    crop_side,
    subnet_of,
    width_of,
):
    ndp = lax.axis_size("dp")
    nall = ndp * NB
    hops = ndp == 8
    hidden = norms_mid.shape[-1]
    cin = features.shape[-1]
    cout = cotangent.shape[-1]
    rows = reduce_a.shape[1]
    er = expand_a.shape[0]
    sr = shortcut.shape[0]
    position = lax.axis_index("chan").astype(jnp.int32)
    place = lax.axis_index("dp").astype(jnp.int32)
    width = jnp.sum(
        jnp.where(subnet_of[:, None] == jnp.arange(4, dtype=jnp.int32)[None, :], width_of[None, :], 0), axis=1
    )
    info = jnp.concatenate([position[None], crop_side, subnet_of, width, place[None]])

    ra_t = reduce_a.T
    sa_t = jnp.transpose(spatial_a, (2, 0, 1)).reshape(rows, TAPS)
    half = (crop_side + 1) // 2
    per16 = jnp.where(crop_side > 8, crop_side * crop_side, 4 * crop_side * crop_side)
    per8 = jnp.where(half > 4, half * half, 4 * half * half)
    lane = jnp.arange(LB, dtype=jnp.int32)[None, :]
    pixels = jnp.where(lane == subnet_of[:, None], per16[:, None], 0)
    pixels = pixels + jnp.where(lane == subnet_of[:, None] + 4, per8[:, None], 0)
    pixels = jnp.concatenate([pixels.astype(F32), jnp.zeros((rows, LB), F32)], axis=0)[: max(rows, FR)]
    prm, prm_out, inv_count = Held("prm"), Held("prm_out"), Held("inv")
    tab1, tab2, tab4, tab5 = [Held("tab", i) for i in range(4)]
    tab3, tabp, tab6 = [Held("tab_out", i) for i in range(3)]
    slots = [
        jnp.transpose(x.reshape(-1, 2, NB, LB), (0, 2, 1, 3)).reshape(-1, 2, LB) for x in (norms_mid, norms_out)
    ]
    slots = [jnp.pad(x, ((0, 0), (0, 6), (0, 0))) for x in slots]
    blank = jnp.zeros((SLOTS, 8, LB), F32)
    state = jnp.concatenate([slots[0], blank[:1], slots[1], blank[TAB:]], axis=0)
    table = ((NB, 8, LB), F32, "hbm")
    one_block = ((NP, LB), F32)
    send = ((NP, LB), BF)
    sends = [one_block, send, send, send]
    stat_all = ((nall, 8, LB), F32)
    stat_own = ((ndp, 8, cout), F32)
    stat_wide = ((ndp, 8, cout + cout // 2), F32)
    map_out = ((NP, cout), F32)
    low_out = ((NP, cout), BF, "hbm")
    low_mid = ((NP, hidden), BF, "hbm")
    tab_out = ((8, cout), F32, "hbm")

    if hops:
        line_ra = along_z(ra_t)
        line_sa = along_z(after(jnp.concatenate([sa_t, pixels.astype(BF)], axis=1), line_ra[1]))
        pieces = across_x(line_ra, *line_ra[1:])
        feat = after(features.reshape(FR, 256, cin), pieces[4])
        rat = Gathered(pieces, rows, 0, cin)
    else:
        rat = Pinned(lax.all_gather(ra_t, "dp", axis=0, tiled=True))
        sa = Pinned(lax.all_gather(sa_t, "dp", axis=0, tiled=True))
        counts = Pinned(lax.psum(pixels, "dp"))
        feat = features.reshape(FR, 256, cin)
    xm, xs, small = call(
        k_prep, [((4, NP, cin), BF), ((4, NP, cin), BF, "hbm"), ((NP, cin), BF)],
        info, Pinned(feat), name="prep",
    )
    pack_mid = jnp.concatenate([expand_a, shortcut, after(reduce_b, small).T], axis=0)
    pack_end = jnp.concatenate(
        [jnp.transpose(after(spatial_b, small), (2, 0, 1)).reshape(rows, TAPS), expand_b], axis=1
    )
    own, near, far, *stacked = call(
        k_first,
        [((4, NP, LB), F32), ((2, 4, NP, LB), BF), ((4, NP, LB), F32)]
        + ([((4, rows, TAPS + LB), BF, "hbm")] if hops else []),
        info, after(xm, pack_mid, pack_end), rat, *(line_sa if hops else []), name="first",
    )
    if hops:
        sa_pieces = [stacked[0], swap_dp(stacked[0], 1)]
        sa = Gathered(sa_pieces, rows, 0, TAPS)
        counts = Gathered(sa_pieces, 16, TAPS, LB)
    near = swap(near, 1)
    far = (far + near[1].astype(F32)).astype(BF)
    mid = lax.all_gather(after(pack_mid, own), "dp", axis=0)

    def mid_rows(first, size):
        if size % 16 == 0:
            return Pinned(mid, lambda ref, info: ref.at[:, first : first + size, :], (ndp, size, cout))
        return Pinned(mid[:, first : first + size].reshape(ndp * size, cout))

    ea = mid_rows(0, er)
    sc = mid_rows(er, sr)
    rbt = mid_rows(er + sr, rows)
    end = lax.all_gather(pack_end, "dp", axis=0, tiled=True)
    sb = Pinned(end, lambda ref, info: ref.at[:, 0:TAPS], (hidden, TAPS))
    eb = Pinned(end, lambda ref, info: ref.at[:, TAPS : TAPS + cout], (hidden, cout))

    far = swap(far, 2)
    zb1, st = call(
        k_stat_first, [((4, NP, LB), BF), stat_all], info, own, near, far, name="stat_one"
    )
    smalls = partners_two_hops(after(small, st))
    st = after(everywhere(st), *smalls[1:])
    own, s1, s2, s3, im1, vh1, stat1, state = call(
        k_down,
        sends + [((NP, TAPS), BF, "hbm"), ((4, NP, LB), BF, "hbm"), tab1, inv_count, table],
        info, st, zb1, prm, sa, counts, state=state, name="down",
    )
    zb, st = call(k_stat, [send, stat_all], info, own, swap(s1, 1), swap(s2, 2), swap(s3, 3), name="stat_two")
    zs = partners(zb)
    smalls = lax.optimization_barrier(tuple(smalls) + (st,))[:4]
    stp, every, zp = call(
        k_proj, [((8, cout), F32), ((NP, NB * cin), BF, "hbm"), low_out], info, *smalls, sc, name="proj"
    )
    st = after(everywhere(st), stp)
    z3, st3, act2, vh2, stat2, state = call(
        k_expand_a, [map_out, ((ndp, 8, 2 * cout), F32), low_mid, low_mid, tab2, table],
        info, st, *zs, stp, prm, inv_count, ea, state=state, name="expand_a",
    )
    st3 = along_dp(st3)
    own, s1, s2, s3, low_a, sl, vh3, vhp, stat3, statp, state = call(
        k_join, sends + [low_out, low_out, low_out, low_out, tab3, tabp, tab_out, tab_out],
        info, st3, z3, Pinned(zp), prm_out, inv_count, rbt, state=state, name="join",
    )
    zb, st = call(k_stat, [send, stat_all], info, own, swap(s1, 1), swap(s2, 2), swap(s3, 3), name="stat_four")
    st = everywhere(st)
    own, s1, s2, s3, im4, vh4, stat4, state = call(
        k_flat, sends + [((NP, TAPS), BF, "hbm"), ((NP, LB), BF, "hbm"), tab4, table],
        info, st, zb, prm, inv_count, sb, state=state, name="flat",
    )
    zb, st = call(k_stat, [send, stat_all], info, own, swap(s1, 1), swap(s2, 2), swap(s3, 3), name="stat_five")
    zs = partners(zb)
    st = everywhere(st)
    z6, st6, act5, vh5, stat5, state = call(
        k_expand_b, [map_out, stat_own, low_mid, low_mid, tab5, table],
        info, st, *zs, prm, inv_count, eb, state=state, name="expand_b",
    )
    vhs4 = partners(after(vh4, st6))
    st6 = after(along_dp(st6), *vhs4[1:])
    gb, vh6, st, output, gbs, stat6, state = call(
        k_output,
        [map_out, ((NP, cout), BF), stat_own, ((FR, 64, cout), F32, "hbm"), low_out, tab6, tab_out],
        info, st6, z6, Pinned(low_a), Pinned(cotangent.reshape(FR, 64, cout)), prm_out, inv_count, state=state, name="output",
    )

    def early(first, size):
        return ((hidden, TAPS + cout), BF, "hbm", lambda ref: ref.at[:, first : first + size], (hidden, size))

    def summed(size, lanes):
        return [((size, lanes), F32, "hbm")] + [((size, lanes), BF, "hbm")] * 3

    def z_parts(sums):
        return [sums[0]] + [swap_dp(sums[k], 2 * k) for k in (1, 2, 3)]

    def reduced(size, width_):
        if hops:
            return [((4, size, width_), BF, "hbm")] * 2
        return [((ndp * size, width_), BF, "hbm")]

    def own_lanes(array):
        return Pinned(array, lambda ref, info: ref.at[:, lanes_of(info[0], LB)], (NP, LB))

    vh1_in = after(vh1, st)
    vhs1 = [vh1, swap(vh1_in, 1), swap(vh1_in, 2)]
    st = after(along_dp(st), *vhs1[1:])
    own, s1, s2, s3, pg6, grad_early, state = call(
        k_back_six, sends + [((2, cout), F32, "hbm"), early(TAPS, cout)],
        info, st, gb, vh6, tab6, prm_out, inv_count, eb, Pinned(act5), state=state, name="back_six",
    )
    gl, st, state = call(
        k_back_stat(3), [send, stat_all],
        info, own, swap(s1, 1), swap(s2, 2), swap(s3, 3), own_lanes(vh5), prm, state=state, name="back_stat_five",
    )
    gs = partners(gl)
    st = everywhere(st)
    hold = pltpu.VMEM((NB, 8, LB), F32)
    pair_mid = ((NB, 2, LB), F32, "hbm")
    gl, st, pg5, grad_early, state = call(
        k_back_five, [send, stat_all, pair_mid, early(0, TAPS)],
        info, st, *gs, Pinned(vh5), tab5, prm, inv_count, sb, Pinned(vh4), Pinned(im4),
        scratch=[pltpu.VMEM((NP, hidden), BF), hold], alias=(grad_early, 3), state=state, name="back_five",
    )
    gs = partners(gl)
    grad_early = reduce_pairs(grad_early)
    st = everywhere(st)
    ga, st, pg4, grad_r, state = call(
        k_back_four, [map_out, stat_wide, pair_mid, ((hidden, cout), BF, "hbm")],
        info, st, *gs, *[Pinned(v) for v in vhs4], tab4, prm, inv_count, rbt, Pinned(gbs), Pinned(sl),
        Pinned(vh3), Pinned(vhp), Pinned(low_a),
        scratch=[pltpu.VMEM((NP, hidden), BF), hold], state=state, name="back_four",
    )
    vhs1.append(swap(after(vhs1[2], st), 1))
    st = after(along_dp(st), vhs1[3], grad_early)
    if hops:
        grads = [((4, rows, 4 * cout), BF, "hbm")] * 2
    else:
        grads = [((hidden, 4 * cout), BF, "hbm")]
    own, s1, s2, s3, gzp, pg3, pgp, *grads, state = call(
        k_back_join, sends + [((NP, cout), BF)] + [((2, cout), F32, "hbm")] * 2 + grads,
        info, st, ga, Pinned(vh3), Pinned(vhp), tab3, tabp, prm_out, inv_count, ea,
        Pinned(act2), Pinned(every), Pinned(grad_r),
        scratch=[pltpu.VMEM((hidden, cout), F32), pltpu.VMEM((ndp * sr, cout), F32)], state=state, name="back_join",
    )
    grad_early = reduce_lines(after(grad_early, grads[0]))
    extra_in, extra_out = [], []
    if hops:
        extra_in = [Pinned(grads[0]), swap_dp(grads[1], 1)]
        extra_out = [((4 * rows, 4 * cout), BF, "hbm")]
    else:
        end_grad = reduce_pairs(grads[0])
    r1, r2, r3 = swap(s1, 1), swap(s2, 2), swap(s3, 3)
    sown, *small_sends = call(
        k_back_small, [((NP, cin), F32)] + [((NP, cin), BF)] * 3,
        info, after(gzp, r1), sc, name="back_small",
    )
    own = after(own, sown)
    gl, st, state = call(
        k_back_stat(1), [send, stat_all],
        info, own, r1, r2, r3, own_lanes(vh2), prm, state=state, name="back_stat_two",
    )
    gs = partners(gl)
    st = everywhere(st)
    small_one = swap(small_sends[0], 1)
    st = after(st, grad_early, small_one)
    gl, st, pg2, saved, *grad_sa, state = call(
        k_back_two, [((4, NP, LB), BF), stat_all, pair_mid, ((4, NP, LB), BF, "hbm")] + extra_out + reduced(rows, TAPS),
        info, st, *gs, Pinned(vh2), tab2, prm, inv_count, sa, Pinned(vh1), Pinned(im1), *extra_in,
        scratch=[pltpu.VMEM((NP, hidden), BF), hold, pltpu.VMEM((hidden, TAPS), F32)], state=state, name="back_two",
    )
    gs = [gl, swap(gl, 1), swap(gl, 2)]
    st = everywhere(st)
    gs.append(swap(after(gs[2], st), 1))
    small_back = [small_one] + [swap(after(small_sends[k - 1], gs[3]), k) for k in (2, 3)]
    extra_in, extra_out = [], []
    if hops:
        end_grad = reduce_lines(grad_sa[0])
        kept, away = grad_sa[2], swap_dp(grad_sa[1], 1)
    gz1, pg1, grad_rat, _ = call(
        k_last, [((4, NP, hidden), BF), pair_mid, ((hidden, cin), BF, "hbm")],
        info, st, Pinned(saved), Pinned(gs[1]), Pinned(gs[2]), gs[3], *[Pinned(v) for v in vhs1], tab1, prm, inv_count,
        Pinned(xs), scratch=[hold], state=state, name="last",
    )
    if hops:
        sums_sa = call(k_hop, summed(rows, TAPS), info, Pinned(after(kept, gz1)), away, name="hop")
        parts_sa = z_parts(sums_sa)
        grad_rat = after(grad_rat, sums_sa[0])
    else:
        parts_sa = [lax.psum_scatter(grad_sa[0], "dp", scatter_dimension=0, tiled=True).astype(F32)]
    spatial, expand, reduce, grad_a, grad_s = call(
        k_end_grads,
        [
            ((9, rows, LB), F32, "hbm"), ((er, cout), F32, "hbm"), ((rows, cout), F32, "hbm"),
            ((er, cout), F32, "hbm"), ((sr, cout), F32, "hbm"),
        ],
        info, Pinned(grad_early), Pinned(end_grad), name="end_grads",
    )
    parts_ra = along_dp(grad_rat.reshape(ndp, rows, cin))
    stats_mid, grad_norms_mid, stats_out, grad_norms_out = call(
        k_tables,
        [
            ((4, 2, 4, hidden), F32, "hbm"), ((4, 2, hidden), F32, "hbm"),
            ((3, 2, 4, cout), F32, "hbm"), ((3, 2, cout), F32, "hbm"),
        ],
        info,
        *[Pinned(x) for x in (stat1, stat2, stat4, stat5, pg1, pg2, pg4, pg5, stat3, statp, stat6, pg3, pgp, pg6)],
        name="tables",
    )
    gf = call(
        k_features, [((FR, 256, cin), F32, "hbm")],
        info, gz1, rat, Pinned(sown), *small_back,
        scratch=[pltpu.VMEM((2, 4, NP, cin), F32)], name="features",
    )[0]
    spatial_sa, grad_rat = call(
        k_final, [((9, rows, LB), F32, "hbm"), ((rows, cin), F32, "hbm")],
        info, *[Pinned(after(x, gf, spatial)) for x in parts_sa[:1]], *[after(x, gf, spatial) for x in parts_sa[1:]],
        after(parts_ra, gf, spatial), name="final",
    )
    grad_reduce_a = grad_rat.T
    grad_spatial_a = jnp.transpose(spatial_sa, (0, 2, 1))
    grad_spatial_b = jnp.transpose(spatial, (0, 2, 1))
    grad_expand_b = expand
    grad_reduce_b = reduce.T
    return (
        output.reshape(FR, 8, 8, cout),
        gf.reshape(FR, 16, 16, cin),
        grad_reduce_a,
        grad_spatial_a,
        grad_a,
        grad_s,
        grad_reduce_b,
        grad_spatial_b,
        grad_expand_b,
        grad_norms_mid,
        grad_norms_out,
        stats_mid,
        stats_out,
    )


def solution(mesh):
    in_specs = (
        P("dp", None, None, "chan"),
        P("dp", None, None, "chan"),
        P("chan", "dp"),
        P(None, "chan", "dp"),
        P("dp", "chan"),
        P("dp", "chan"),
        P("chan", "dp"),
        P(None, "chan", "dp"),
        P("dp", "chan"),
        P(),
        P(None, None, "chan"),
        P("dp"),
        P("dp"),
        P(),
    )
    out_specs = (
        P("dp", None, None, "chan"),
        P("dp", None, None, "chan"),
        P("chan", "dp"),
        P(None, "chan", "dp"),
        P("dp", "chan"),
        P("dp", "chan"),
        P("chan", "dp"),
        P(None, "chan", "dp"),
        P("dp", "chan"),
        P(),
        P(None, None, "chan"),
        P(),
        P(None, None, None, "chan"),
    )
    return jax.shard_map(shards, mesh=mesh, in_specs=in_specs, out_specs=out_specs, check_vma=False)
```
